128 devices in a mesh: section: 4 (over y_hi, core), rep: 32 (over y_lo, x, z).
Axes of the slice: x: 4, y: 4 (y_hi: 2, y_lo: 2; y = y_hi * 2 + y_lo), z: 4, core: 2. Of those that a mesh axis runs over, the one named last changes fastest.
Arguments:
- block_inputs: bfloat16 [2, 2, 32, 3072], P(None, None, 'rep'), may hold values from -6 to 6
- routes: int32 [2, 3, 2, 4], replicated, may hold values from 0 to 1
- cotangent: bfloat16 [2, 4, 32, 3072], P(None, None, 'rep'), may hold values from -6 to 6
- gossip_peer: int32 [4, 2], replicated, may hold values from 0 to 1, as said below
- w_in: bfloat16 [4, 3072, 24576], P('section', None, 'rep'), may hold values from -6 to 6
- w_out: bfloat16 [4, 24576, 3072], P('section', 'rep'), may hold values from -6 to 6
Outputs:
- new_in: bfloat16 [4, 3072, 24576], P('section', None, 'rep')
- new_out: bfloat16 [4, 24576, 3072], P('section', 'rep')
The draws below stay inside these ranges and needn't reach their ends.
Inputs may be any that keep to these rules, and one draw needn't show every extreme that they name: `gossip_peer`: row s maps each replica to itself or to the other replica, the same way for the whole row; at least one row pairs the two replicas.
All inputs are finite; a program needn't handle non-finite values.
Results may differ from the reference program's by a relative error of at most 0.017.
Values may be sent and summed in bfloat16 or wider, within the bound.
A program may use at most 256 MiB of HBM per device.

```python
import jax
import jax.numpy as jnp
from jax import lax

D = 3072
FW = 12288
REPL = 2
NB = 2
M = 2
BR = 16
CAP = 4
N_SECTION = 4


def draw_gossip_peer(key, part):
    flips = jax.random.randint(jax.random.fold_in(key, 1), (N_SECTION,), 0, 2).astype(jnp.int32)
    forced = jax.random.randint(jax.random.fold_in(key, 2), (), 0, N_SECTION).astype(jnp.int32)
    flips = jnp.maximum(flips, (jnp.arange(N_SECTION, dtype=jnp.int32) == forced).astype(jnp.int32))
    replica_ids = jnp.arange(REPL, dtype=jnp.int32)
    return jnp.bitwise_xor(replica_ids[None, :], flips[:, None]).astype(jnp.int32)


def place_ends(result, rng, smallest, high):
    index_at = [jax.random.randint(jax.random.fold_in(rng, axis), (), 0, length) for axis, length in enumerate(result.shape)]
    widest = result.shape.index(max(result.shape))
    beside = index_at[:widest] + [(index_at[widest] + 1) % result.shape[widest]] + index_at[widest + 1:]
    return result.at[tuple(index_at)].set(smallest).at[tuple(beside)].set(high)


def block_scale(stream_key, extent, pieces, low, largest):
    level = 1.0
    for axis_at, shards_of in pieces:
        steps = jax.random.uniform(jax.random.fold_in(jax.random.fold_in(stream_key, 6), axis_at), (shards_of,), jnp.float32, low / len(pieces), largest / len(pieces))
        level = level * jnp.repeat(jnp.exp(steps), extent[axis_at] // shards_of).reshape((-1,) + (1,) * (len(extent) - 1 - axis_at))
    return level


def bell_draw(own_key, dims, scale, most, cuts=(), held_as=jnp.bfloat16):
    level = block_scale(own_key, dims, cuts, -0.22, 0.18) if cuts else 1.0
    result = jax.random.normal(own_key, dims, jnp.float32) * scale * level
    return jnp.minimum(jnp.maximum(result, -most), most).astype(held_as)


def setup_inputs(seed: int = 0) -> dict:
    streams_of = jax.random.split(jax.random.key(seed), 7)
    return {
        "block_inputs": bell_draw(streams_of[0], (M, NB, REPL * BR, D), 1.0, 6.0, ((2, 32),)),
        "routes": place_ends(jax.random.randint(streams_of[1], (M, N_SECTION - 1, REPL, CAP), 0, REPL), jax.random.fold_in(streams_of[1], 1), 0, REPL - 1).astype(jnp.int32),
        "cotangent": bell_draw(streams_of[2], (M, CAP, REPL * BR, D), 1.0, 6.0, ((2, 32),)),
        "gossip_peer": draw_gossip_peer(jax.random.fold_in(streams_of[6], 71), 0),
        "w_in": bell_draw(streams_of[4], (N_SECTION, D, REPL * FW), 1.0, 6.0, ((0, 4), (2, 32))),
        "w_out": bell_draw(streams_of[5], (N_SECTION, REPL * FW, D), 1.0, 6.0, ((0, 4), (1, 32))),
    }


EPSILON = 1e-06
GELU_SCALE = 0.7978845608028654
LEARNING = 8.0

def gelu_parts(preact):
    inner = GELU_SCALE * (preact + 0.044715 * preact * preact * preact)
    tanh_val = jnp.tanh(inner)
    gelu_val = 0.5 * preact * (1.0 + tanh_val)
    slopes = 0.5 * (1.0 + tanh_val) + 0.5 * preact * (1.0 - tanh_val * tanh_val) * GELU_SCALE * (1.0 + 3.0 * 0.044715 * preact * preact)
    return (gelu_val, slopes)

def layer_front(inputs, w_in):
    widened = inputs.astype(jnp.float32)
    inverse = lax.rsqrt(lax.optimization_barrier(jnp.mean(widened * widened, axis=-1, keepdims=True)) + EPSILON)
    normed = (widened * inverse).astype(jnp.bfloat16)
    preact = jnp.dot(normed, w_in, preferred_element_type=jnp.float32) * w_in.shape[0] ** (-0.5)
    return (widened, inverse, normed, preact)

def layer_forward(inputs, w_in, w_out):
    widened, inverse, normed, preact = layer_front(inputs, w_in)
    gelu_val, slopes = gelu_parts(preact)
    activated = gelu_val.astype(jnp.bfloat16)
    mixed_out = jnp.dot(activated, w_out, preferred_element_type=jnp.float32) * w_out.shape[0] ** (-0.5)
    return (widened + mixed_out).astype(jnp.bfloat16)

def layer_backward(inputs, w_in, w_out, upstream):
    widened, inverse, normed, preact = layer_front(inputs, w_in)
    gelu_val, slopes = gelu_parts(preact)
    activated = gelu_val.astype(jnp.bfloat16)
    factor_in = w_in.shape[0] ** (-0.5)
    factor_out = w_out.shape[0] ** (-0.5)
    d_out = jnp.dot(activated.T, upstream, preferred_element_type=jnp.float32) * factor_out
    d_act = jnp.dot(upstream, w_out.T, preferred_element_type=jnp.float32) * factor_out
    d_pre = (d_act * slopes).astype(jnp.bfloat16)
    d_in = jnp.dot(normed.T, d_pre, preferred_element_type=jnp.float32) * factor_in
    d_normed = jnp.dot(d_pre, w_in.T, preferred_element_type=jnp.float32) * factor_in
    grad_in = upstream.astype(jnp.float32) + inverse * d_normed - widened * inverse * inverse * inverse * lax.optimization_barrier(jnp.mean(d_normed * widened, axis=-1, keepdims=True))
    return (grad_in.astype(jnp.bfloat16), d_in, d_out)

def route_tables(routes, blocks):
    micro_count, bound_count, replicas, capacity = routes.shape
    slot_ids = jnp.arange(capacity, dtype=jnp.int32)
    replica_ids = jnp.arange(replicas, dtype=jnp.int32)
    live_now = jnp.broadcast_to(slot_ids[None, None, :] < blocks, (micro_count, replicas, capacity))
    link_list = []
    live_list = [live_now]
    for bound_idx in range(bound_count):
        target = jnp.where(live_now, routes[:, bound_idx].astype(jnp.int32), -1).reshape(micro_count, replicas * capacity)
        matches = (target[:, :, None] == replica_ids[None, None, :]).astype(jnp.int32)
        before = jnp.cumsum(matches, axis=1) - matches
        position = lax.optimization_barrier(jnp.sum(matches * before, axis=2))
        link_table = matches[:, :, :, None] * (position[:, :, None, None] == slot_ids[None, None, None, :]).astype(jnp.int32)
        link_table = link_table.reshape(micro_count, replicas, capacity, replicas, capacity)
        link_list.append(link_table.astype(jnp.float32))
        live_now = lax.optimization_barrier(jnp.sum(link_table, axis=(1, 2))) > 0
        live_list.append(live_now)
    return (link_list, live_list)

def reference(block_inputs, routes, cotangent, gossip_peer, w_in, w_out):
    section_count = w_in.shape[0]
    model_width = w_in.shape[1]
    replicas = gossip_peer.shape[1]
    hidden = w_in.shape[2] // replicas
    micro_count = block_inputs.shape[0]
    blocks = block_inputs.shape[1]
    row_count = block_inputs.shape[2] // replicas
    capacity = cotangent.shape[1]
    link_list, live_list = route_tables(routes, blocks)
    w_in_rep = w_in.reshape(section_count, model_width, replicas, hidden).transpose(0, 2, 1, 3)
    w_out_rep = w_out.reshape(section_count, replicas, hidden, model_width)

    def forward_one(operands):
        flat = operands[0].reshape(-1, model_width)
        return layer_forward(flat, operands[1], operands[2]).reshape(capacity, row_count, model_width)

    def backward_one(operands):
        flat = operands[0].reshape(-1, model_width)
        grad_in, d_in, d_out = layer_backward(flat, operands[1], operands[2], operands[3].reshape(-1, model_width))
        return (grad_in.reshape(capacity, row_count, model_width), d_in, d_out)
    kept_rows = []
    for micro_idx in range(micro_count):
        entering = block_inputs[micro_idx].reshape(blocks, replicas, row_count, model_width).transpose(1, 0, 2, 3)
        holding = jnp.zeros((replicas, capacity, row_count, model_width), jnp.bfloat16).at[:, :blocks].set(entering)
        per_section = []
        for depth_idx in range(section_count):
            per_section.append(holding)
            if depth_idx < section_count - 1:
                outputs = lax.map(forward_one, (holding, w_in_rep[depth_idx], w_out_rep[depth_idx]))
                holding = jnp.einsum('qjdk,qjbe->dkbe', link_list[depth_idx][micro_idx], outputs.astype(jnp.float32)).astype(jnp.bfloat16)
        kept_rows.append(per_section)
    upstreams = []
    for micro_idx in range(micro_count):
        first_up = cotangent[micro_idx].reshape(capacity, replicas, row_count, model_width).transpose(1, 0, 2, 3)
        upstreams.append(jnp.where(live_list[section_count - 1][micro_idx][:, :, None, None], first_up, jnp.zeros((), jnp.bfloat16)))
    new_in_list = []
    new_out_list = []
    for depth_idx in reversed(range(section_count)):
        accum_in = jnp.zeros((replicas, model_width, hidden), jnp.float32)
        accum_out = jnp.zeros((replicas, hidden, model_width), jnp.float32)
        for micro_idx in range(micro_count):
            grad_in, d_in, d_out = lax.map(backward_one, (kept_rows[micro_idx][depth_idx], w_in_rep[depth_idx], w_out_rep[depth_idx], upstreams[micro_idx]))
            accum_in = accum_in + d_in
            accum_out = accum_out + d_out
            if depth_idx > 0:
                upstreams[micro_idx] = jnp.einsum('qjdk,dkbe->qjbe', link_list[depth_idx - 1][micro_idx], grad_in.astype(jnp.float32)).astype(jnp.bfloat16)
        stepped_in = (w_in_rep[depth_idx].astype(jnp.float32) - LEARNING * accum_in).astype(jnp.bfloat16)
        stepped_out = (w_out_rep[depth_idx].astype(jnp.float32) - LEARNING * accum_out).astype(jnp.bfloat16)
        peer_ids = gossip_peer[depth_idx].astype(jnp.int32)
        other_in = stepped_in[peer_ids]
        other_out = stepped_out[peer_ids]
        new_in_list.insert(0, (0.5 * (stepped_in.astype(jnp.float32) + other_in.astype(jnp.float32))).astype(jnp.bfloat16))
        new_out_list.insert(0, (0.5 * (stepped_out.astype(jnp.float32) + other_out.astype(jnp.float32))).astype(jnp.bfloat16))
    new_in = jnp.stack(new_in_list).transpose(0, 2, 1, 3).reshape(section_count, model_width, replicas * hidden)
    new_out = jnp.stack(new_out_list).reshape(section_count, replicas * hidden, model_width)
    return (new_in, new_out)
```

```python
import jax
import jax.numpy as jnp
from jax import lax
from jax.sharding import PartitionSpec as P

EPSILON = 1e-06
GELU_SCALE = 0.7978845608028654
LEARNING = 8.0


def swapped(value, axis, apart):
    mask = 2**apart
    pairs = [(source, source ^ mask) for source in range(lax.axis_size(axis))]
    return lax.ppermute(value, axis, pairs)


def passed_along(value, axis, steps):
    count = lax.axis_size(axis)
    leading, last = (max(0, -steps), min(count, count - steps))
    return lax.ppermute(value, axis, [(source, source + steps) for source in range(leading, last)])


def gelu_parts(preact):
    inner = GELU_SCALE * (preact + 0.044715 * preact * preact * preact)
    tanh_val = jnp.tanh(inner)
    gelu_val = 0.5 * preact * (1.0 + tanh_val)
    slopes = 0.5 * (1.0 + tanh_val) + 0.5 * preact * (1.0 - tanh_val * tanh_val) * GELU_SCALE * (
        1.0 + 3.0 * 0.044715 * preact * preact
    )
    return (gelu_val, slopes)


def route_tables(routes, blocks):
    micro_count, bound_count, replicas, capacity = routes.shape
    slot_ids = jnp.arange(capacity, dtype=jnp.int32)
    replica_ids = jnp.arange(replicas, dtype=jnp.int32)
    live_now = jnp.broadcast_to(slot_ids[None, None, :] < blocks, (micro_count, replicas, capacity))
    link_list = []
    live_list = [live_now]
    for bound_idx in range(bound_count):
        target = jnp.where(live_now, routes[:, bound_idx], -1).reshape(
            micro_count, replicas * capacity
        )
        matches = (target[:, :, None] == replica_ids[None, None, :]).astype(jnp.int32)
        before = jnp.cumsum(matches, axis=1) - matches
        position = jnp.sum(matches * before, axis=2)
        link_table = matches[:, :, :, None] * (
            position[:, :, None, None] == slot_ids[None, None, None, :]
        ).astype(jnp.int32)
        link_table = link_table.reshape(micro_count, replicas, capacity, replicas, capacity)
        link_list.append(link_table.astype(jnp.float32))
        live_now = jnp.sum(link_table, axis=(1, 2)) > 0
        live_list.append(live_now)
    return (link_list, live_list)


def share_sum(partial_value, shard_idx, group_bits):
    current = partial_value
    for bit_pos in reversed(range(group_bits)):
        half_size = current.shape[0] // 2
        upper_bit = jnp.bitwise_and(jnp.right_shift(shard_idx, bit_pos), 1) == 1
        kept_half = jnp.where(upper_bit, current[half_size:], current[:half_size])
        sent_half = jnp.where(upper_bit, current[:half_size], current[half_size:])
        current = kept_half + swapped(sent_half.astype(jnp.bfloat16), "rep", bit_pos).astype(
            sent_half.dtype
        )
    return current[0]


def gather_rows(row_piece, shard_idx, group_bits):
    current = row_piece[None]
    for bit_pos in range(group_bits):
        partner_rows = swapped(current, "rep", bit_pos)
        upper_bit = jnp.bitwise_and(jnp.right_shift(shard_idx, bit_pos), 1) == 1
        current = jnp.where(
            upper_bit,
            jnp.concatenate([partner_rows, current], axis=0),
            jnp.concatenate([current, partner_rows], axis=0),
        )
    return current


def layer_front(flat_rows, weight_in, scale_in):
    widened = flat_rows.astype(jnp.float32)
    inverse = lax.rsqrt(jnp.mean(widened * widened, axis=-1, keepdims=True) + EPSILON)
    normed = (widened * inverse).astype(jnp.bfloat16)
    preact = jnp.dot(normed, weight_in, preferred_element_type=jnp.float32) * scale_in
    return (widened, inverse, normed, preact)


def own_part(flat_array, layout, shard_idx):
    return lax.dynamic_index_in_dim(flat_array.reshape(layout), shard_idx, 0, keepdims=False)


def layer_rest(widened, preact, weight_out, scale_out, layout, shard_idx, group_bits):
    gelu_val, slopes = gelu_parts(preact)
    activated = gelu_val.astype(jnp.bfloat16)
    partial_value = jnp.dot(activated, weight_out, preferred_element_type=jnp.float32) * scale_out
    summed = share_sum(partial_value.reshape(layout), shard_idx, group_bits)
    return (own_part(widened, layout, shard_idx) + summed).astype(jnp.bfloat16)


def layer_backward(
    inputs,
    normed,
    preact,
    weight_in,
    weight_out,
    up_full,
    up_piece,
    scale_in,
    scale_out,
    layout,
    shard_idx,
    group_bits,
):
    widened = inputs.astype(jnp.float32)
    inverse = lax.rsqrt(jnp.mean(widened * widened, axis=-1, keepdims=True) + EPSILON)
    gelu_val, slopes = gelu_parts(preact)
    activated = gelu_val.astype(jnp.bfloat16)
    d_out = (
        lax.dot_general(
            activated, up_full, (((0,), (0,)), ((), ())), preferred_element_type=jnp.float32
        )
        * scale_out
    )
    d_act = (
        lax.dot_general(
            up_full, weight_out, (((1,), (1,)), ((), ())), preferred_element_type=jnp.float32
        )
        * scale_out
    )
    d_pre = (d_act * slopes).astype(jnp.bfloat16)
    d_in = (
        lax.dot_general(normed, d_pre, (((0,), (0,)), ((), ())), preferred_element_type=jnp.float32)
        * scale_in
    )
    d_normed = (
        lax.dot_general(
            d_pre, weight_in, (((1,), (1,)), ((), ())), preferred_element_type=jnp.float32
        )
        * scale_in
    )
    normed_piece = share_sum(d_normed.reshape(layout), shard_idx, group_bits)
    wide_piece = own_part(widened, layout, shard_idx)
    inv_piece = own_part(inverse, layout[:-1] + (1,), shard_idx)
    grad_piece = (
        up_piece.astype(jnp.float32)
        + inv_piece * normed_piece
        - wide_piece
        * inv_piece
        * inv_piece
        * inv_piece
        * jnp.mean(normed_piece * wide_piece, axis=-1, keepdims=True)
    )
    return (grad_piece.astype(jnp.bfloat16), d_in, d_out)


def peer_grads(rows, ups, weight_in, weight_out, scale_in, scale_out):
    widened, inverse, normed, preact = layer_front(rows, weight_in, scale_in)
    gelu_val, slopes = gelu_parts(preact)
    activated = gelu_val.astype(jnp.bfloat16)
    d_out = (
        lax.dot_general(activated, ups, (((0,), (0,)), ((), ())), preferred_element_type=jnp.float32)
        * scale_out
    )
    d_act = (
        lax.dot_general(ups, weight_out, (((1,), (1,)), ((), ())), preferred_element_type=jnp.float32)
        * scale_out
    )
    d_pre = (d_act * slopes).astype(jnp.bfloat16)
    d_in = (
        lax.dot_general(normed, d_pre, (((0,), (0,)), ((), ())), preferred_element_type=jnp.float32)
        * scale_in
    )
    return (d_in, d_out)


def send_ahead(outbound, group_size, rep_count, replicas):
    moved = passed_along(outbound, "section", 1)
    spread = jnp.broadcast_to(moved[:, None], (replicas, group_size) + moved.shape[1:])
    spread = spread.reshape((rep_count,) + moved.shape[1:])
    received = lax.all_to_all(spread, "rep", split_axis=0, concat_axis=0, tiled=True)
    received = received.reshape((replicas, group_size) + moved.shape[1:])
    merged = jnp.sum(received.astype(jnp.float32), axis=0).astype(jnp.bfloat16)
    return merged.reshape(-1, moved.shape[-1])


def send_back(grad_piece, group_size, rep_count, replicas):
    moved = passed_along(grad_piece, "section", -1)
    spread = jnp.broadcast_to(moved[None], (rep_count,) + moved.shape)
    received = lax.all_to_all(spread, "rep", split_axis=0, concat_axis=0, tiled=True)
    return received.reshape((replicas, group_size) + moved.shape)


def stash(stack, item, slot_idx, usable):
    current = lax.dynamic_index_in_dim(stack, slot_idx, 0, keepdims=False)
    return lax.dynamic_update_index_in_dim(stack, jnp.where(usable, item, current), slot_idx, 0)


def on_device(block_inputs, routes, cotangent, gossip_peer, w_in, w_out):
    section_count = lax.axis_size("section")
    rep_count = lax.axis_size("rep")
    replicas = gossip_peer.shape[1]
    group_size = rep_count // replicas
    group_bits = group_size.bit_length() - 1
    my_section = lax.axis_index("section")
    rep_idx = lax.axis_index("rep")
    replica = rep_idx // group_size
    shard_idx = rep_idx % group_size
    micro_count, blocks, piece_rows, model_width = block_inputs.shape
    capacity = cotangent.shape[1]
    weight_in = w_in[0]
    weight_out = w_out[0]
    hidden = weight_in.shape[1]
    scale_in = model_width ** (-0.5)
    scale_out = (hidden * group_size) ** (-0.5)
    layout = (group_size, capacity, piece_rows, model_width)
    peer_in = swapped(weight_in, "rep", group_bits)
    peer_out = swapped(weight_out, "rep", group_bits)
    link_list, live_list = route_tables(routes, blocks)
    link_stack = jnp.stack(link_list + [jnp.zeros_like(link_list[0])])
    own_links = lax.dynamic_index_in_dim(link_stack, my_section, 0, keepdims=False)
    own_links = lax.dynamic_index_in_dim(own_links, replica, 1, keepdims=False)
    own_flat = own_links.reshape(micro_count, capacity, replicas * capacity).astype(jnp.bfloat16)
    last_live = lax.dynamic_index_in_dim(live_list[section_count - 1], replica, 1, keepdims=False)
    tick_count = micro_count + section_count - 1
    flat_count = group_size * capacity * piece_rows
    kept_inputs = jnp.zeros((micro_count, flat_count, model_width), jnp.bfloat16)
    arrived = jnp.zeros((flat_count, model_width), jnp.bfloat16)
    for moment in range(tick_count):
        offset = moment - my_section
        usable = jnp.logical_and(offset >= 0, offset < micro_count)
        slot_idx = jnp.clip(offset, 0, micro_count - 1)
        flat_rows = arrived
        if moment < micro_count:
            opening = jnp.concatenate(
                [
                    block_inputs[moment],
                    jnp.zeros((capacity - blocks, piece_rows, model_width), jnp.bfloat16),
                ],
                axis=0,
            )
            opened = gather_rows(opening, shard_idx, group_bits).reshape(flat_count, model_width)
            flat_rows = jnp.where(my_section == 0, opened, arrived)
        kept_inputs = stash(kept_inputs, flat_rows, slot_idx, usable)
        if moment < tick_count - 1:
            widened, inverse, normed, preact = layer_front(flat_rows, weight_in, scale_in)
            out_piece = layer_rest(
                widened, preact, weight_out, scale_out, layout, shard_idx, group_bits
            )
        if moment < tick_count - 1:
            routing = lax.dynamic_index_in_dim(own_flat, slot_idx, 0, keepdims=False)
            outbound = lax.dot_general(
                routing,
                out_piece.reshape(capacity, piece_rows * model_width),
                (((0,), (0,)), ((), ())),
                preferred_element_type=jnp.float32,
            )
            outbound = outbound.astype(jnp.bfloat16).reshape(
                replicas, capacity, piece_rows, model_width
            )
            arrived = send_ahead(outbound, group_size, rep_count, replicas)
    accum_in = jnp.zeros((model_width, hidden), jnp.float32)
    accum_out = jnp.zeros((hidden, model_width), jnp.float32)
    routed = jnp.zeros((replicas, group_size, capacity, piece_rows, model_width), jnp.bfloat16)
    kept_ups = jnp.zeros((micro_count, flat_count, model_width), jnp.bfloat16)
    for moment in range(tick_count):
        offset = moment - (section_count - 1 - my_section)
        usable = jnp.logical_and(offset >= 0, offset < micro_count)
        slot_idx = jnp.clip(offset, 0, micro_count - 1)
        routing = lax.dynamic_index_in_dim(own_flat, slot_idx, 0, keepdims=False)
        placed_full = jnp.einsum(
            "kqj,qgjpd->gkpd",
            routing.reshape(capacity, replicas, capacity),
            routed,
            preferred_element_type=jnp.float32,
        ).astype(jnp.bfloat16)
        placed = lax.dynamic_index_in_dim(placed_full, shard_idx, 0, keepdims=False)
        placed_flat = placed_full.reshape(flat_count, model_width)
        if moment < micro_count:
            opening = jnp.where(
                last_live[moment][:, None, None], cotangent[moment], jnp.zeros((), jnp.bfloat16)
            )
            opened = gather_rows(opening, shard_idx, group_bits).reshape(flat_count, model_width)
            at_end = my_section == section_count - 1
            up_piece = jnp.where(at_end, opening, placed)
            up_full = jnp.where(at_end, opened, placed_flat)
        else:
            up_piece = placed
            up_full = placed_flat
        kept_ups = stash(kept_ups, up_full, slot_idx, usable)
        inputs = lax.dynamic_index_in_dim(kept_inputs, slot_idx, 0, keepdims=False)
        widened, inverse, normed, preact = layer_front(inputs, weight_in, scale_in)
        grad_piece, d_in, d_out = layer_backward(
            inputs,
            normed,
            preact,
            weight_in,
            weight_out,
            up_full,
            up_piece,
            scale_in,
            scale_out,
            layout,
            shard_idx,
            group_bits,
        )
        accum_in = accum_in + jnp.where(usable, d_in, 0.0)
        accum_out = accum_out + jnp.where(usable, d_out, 0.0)
        if moment < tick_count - 1:
            routed = send_back(grad_piece, group_size, rep_count, replicas)
    stepped_in = (weight_in.astype(jnp.float32) - LEARNING * accum_in).astype(jnp.bfloat16)
    stepped_out = (weight_out.astype(jnp.float32) - LEARNING * accum_out).astype(jnp.bfloat16)
    partner = gossip_peer[my_section, replica]
    paired = partner != replica
    peer_rows = swapped(kept_inputs, "rep", group_bits).reshape(-1, model_width)
    peer_ups = swapped(kept_ups, "rep", group_bits).reshape(-1, model_width)
    peer_d_in, peer_d_out = peer_grads(peer_rows, peer_ups, peer_in, peer_out, scale_in, scale_out)
    other_in = (peer_in.astype(jnp.float32) - LEARNING * peer_d_in).astype(jnp.bfloat16)
    other_out = (peer_out.astype(jnp.float32) - LEARNING * peer_d_out).astype(jnp.bfloat16)
    chosen_in = jnp.where(paired, other_in, stepped_in)
    chosen_out = jnp.where(paired, other_out, stepped_out)
    new_in = (0.5 * (stepped_in.astype(jnp.float32) + chosen_in.astype(jnp.float32))).astype(
        jnp.bfloat16
    )
    new_out = (0.5 * (stepped_out.astype(jnp.float32) + chosen_out.astype(jnp.float32))).astype(
        jnp.bfloat16
    )
    return (new_in[None], new_out[None])


def solution(mesh):
    return jax.shard_map(
        on_device,
        mesh=mesh,
        in_specs=(
            P(None, None, "rep", None),
            P(),
            P(None, None, "rep", None),
            P(),
            P("section", None, "rep"),
            P("section", "rep", None),
        ),
        out_specs=(P("section", None, "rep"), P("section", "rep", None)),
        check_vma=False,
    )
```

```python
import numpy as np
import jax
import jax.numpy as jnp
from jax import lax
from jax.sharding import Mesh, PartitionSpec as P

EPSILON = 1e-06
GELU_SCALE = 0.7978845608028654
LEARNING = 8.0
PAIR = ("section", "half")


def gelu_parts(preact):
    inner = GELU_SCALE * (preact + 0.044715 * preact * preact * preact)
    tanh_val = jnp.tanh(inner)
    gelu_val = 0.5 * preact * (1.0 + tanh_val)
    slopes = 0.5 * (1.0 + tanh_val) + 0.5 * preact * (1.0 - tanh_val * tanh_val) * GELU_SCALE * (
        1.0 + 3.0 * 0.044715 * preact * preact
    )
    return (gelu_val, slopes)


def route_tables(routes, blocks):
    micro_count, bound_count, replicas, capacity = routes.shape
    slot_ids = jnp.arange(capacity, dtype=jnp.int32)
    replica_ids = jnp.arange(replicas, dtype=jnp.int32)
    live_now = jnp.broadcast_to(slot_ids[None, None, :] < blocks, (micro_count, replicas, capacity))
    link_list = []
    live_list = [live_now]
    for bound_idx in range(bound_count):
        target = jnp.where(live_now, routes[:, bound_idx], -1).reshape(
            micro_count, replicas * capacity
        )
        matches = (target[:, :, None] == replica_ids[None, None, :]).astype(jnp.int32)
        before = jnp.cumsum(matches, axis=1) - matches
        position = jnp.sum(matches * before, axis=2)
        link_table = matches[:, :, :, None] * (
            position[:, :, None, None] == slot_ids[None, None, None, :]
        ).astype(jnp.int32)
        link_table = link_table.reshape(micro_count, replicas, capacity, replicas, capacity)
        link_list.append(link_table.astype(jnp.float32))
        live_now = jnp.sum(link_table, axis=(1, 2)) > 0
        live_list.append(live_now)
    return (link_list, live_list)


def layer_front(flat_rows, weight_in, scale_in):
    widened = flat_rows.astype(jnp.float32)
    inverse = lax.rsqrt(jnp.mean(widened * widened, axis=-1, keepdims=True) + EPSILON)
    normed = (widened * inverse).astype(jnp.bfloat16)
    preact = jnp.dot(normed, weight_in, preferred_element_type=jnp.float32) * scale_in
    return (widened, inverse, normed, preact)


def gather_rows(piece):
    return lax.all_gather(piece, "plane", axis=0, tiled=True)


def own_rows(full, shard_idx):
    return lax.dynamic_slice_in_dim(full, shard_idx, 1, axis=0)


def forward_piece(x_full, weight_in, weight_out, scale_in, scale_out, shard_idx):
    shape = x_full.shape
    widened, inverse, normed, preact = layer_front(x_full.reshape(-1, shape[-1]), weight_in, scale_in)
    gelu_val, slopes = gelu_parts(preact)
    activated = gelu_val.astype(jnp.bfloat16)
    partial_value = jnp.dot(activated, weight_out, preferred_element_type=jnp.float32) * scale_out
    summed = lax.psum_scatter(partial_value.reshape(shape), "plane", scatter_dimension=0, tiled=True)
    return (own_rows(x_full, shard_idx).astype(jnp.float32) + summed).astype(jnp.bfloat16)


def backward_piece(x_full, up_full, up_piece, weight_in, weight_out, scale_in, scale_out, shard_idx):
    shape = x_full.shape
    widened, inverse, normed, preact = layer_front(x_full.reshape(-1, shape[-1]), weight_in, scale_in)
    gelu_val, slopes = gelu_parts(preact)
    d_act = (
        lax.dot_general(
            up_full.reshape(-1, shape[-1]), weight_out, (((1,), (1,)), ((), ())),
            preferred_element_type=jnp.float32,
        )
        * scale_out
    )
    d_pre = (d_act * slopes).astype(jnp.bfloat16)
    d_normed = (
        lax.dot_general(d_pre, weight_in, (((1,), (1,)), ((), ())), preferred_element_type=jnp.float32)
        * scale_in
    )
    normed_piece = lax.psum_scatter(d_normed.reshape(shape), "plane", scatter_dimension=0, tiled=True)
    wide_piece = own_rows(x_full, shard_idx).astype(jnp.float32)
    inv_piece = own_rows(inverse.reshape(shape[:-1] + (1,)), shard_idx)
    grad_piece = (
        up_piece.astype(jnp.float32)
        + inv_piece * normed_piece
        - wide_piece
        * inv_piece
        * inv_piece
        * inv_piece
        * jnp.mean(normed_piece * wide_piece, axis=-1, keepdims=True)
    )
    return grad_piece.astype(jnp.bfloat16)


def weight_grads(x_full, up_full, weight_in, weight_out, scale_in, scale_out):
    width = x_full.shape[-1]
    widened, inverse, normed, preact = layer_front(x_full.reshape(-1, width), weight_in, scale_in)
    gelu_val, slopes = gelu_parts(preact)
    activated = gelu_val.astype(jnp.bfloat16)
    ups = up_full.reshape(-1, width)
    d_out = (
        lax.dot_general(activated, ups, (((0,), (0,)), ((), ())), preferred_element_type=jnp.float32)
        * scale_out
    )
    d_act = (
        lax.dot_general(ups, weight_out, (((1,), (1,)), ((), ())), preferred_element_type=jnp.float32)
        * scale_out
    )
    d_pre = (d_act * slopes).astype(jnp.bfloat16)
    d_in = (
        lax.dot_general(normed, d_pre, (((0,), (0,)), ((), ())), preferred_element_type=jnp.float32)
        * scale_in
    )
    return (d_in, d_out)


def cross_boundary(piece, source, target, replicas):
    straight = [(source * replicas + h, target * replicas + h) for h in range(replicas)]
    crossed = [(source * replicas + h, target * replicas + (replicas - 1 - h)) for h in range(replicas)]
    return (lax.ppermute(piece, PAIR, straight), lax.ppermute(piece, PAIR, crossed))


def on_device(block_inputs, routes, cotangent, gossip_peer, w_in, w_out):
    section_count = lax.axis_size("section")
    replicas = lax.axis_size("half")
    group_size = lax.axis_size("plane")
    my_section = lax.axis_index("section")
    replica = lax.axis_index("half")
    shard_idx = lax.axis_index("plane")
    micro_count, blocks, piece_rows, model_width = block_inputs.shape
    capacity = cotangent.shape[1]
    weight_in = w_in[0]
    weight_out = w_out[0]
    hidden = weight_in.shape[1]
    scale_in = model_width ** (-0.5)
    scale_out = (hidden * group_size) ** (-0.5)
    link_list, live_list = route_tables(routes, blocks)

    opening = jnp.concatenate(
        [
            block_inputs,
            jnp.zeros((micro_count, capacity - blocks, piece_rows, model_width), jnp.bfloat16),
        ],
        axis=1,
    ).transpose(2, 0, 1, 3)
    x_cur = gather_rows(opening)
    x_keep = x_cur
    for bound in range(section_count - 1):
        piece = forward_piece(x_cur, weight_in, weight_out, scale_in, scale_out, shard_idx)
        straight, crossed = cross_boundary(piece, bound, bound + 1, replicas)
        sources = jnp.stack(
            [jnp.where(replica == h, straight, crossed) for h in range(replicas)]
        )[:, 0]
        mine = lax.dynamic_index_in_dim(link_list[bound], replica, 3, keepdims=False)
        routed = jnp.einsum(
            "mqjk,qmjd->mkd", mine.astype(jnp.bfloat16), sources,
            preferred_element_type=jnp.float32,
        ).astype(jnp.bfloat16)[None]
        x_cur = gather_rows(routed)
        x_keep = jnp.where(my_section == bound + 1, x_cur, x_keep)

    last_live = lax.dynamic_index_in_dim(live_list[section_count - 1], replica, 1, keepdims=False)
    up_piece = jnp.where(
        last_live[None, :, :, None], cotangent.transpose(2, 0, 1, 3), jnp.zeros((), jnp.bfloat16)
    )
    up_full = gather_rows(up_piece)
    up_keep = up_full
    for depth in reversed(range(1, section_count)):
        grad_piece = backward_piece(
            x_keep, up_full, up_piece, weight_in, weight_out, scale_in, scale_out, shard_idx
        )
        straight, crossed = cross_boundary(grad_piece, depth, depth - 1, replicas)
        sources = jnp.stack(
            [jnp.where(replica == h, straight, crossed) for h in range(replicas)]
        )[:, 0]
        mine = lax.dynamic_index_in_dim(link_list[depth - 1], replica, 1, keepdims=False)
        up_piece = jnp.einsum(
            "mjdk,dmkD->mjD", mine.astype(jnp.bfloat16), sources,
            preferred_element_type=jnp.float32,
        ).astype(jnp.bfloat16)[None]
        up_full = gather_rows(up_piece)
        up_keep = jnp.where(my_section == depth - 1, up_full, up_keep)

    accum_in, accum_out = weight_grads(x_keep, up_keep, weight_in, weight_out, scale_in, scale_out)
    stepped_in = (weight_in.astype(jnp.float32) - LEARNING * accum_in).astype(jnp.bfloat16)
    stepped_out = (weight_out.astype(jnp.float32) - LEARNING * accum_out).astype(jnp.bfloat16)
    partner = gossip_peer[my_section, replica]
    paired = partner != replica
    swap = [(h, replicas - 1 - h) for h in range(replicas)]
    other_in = lax.ppermute(stepped_in, "half", swap)
    other_out = lax.ppermute(stepped_out, "half", swap)
    chosen_in = jnp.where(paired, other_in, stepped_in)
    chosen_out = jnp.where(paired, other_out, stepped_out)
    new_in = (0.5 * (stepped_in.astype(jnp.float32) + chosen_in.astype(jnp.float32))).astype(
        jnp.bfloat16
    )
    new_out = (0.5 * (stepped_out.astype(jnp.float32) + chosen_out.astype(jnp.float32))).astype(
        jnp.bfloat16
    )
    return (new_in[None], new_out[None])


def solution(mesh):
    sections = mesh.shape["section"]
    reps = mesh.shape["rep"]
    inner = Mesh(np.asarray(mesh.devices).reshape(sections, 2, reps // 2), ("section", "half", "plane"))
    rows = ("half", "plane")
    return jax.shard_map(
        on_device,
        mesh=inner,
        in_specs=(
            P(None, None, rows, None),
            P(),
            P(None, None, rows, None),
            P(),
            P("section", None, rows),
            P("section", rows, None),
        ),
        out_specs=(P("section", None, rows), P("section", rows, None)),
        check_vma=False,
    )
```

```python
import numpy as np
import jax
import jax.numpy as jnp
from jax import lax
from jax.experimental import pallas as pl
from jax.experimental.pallas import tpu as pltpu
from jax.sharding import Mesh, PartitionSpec as P

EPSILON = 1e-06
GELU_SCALE = 0.7978845608028654
LEARNING = 8.0
PAIR = ("section", "half")


def gelu_parts(preact):
    inner = GELU_SCALE * (preact + 0.044715 * preact * preact * preact)
    tanh_val = jnp.tanh(inner)
    gelu_val = 0.5 * preact * (1.0 + tanh_val)
    slopes = 0.5 * (1.0 + tanh_val) + 0.5 * preact * (1.0 - tanh_val * tanh_val) * GELU_SCALE * (
        1.0 + 3.0 * 0.044715 * preact * preact
    )
    return (gelu_val, slopes)


def route_tables(routes, blocks):
    micro_count, bound_count, replicas, capacity = routes.shape
    slot_ids = jnp.arange(capacity, dtype=jnp.int32)
    replica_ids = jnp.arange(replicas, dtype=jnp.int32)
    live_now = jnp.broadcast_to(slot_ids[None, None, :] < blocks, (micro_count, replicas, capacity))
    link_list = []
    live_list = [live_now]
    for bound_idx in range(bound_count):
        target = jnp.where(live_now, routes[:, bound_idx], -1).reshape(
            micro_count, replicas * capacity
        )
        matches = (target[:, :, None] == replica_ids[None, None, :]).astype(jnp.int32)
        before = jnp.cumsum(matches, axis=1) - matches
        position = jnp.sum(matches * before, axis=2)
        link_table = matches[:, :, :, None] * (
            position[:, :, None, None] == slot_ids[None, None, None, :]
        ).astype(jnp.int32)
        link_table = link_table.reshape(micro_count, replicas, capacity, replicas, capacity)
        link_list.append(link_table.astype(jnp.float32))
        live_now = jnp.sum(link_table, axis=(1, 2)) > 0
        live_list.append(live_now)
    return (link_list, live_list)


def layer_front(flat_rows, weight_in, scale_in):
    widened = flat_rows.astype(jnp.float32)
    inverse = lax.rsqrt(jnp.mean(widened * widened, axis=-1, keepdims=True) + EPSILON)
    normed = (widened * inverse).astype(jnp.bfloat16)
    preact = jnp.dot(normed, weight_in, preferred_element_type=jnp.float32) * scale_in
    return (widened, inverse, normed, preact)


def plane_kernel(count, spread, x_ref, out_ref, held, send_sem, recv_sem):
    section = lax.axis_index("section")
    half = lax.axis_index("half")
    me = lax.axis_index("plane")
    barrier = pltpu.get_barrier_semaphore()
    for step in range(1, count):
        peer = lax.rem(me + step, count)
        pl.semaphore_signal(
            barrier, inc=1, device_id=(section, half, peer), device_id_type=pl.DeviceIdType.MESH
        )
    pl.semaphore_wait(barrier, count - 1)
    copies = []
    for step in range(1, count):
        peer = lax.rem(me + step, count)
        copy = pltpu.make_async_remote_copy(
            src_ref=x_ref.at[0] if spread else x_ref.at[peer],
            dst_ref=held.at[me],
            send_sem=send_sem.at[step],
            recv_sem=recv_sem.at[step],
            device_id=(section, half, peer),
            device_id_type=pl.DeviceIdType.MESH,
        )
        copy.start()
        copies.append(copy)
    own = x_ref[0] if spread else x_ref[me]
    for copy in copies:
        copy.wait()
    out_ref[...] = held[...]
    out_ref[me] = own


def plane_call(value, count, spread, ident):
    shape = (count,) + value.shape[1:]
    return pl.pallas_call(
        lambda *refs: plane_kernel(count, spread, *refs),
        out_shape=jax.ShapeDtypeStruct(shape, value.dtype),
        in_specs=[pl.BlockSpec(memory_space=pltpu.VMEM)],
        out_specs=pl.BlockSpec(memory_space=pltpu.VMEM),
        scratch_shapes=[
            pltpu.VMEM(shape, value.dtype),
            pltpu.SemaphoreType.DMA((count,)),
            pltpu.SemaphoreType.DMA((count,)),
        ],
        compiler_params=pltpu.CompilerParams(collective_id=ident, has_side_effects=True),
    )(value)


def gather_rows(piece):
    return plane_call(piece, lax.axis_size("plane"), True, 1)


def sum_rows(partial_value):
    parts = plane_call(partial_value.astype(jnp.bfloat16), lax.axis_size("plane"), False, 0)
    return jnp.sum(parts.astype(jnp.float32), axis=0, keepdims=True)


def own_rows(full, shard_idx):
    return lax.dynamic_slice_in_dim(full, shard_idx, 1, axis=0)


def forward_piece(x_full, weight_in, weight_out, scale_in, scale_out, shard_idx):
    shape = x_full.shape
    widened, inverse, normed, preact = layer_front(x_full.reshape(-1, shape[-1]), weight_in, scale_in)
    gelu_val, slopes = gelu_parts(preact)
    activated = gelu_val.astype(jnp.bfloat16)
    partial_value = jnp.dot(activated, weight_out, preferred_element_type=jnp.float32) * scale_out
    summed = sum_rows(partial_value.reshape(shape))
    return (own_rows(x_full, shard_idx).astype(jnp.float32) + summed).astype(jnp.bfloat16)


def backward_piece(x_full, up_full, up_piece, weight_in, weight_out, scale_in, scale_out, shard_idx):
    shape = x_full.shape
    widened, inverse, normed, preact = layer_front(x_full.reshape(-1, shape[-1]), weight_in, scale_in)
    gelu_val, slopes = gelu_parts(preact)
    d_act = (
        lax.dot_general(
            up_full.reshape(-1, shape[-1]), weight_out, (((1,), (1,)), ((), ())),
            preferred_element_type=jnp.float32,
        )
        * scale_out
    )
    d_pre = (d_act * slopes).astype(jnp.bfloat16)
    d_normed = (
        lax.dot_general(d_pre, weight_in, (((1,), (1,)), ((), ())), preferred_element_type=jnp.float32)
        * scale_in
    )
    normed_piece = sum_rows(d_normed.reshape(shape))
    wide_piece = own_rows(x_full, shard_idx).astype(jnp.float32)
    inv_piece = own_rows(inverse.reshape(shape[:-1] + (1,)), shard_idx)
    grad_piece = (
        up_piece.astype(jnp.float32)
        + inv_piece * normed_piece
        - wide_piece
        * inv_piece
        * inv_piece
        * inv_piece
        * jnp.mean(normed_piece * wide_piece, axis=-1, keepdims=True)
    )
    return grad_piece.astype(jnp.bfloat16)


def weight_grads(x_full, up_full, weight_in, weight_out, scale_in, scale_out):
    width = x_full.shape[-1]
    widened, inverse, normed, preact = layer_front(x_full.reshape(-1, width), weight_in, scale_in)
    gelu_val, slopes = gelu_parts(preact)
    activated = gelu_val.astype(jnp.bfloat16)
    ups = up_full.reshape(-1, width)
    d_out = (
        lax.dot_general(activated, ups, (((0,), (0,)), ((), ())), preferred_element_type=jnp.float32)
        * scale_out
    )
    d_act = (
        lax.dot_general(ups, weight_out, (((1,), (1,)), ((), ())), preferred_element_type=jnp.float32)
        * scale_out
    )
    d_pre = (d_act * slopes).astype(jnp.bfloat16)
    d_in = (
        lax.dot_general(normed, d_pre, (((0,), (0,)), ((), ())), preferred_element_type=jnp.float32)
        * scale_in
    )
    return (d_in, d_out)


def cross_boundary(piece, source, target, replicas):
    straight = [(source * replicas + h, target * replicas + h) for h in range(replicas)]
    crossed = [(source * replicas + h, target * replicas + (replicas - 1 - h)) for h in range(replicas)]
    return (lax.ppermute(piece, PAIR, straight), lax.ppermute(piece, PAIR, crossed))


def on_device(block_inputs, routes, cotangent, gossip_peer, w_in, w_out):
    section_count = lax.axis_size("section")
    replicas = lax.axis_size("half")
    group_size = lax.axis_size("plane")
    my_section = lax.axis_index("section")
    replica = lax.axis_index("half")
    shard_idx = lax.axis_index("plane")
    micro_count, blocks, piece_rows, model_width = block_inputs.shape
    capacity = cotangent.shape[1]
    weight_in = w_in[0]
    weight_out = w_out[0]
    hidden = weight_in.shape[1]
    scale_in = model_width ** (-0.5)
    scale_out = (hidden * group_size) ** (-0.5)
    link_list, live_list = route_tables(routes, blocks)

    opening = jnp.concatenate(
        [
            block_inputs,
            jnp.zeros((micro_count, capacity - blocks, piece_rows, model_width), jnp.bfloat16),
        ],
        axis=1,
    ).transpose(2, 0, 1, 3)
    x_cur = gather_rows(opening)
    x_keep = x_cur
    for bound in range(section_count - 1):
        piece = forward_piece(x_cur, weight_in, weight_out, scale_in, scale_out, shard_idx)
        straight, crossed = cross_boundary(piece, bound, bound + 1, replicas)
        sources = jnp.stack(
            [jnp.where(replica == h, straight, crossed) for h in range(replicas)]
        )[:, 0]
        mine = lax.dynamic_index_in_dim(link_list[bound], replica, 3, keepdims=False)
        routed = jnp.einsum(
            "mqjk,qmjd->mkd", mine.astype(jnp.bfloat16), sources,
            preferred_element_type=jnp.float32,
        ).astype(jnp.bfloat16)[None]
        x_cur = gather_rows(routed)
        x_keep = jnp.where(my_section == bound + 1, x_cur, x_keep)

    last_live = lax.dynamic_index_in_dim(live_list[section_count - 1], replica, 1, keepdims=False)
    up_piece = jnp.where(
        last_live[None, :, :, None], cotangent.transpose(2, 0, 1, 3), jnp.zeros((), jnp.bfloat16)
    )
    up_full = gather_rows(up_piece)
    up_keep = up_full
    for depth in reversed(range(1, section_count)):
        grad_piece = backward_piece(
            x_keep, up_full, up_piece, weight_in, weight_out, scale_in, scale_out, shard_idx
        )
        straight, crossed = cross_boundary(grad_piece, depth, depth - 1, replicas)
        sources = jnp.stack(
            [jnp.where(replica == h, straight, crossed) for h in range(replicas)]
        )[:, 0]
        mine = lax.dynamic_index_in_dim(link_list[depth - 1], replica, 1, keepdims=False)
        up_piece = jnp.einsum(
            "mjdk,dmkD->mjD", mine.astype(jnp.bfloat16), sources,
            preferred_element_type=jnp.float32,
        ).astype(jnp.bfloat16)[None]
        up_full = gather_rows(up_piece)
        up_keep = jnp.where(my_section == depth - 1, up_full, up_keep)

    accum_in, accum_out = weight_grads(x_keep, up_keep, weight_in, weight_out, scale_in, scale_out)
    stepped_in = (weight_in.astype(jnp.float32) - LEARNING * accum_in).astype(jnp.bfloat16)
    stepped_out = (weight_out.astype(jnp.float32) - LEARNING * accum_out).astype(jnp.bfloat16)
    partner = gossip_peer[my_section, replica]
    paired = partner != replica
    swap = [(h, replicas - 1 - h) for h in range(replicas)]
    other_in = lax.ppermute(stepped_in, "half", swap)
    other_out = lax.ppermute(stepped_out, "half", swap)
    chosen_in = jnp.where(paired, other_in, stepped_in)
    chosen_out = jnp.where(paired, other_out, stepped_out)
    new_in = (0.5 * (stepped_in.astype(jnp.float32) + chosen_in.astype(jnp.float32))).astype(
        jnp.bfloat16
    )
    new_out = (0.5 * (stepped_out.astype(jnp.float32) + chosen_out.astype(jnp.float32))).astype(
        jnp.bfloat16
    )
    return (new_in[None], new_out[None])


def solution(mesh):
    sections = mesh.shape["section"]
    reps = mesh.shape["rep"]
    inner = Mesh(np.asarray(mesh.devices).reshape(sections, 2, reps // 2), ("section", "half", "plane"))
    rows = ("half", "plane")
    return jax.shard_map(
        on_device,
        mesh=inner,
        in_specs=(
            P(None, None, rows, None),
            P(),
            P(None, None, rows, None),
            P(),
            P("section", None, rows),
            P("section", rows, None),
        ),
        out_specs=(P("section", None, rows), P("section", rows, None)),
        check_vma=False,
    )
```

```python
import numpy as np
import jax
import jax.numpy as jnp
from jax import lax
from jax.experimental import pallas as pl
from jax.experimental.pallas import tpu as pltpu
from jax.sharding import Mesh, PartitionSpec as P

EPSILON = 1e-06
GELU_SCALE = 0.7978845608028654
LEARNING = 8.0
PAIR = ("section", "half")


def gelu_parts(preact):
    inner = GELU_SCALE * (preact + 0.044715 * preact * preact * preact)
    tanh_val = jnp.tanh(inner)
    gelu_val = 0.5 * preact * (1.0 + tanh_val)
    slopes = 0.5 * (1.0 + tanh_val) + 0.5 * preact * (1.0 - tanh_val * tanh_val) * GELU_SCALE * (
        1.0 + 3.0 * 0.044715 * preact * preact
    )
    return (gelu_val, slopes)


def route_tables(routes, blocks):
    micro_count, bound_count, replicas, capacity = routes.shape
    slot_ids = jnp.arange(capacity, dtype=jnp.int32)
    replica_ids = jnp.arange(replicas, dtype=jnp.int32)
    live_now = jnp.broadcast_to(slot_ids[None, None, :] < blocks, (micro_count, replicas, capacity))
    link_list = []
    live_list = [live_now]
    for bound_idx in range(bound_count):
        target = jnp.where(live_now, routes[:, bound_idx], -1).reshape(
            micro_count, replicas * capacity
        )
        matches = (target[:, :, None] == replica_ids[None, None, :]).astype(jnp.int32)
        before = jnp.cumsum(matches, axis=1) - matches
        position = jnp.sum(matches * before, axis=2)
        link_table = matches[:, :, :, None] * (
            position[:, :, None, None] == slot_ids[None, None, None, :]
        ).astype(jnp.int32)
        link_table = link_table.reshape(micro_count, replicas, capacity, replicas, capacity)
        link_list.append(link_table.astype(jnp.float32))
        live_now = jnp.sum(link_table, axis=(1, 2)) > 0
        live_list.append(live_now)
    return (link_list, live_list)


def layer_front(flat_rows, weight_in, scale_in):
    widened = flat_rows.astype(jnp.float32)
    inverse = lax.rsqrt(jnp.mean(widened * widened, axis=-1, keepdims=True) + EPSILON)
    normed = (widened * inverse).astype(jnp.bfloat16)
    preact = jnp.dot(normed, weight_in, preferred_element_type=jnp.float32) * scale_in
    return (widened, inverse, normed, preact)


def plane_kernel(count, spread, x_ref, out_ref, held, send_sem, recv_sem):
    section = lax.axis_index("section")
    half = lax.axis_index("half")
    me = lax.axis_index("plane")
    barrier = pltpu.get_barrier_semaphore()
    for step in range(1, count):
        peer = lax.rem(me + step, count)
        pl.semaphore_signal(
            barrier, inc=1, device_id=(section, half, peer), device_id_type=pl.DeviceIdType.MESH
        )
    pl.semaphore_wait(barrier, count - 1)
    copies = []
    for step in range(1, count):
        peer = lax.rem(me + step, count)
        copy = pltpu.make_async_remote_copy(
            src_ref=x_ref.at[0] if spread else x_ref.at[peer],
            dst_ref=held.at[me],
            send_sem=send_sem.at[step],
            recv_sem=recv_sem.at[step],
            device_id=(section, half, peer),
            device_id_type=pl.DeviceIdType.MESH,
        )
        copy.start()
        copies.append(copy)
    own = x_ref[0] if spread else x_ref[me]
    for copy in copies:
        copy.wait()
    out_ref[...] = held[...]
    out_ref[me] = own


def plane_call(value, count, spread, ident):
    lanes = value[0].size // 16
    dense = plane_dense(value.reshape(value.shape[0], 16, lanes), count, spread, ident)
    return dense.reshape((count,) + value.shape[1:])


def plane_dense(value, count, spread, ident):
    shape = (count,) + value.shape[1:]
    return pl.pallas_call(
        lambda *refs: plane_kernel(count, spread, *refs),
        out_shape=jax.ShapeDtypeStruct(shape, value.dtype),
        in_specs=[pl.BlockSpec(memory_space=pltpu.VMEM)],
        out_specs=pl.BlockSpec(memory_space=pltpu.VMEM),
        scratch_shapes=[
            pltpu.VMEM(shape, value.dtype),
            pltpu.SemaphoreType.DMA((count,)),
            pltpu.SemaphoreType.DMA((count,)),
        ],
        compiler_params=pltpu.CompilerParams(collective_id=ident, has_side_effects=True),
    )(value)


def gather_rows(piece):
    return plane_call(piece, lax.axis_size("plane"), True, 1)


def sum_rows(partial_value):
    parts = plane_call(partial_value.astype(jnp.bfloat16), lax.axis_size("plane"), False, 0)
    return jnp.sum(parts.astype(jnp.float32), axis=0, keepdims=True)


def own_rows(full, shard_idx):
    return lax.dynamic_slice_in_dim(full, shard_idx, 1, axis=0)


def forward_piece(x_full, weight_in, weight_out, scale_in, scale_out, shard_idx):
    shape = x_full.shape
    widened, inverse, normed, preact = layer_front(x_full.reshape(-1, shape[-1]), weight_in, scale_in)
    gelu_val, slopes = gelu_parts(preact)
    activated = gelu_val.astype(jnp.bfloat16)
    partial_value = jnp.dot(activated, weight_out, preferred_element_type=jnp.float32) * scale_out
    summed = sum_rows(partial_value.reshape(shape))
    return (own_rows(x_full, shard_idx).astype(jnp.float32) + summed).astype(jnp.bfloat16)


def backward_piece(x_full, up_full, up_piece, weight_in, weight_out, scale_in, scale_out, shard_idx):
    shape = x_full.shape
    widened, inverse, normed, preact = layer_front(x_full.reshape(-1, shape[-1]), weight_in, scale_in)
    gelu_val, slopes = gelu_parts(preact)
    d_act = (
        lax.dot_general(
            up_full.reshape(-1, shape[-1]), weight_out, (((1,), (1,)), ((), ())),
            preferred_element_type=jnp.float32,
        )
        * scale_out
    )
    d_pre = (d_act * slopes).astype(jnp.bfloat16)
    d_normed = (
        lax.dot_general(d_pre, weight_in, (((1,), (1,)), ((), ())), preferred_element_type=jnp.float32)
        * scale_in
    )
    normed_piece = sum_rows(d_normed.reshape(shape))
    wide_piece = own_rows(x_full, shard_idx).astype(jnp.float32)
    inv_piece = own_rows(inverse.reshape(shape[:-1] + (1,)), shard_idx)
    grad_piece = (
        up_piece.astype(jnp.float32)
        + inv_piece * normed_piece
        - wide_piece
        * inv_piece
        * inv_piece
        * inv_piece
        * jnp.mean(normed_piece * wide_piece, axis=-1, keepdims=True)
    )
    return grad_piece.astype(jnp.bfloat16)


def weight_grads(x_full, up_full, weight_in, weight_out, scale_in, scale_out):
    width = x_full.shape[-1]
    widened, inverse, normed, preact = layer_front(x_full.reshape(-1, width), weight_in, scale_in)
    gelu_val, slopes = gelu_parts(preact)
    activated = gelu_val.astype(jnp.bfloat16)
    ups = up_full.reshape(-1, width)
    d_out = (
        lax.dot_general(activated, ups, (((0,), (0,)), ((), ())), preferred_element_type=jnp.float32)
        * scale_out
    )
    d_act = (
        lax.dot_general(ups, weight_out, (((1,), (1,)), ((), ())), preferred_element_type=jnp.float32)
        * scale_out
    )
    d_pre = (d_act * slopes).astype(jnp.bfloat16)
    d_in = (
        lax.dot_general(normed, d_pre, (((0,), (0,)), ((), ())), preferred_element_type=jnp.float32)
        * scale_in
    )
    return (d_in, d_out)


def cross_boundary(piece, source, target, replicas):
    straight = [(source * replicas + h, target * replicas + h) for h in range(replicas)]
    crossed = [(source * replicas + h, target * replicas + (replicas - 1 - h)) for h in range(replicas)]
    return (lax.ppermute(piece, PAIR, straight), lax.ppermute(piece, PAIR, crossed))


def on_device(block_inputs, routes, cotangent, gossip_peer, w_in, w_out):
    section_count = lax.axis_size("section")
    replicas = lax.axis_size("half")
    group_size = lax.axis_size("plane")
    my_section = lax.axis_index("section")
    replica = lax.axis_index("half")
    shard_idx = lax.axis_index("plane")
    micro_count, blocks, piece_rows, model_width = block_inputs.shape
    capacity = cotangent.shape[1]
    weight_in = w_in[0]
    weight_out = w_out[0]
    hidden = weight_in.shape[1]
    scale_in = model_width ** (-0.5)
    scale_out = (hidden * group_size) ** (-0.5)
    link_list, live_list = route_tables(routes, blocks)

    opening = jnp.concatenate(
        [
            block_inputs,
            jnp.zeros((micro_count, capacity - blocks, piece_rows, model_width), jnp.bfloat16),
        ],
        axis=1,
    ).transpose(2, 0, 1, 3)
    x_cur = gather_rows(opening)
    x_keep = x_cur
    for bound in range(section_count - 1):
        piece = forward_piece(x_cur, weight_in, weight_out, scale_in, scale_out, shard_idx)
        straight, crossed = cross_boundary(piece, bound, bound + 1, replicas)
        sources = jnp.stack(
            [jnp.where(replica == h, straight, crossed) for h in range(replicas)]
        )[:, 0]
        mine = lax.dynamic_index_in_dim(link_list[bound], replica, 3, keepdims=False)
        routed = jnp.einsum(
            "mqjk,qmjd->mkd", mine.astype(jnp.bfloat16), sources,
            preferred_element_type=jnp.float32,
        ).astype(jnp.bfloat16)[None]
        x_cur = gather_rows(routed)
        x_keep = jnp.where(my_section == bound + 1, x_cur, x_keep)

    last_live = lax.dynamic_index_in_dim(live_list[section_count - 1], replica, 1, keepdims=False)
    up_piece = jnp.where(
        last_live[None, :, :, None], cotangent.transpose(2, 0, 1, 3), jnp.zeros((), jnp.bfloat16)
    )
    up_full = gather_rows(up_piece)
    up_keep = up_full
    for depth in reversed(range(1, section_count)):
        grad_piece = backward_piece(
            x_keep, up_full, up_piece, weight_in, weight_out, scale_in, scale_out, shard_idx
        )
        straight, crossed = cross_boundary(grad_piece, depth, depth - 1, replicas)
        sources = jnp.stack(
            [jnp.where(replica == h, straight, crossed) for h in range(replicas)]
        )[:, 0]
        mine = lax.dynamic_index_in_dim(link_list[depth - 1], replica, 1, keepdims=False)
        up_piece = jnp.einsum(
            "mjdk,dmkD->mjD", mine.astype(jnp.bfloat16), sources,
            preferred_element_type=jnp.float32,
        ).astype(jnp.bfloat16)[None]
        up_full = gather_rows(up_piece)
        up_keep = jnp.where(my_section == depth - 1, up_full, up_keep)

    accum_in, accum_out = weight_grads(x_keep, up_keep, weight_in, weight_out, scale_in, scale_out)
    stepped_in = (weight_in.astype(jnp.float32) - LEARNING * accum_in).astype(jnp.bfloat16)
    stepped_out = (weight_out.astype(jnp.float32) - LEARNING * accum_out).astype(jnp.bfloat16)
    partner = gossip_peer[my_section, replica]
    paired = partner != replica
    swap = [(h, replicas - 1 - h) for h in range(replicas)]
    other_in = lax.ppermute(stepped_in, "half", swap)
    other_out = lax.ppermute(stepped_out, "half", swap)
    chosen_in = jnp.where(paired, other_in, stepped_in)
    chosen_out = jnp.where(paired, other_out, stepped_out)
    new_in = (0.5 * (stepped_in.astype(jnp.float32) + chosen_in.astype(jnp.float32))).astype(
        jnp.bfloat16
    )
    new_out = (0.5 * (stepped_out.astype(jnp.float32) + chosen_out.astype(jnp.float32))).astype(
        jnp.bfloat16
    )
    return (new_in[None], new_out[None])


def solution(mesh):
    sections = mesh.shape["section"]
    reps = mesh.shape["rep"]
    inner = Mesh(np.asarray(mesh.devices).reshape(sections, 2, reps // 2), ("section", "half", "plane"))
    rows = ("half", "plane")
    return jax.shard_map(
        on_device,
        mesh=inner,
        in_specs=(
            P(None, None, rows, None),
            P(),
            P(None, None, rows, None),
            P(),
            P("section", None, rows),
            P("section", rows, None),
        ),
        out_specs=(P("section", None, rows), P("section", rows, None)),
        check_vma=False,
    )
```

```python
import numpy as np
import jax
import jax.numpy as jnp
from jax import lax
from jax.experimental import pallas as pl
from jax.experimental.pallas import tpu as pltpu
from jax.sharding import Mesh, PartitionSpec as P

EPSILON = 1e-06
GELU_SCALE = 0.7978845608028654
LEARNING = 8.0
PAIR = ("section", "half")


def gelu_parts(preact):
    inner = GELU_SCALE * (preact + 0.044715 * preact * preact * preact)
    tanh_val = jnp.tanh(inner)
    gelu_val = 0.5 * preact * (1.0 + tanh_val)
    slopes = 0.5 * (1.0 + tanh_val) + 0.5 * preact * (1.0 - tanh_val * tanh_val) * GELU_SCALE * (
        1.0 + 3.0 * 0.044715 * preact * preact
    )
    return (gelu_val, slopes)


def route_tables(routes, blocks):
    micro_count, bound_count, replicas, capacity = routes.shape
    slot_ids = jnp.arange(capacity, dtype=jnp.int32)
    replica_ids = jnp.arange(replicas, dtype=jnp.int32)
    live_now = jnp.broadcast_to(slot_ids[None, None, :] < blocks, (micro_count, replicas, capacity))
    link_list = []
    live_list = [live_now]
    for bound_idx in range(bound_count):
        target = jnp.where(live_now, routes[:, bound_idx], -1).reshape(
            micro_count, replicas * capacity
        )
        matches = (target[:, :, None] == replica_ids[None, None, :]).astype(jnp.int32)
        before = jnp.cumsum(matches, axis=1) - matches
        position = jnp.sum(matches * before, axis=2)
        link_table = matches[:, :, :, None] * (
            position[:, :, None, None] == slot_ids[None, None, None, :]
        ).astype(jnp.int32)
        link_table = link_table.reshape(micro_count, replicas, capacity, replicas, capacity)
        link_list.append(link_table.astype(jnp.float32))
        live_now = jnp.sum(link_table, axis=(1, 2)) > 0
        live_list.append(live_now)
    return (link_list, live_list)


def layer_front(flat_rows, weight_in, scale_in):
    widened = flat_rows.astype(jnp.float32)
    inverse = lax.rsqrt(jnp.mean(widened * widened, axis=-1, keepdims=True) + EPSILON)
    normed = (widened * inverse).astype(jnp.bfloat16)
    preact = jnp.dot(normed, weight_in, preferred_element_type=jnp.float32) * scale_in
    return (widened, inverse, normed, preact)


def plane_kernel(count, spread, x_ref, out_ref, held, send_sem, recv_sem):
    section = lax.axis_index("section")
    half = lax.axis_index("half")
    me = lax.axis_index("plane")
    barrier = pltpu.get_barrier_semaphore()
    for step in range(1, count):
        peer = lax.rem(me + step, count)
        pl.semaphore_signal(
            barrier, inc=1, device_id=(section, half, peer), device_id_type=pl.DeviceIdType.MESH
        )
    pl.semaphore_wait(barrier, count - 1)
    copies = []
    for step in range(1, count):
        peer = lax.rem(me + step, count)
        copy = pltpu.make_async_remote_copy(
            src_ref=x_ref.at[0] if spread else x_ref.at[peer],
            dst_ref=held.at[me],
            send_sem=send_sem.at[step],
            recv_sem=recv_sem.at[step],
            device_id=(section, half, peer),
            device_id_type=pl.DeviceIdType.MESH,
        )
        copy.start()
        copies.append(copy)
    own = x_ref[0] if spread else x_ref[me]
    for copy in copies:
        copy.wait()
    out_ref[...] = held[...]
    out_ref[me] = own


def plane_call(value, count, spread, ident):
    lanes = value[0].size // 16
    dense = plane_dense(value.reshape(value.shape[0], 16, lanes), count, spread, ident)
    return dense.reshape((count,) + value.shape[1:])


def plane_dense(value, count, spread, ident):
    shape = (count,) + value.shape[1:]
    return pl.pallas_call(
        lambda *refs: plane_kernel(count, spread, *refs),
        out_shape=jax.ShapeDtypeStruct(shape, value.dtype),
        in_specs=[pl.BlockSpec(memory_space=pltpu.VMEM)],
        out_specs=pl.BlockSpec(memory_space=pltpu.VMEM),
        scratch_shapes=[
            pltpu.VMEM(shape, value.dtype),
            pltpu.SemaphoreType.DMA((count,)),
            pltpu.SemaphoreType.DMA((count,)),
        ],
        compiler_params=pltpu.CompilerParams(collective_id=ident, has_side_effects=True),
    )(value)


def gather_rows(piece):
    return plane_call(piece, lax.axis_size("plane"), True, 1)


def sum_rows(partial_value):
    parts = plane_call(partial_value.astype(jnp.bfloat16), lax.axis_size("plane"), False, 0)
    return jnp.sum(parts.astype(jnp.float32), axis=0, keepdims=True)


def own_rows(full, shard_idx):
    return lax.dynamic_slice_in_dim(full, shard_idx, 1, axis=0)


def forward_piece(x_full, weight_in, weight_out, scale_in, scale_out, shard_idx):
    shape = x_full.shape
    widened, inverse, normed, preact = layer_front(x_full.reshape(-1, shape[-1]), weight_in, scale_in)
    gelu_val, slopes = gelu_parts(preact)
    activated = gelu_val.astype(jnp.bfloat16)
    partial_value = jnp.dot(activated, weight_out, preferred_element_type=jnp.float32) * scale_out
    summed = sum_rows(partial_value.reshape(shape))
    return (own_rows(x_full, shard_idx).astype(jnp.float32) + summed).astype(jnp.bfloat16)


def backward_piece(x_full, up_full, up_piece, weight_in, weight_out, scale_in, scale_out, shard_idx):
    shape = x_full.shape
    widened, inverse, normed, preact = layer_front(x_full.reshape(-1, shape[-1]), weight_in, scale_in)
    gelu_val, slopes = gelu_parts(preact)
    d_act = (
        lax.dot_general(
            up_full.reshape(-1, shape[-1]), weight_out, (((1,), (1,)), ((), ())),
            preferred_element_type=jnp.float32,
        )
        * scale_out
    )
    d_pre = (d_act * slopes).astype(jnp.bfloat16)
    d_normed = (
        lax.dot_general(d_pre, weight_in, (((1,), (1,)), ((), ())), preferred_element_type=jnp.float32)
        * scale_in
    )
    normed_piece = sum_rows(d_normed.reshape(shape))
    wide_piece = own_rows(x_full, shard_idx).astype(jnp.float32)
    inv_piece = own_rows(inverse.reshape(shape[:-1] + (1,)), shard_idx)
    grad_piece = (
        up_piece.astype(jnp.float32)
        + inv_piece * normed_piece
        - wide_piece
        * inv_piece
        * inv_piece
        * inv_piece
        * jnp.mean(normed_piece * wide_piece, axis=-1, keepdims=True)
    )
    return grad_piece.astype(jnp.bfloat16)


def weight_grads(x_full, up_full, weight_in, weight_out, scale_in, scale_out):
    width = x_full.shape[-1]
    widened, inverse, normed, preact = layer_front(x_full.reshape(-1, width), weight_in, scale_in)
    gelu_val, slopes = gelu_parts(preact)
    activated = gelu_val.astype(jnp.bfloat16)
    ups = up_full.reshape(-1, width)
    d_out = (
        lax.dot_general(activated, ups, (((0,), (0,)), ((), ())), preferred_element_type=jnp.float32)
        * scale_out
    )
    d_act = (
        lax.dot_general(ups, weight_out, (((1,), (1,)), ((), ())), preferred_element_type=jnp.float32)
        * scale_out
    )
    d_pre = (d_act * slopes).astype(jnp.bfloat16)
    d_in = (
        lax.dot_general(normed, d_pre, (((0,), (0,)), ((), ())), preferred_element_type=jnp.float32)
        * scale_in
    )
    return (d_in, d_out)


def cross_boundary(piece, source, target, replicas):
    straight = [(source * replicas + h, target * replicas + h) for h in range(replicas)]
    crossed = [(source * replicas + h, target * replicas + (replicas - 1 - h)) for h in range(replicas)]
    return (lax.ppermute(piece, PAIR, straight), lax.ppermute(piece, PAIR, crossed))


def swap_sections(stepped_in, stepped_out, chosen, section_count, replicas):
    pairs = [
        (section * replicas + h, section * replicas + replicas - 1 - h)
        for section in range(section_count)
        if (chosen >> section) & 1
        for h in range(replicas)
    ]
    if not pairs:
        return (jnp.zeros_like(stepped_in), jnp.zeros_like(stepped_out))
    return (lax.ppermute(stepped_in, PAIR, pairs), lax.ppermute(stepped_out, PAIR, pairs))


def on_device(block_inputs, routes, cotangent, gossip_peer, w_in, w_out):
    section_count = lax.axis_size("section")
    replicas = lax.axis_size("half")
    group_size = lax.axis_size("plane")
    my_section = lax.axis_index("section")
    replica = lax.axis_index("half")
    shard_idx = lax.axis_index("plane")
    micro_count, blocks, piece_rows, model_width = block_inputs.shape
    capacity = cotangent.shape[1]
    weight_in = w_in[0]
    weight_out = w_out[0]
    hidden = weight_in.shape[1]
    scale_in = model_width ** (-0.5)
    scale_out = (hidden * group_size) ** (-0.5)
    link_list, live_list = route_tables(routes, blocks)

    opening = jnp.concatenate(
        [
            block_inputs,
            jnp.zeros((micro_count, capacity - blocks, piece_rows, model_width), jnp.bfloat16),
        ],
        axis=1,
    ).transpose(2, 0, 1, 3)
    x_cur = gather_rows(opening)
    x_keep = x_cur
    for bound in range(section_count - 1):
        piece = forward_piece(x_cur, weight_in, weight_out, scale_in, scale_out, shard_idx)
        straight, crossed = cross_boundary(piece, bound, bound + 1, replicas)
        sources = jnp.stack(
            [jnp.where(replica == h, straight, crossed) for h in range(replicas)]
        )[:, 0]
        mine = lax.dynamic_index_in_dim(link_list[bound], replica, 3, keepdims=False)
        routed = jnp.einsum(
            "mqjk,qmjd->mkd", mine.astype(jnp.bfloat16), sources,
            preferred_element_type=jnp.float32,
        ).astype(jnp.bfloat16)[None]
        x_cur = gather_rows(routed)
        x_keep = jnp.where(my_section == bound + 1, x_cur, x_keep)

    last_live = lax.dynamic_index_in_dim(live_list[section_count - 1], replica, 1, keepdims=False)
    up_piece = jnp.where(
        last_live[None, :, :, None], cotangent.transpose(2, 0, 1, 3), jnp.zeros((), jnp.bfloat16)
    )
    up_full = gather_rows(up_piece)
    up_keep = up_full
    for depth in reversed(range(1, section_count)):
        grad_piece = backward_piece(
            x_keep, up_full, up_piece, weight_in, weight_out, scale_in, scale_out, shard_idx
        )
        straight, crossed = cross_boundary(grad_piece, depth, depth - 1, replicas)
        sources = jnp.stack(
            [jnp.where(replica == h, straight, crossed) for h in range(replicas)]
        )[:, 0]
        mine = lax.dynamic_index_in_dim(link_list[depth - 1], replica, 1, keepdims=False)
        up_piece = jnp.einsum(
            "mjdk,dmkD->mjD", mine.astype(jnp.bfloat16), sources,
            preferred_element_type=jnp.float32,
        ).astype(jnp.bfloat16)[None]
        up_full = gather_rows(up_piece)
        up_keep = jnp.where(my_section == depth - 1, up_full, up_keep)

    accum_in, accum_out = weight_grads(x_keep, up_keep, weight_in, weight_out, scale_in, scale_out)
    stepped_in = (weight_in.astype(jnp.float32) - LEARNING * accum_in).astype(jnp.bfloat16)
    stepped_out = (weight_out.astype(jnp.float32) - LEARNING * accum_out).astype(jnp.bfloat16)
    partner = gossip_peer[my_section, replica]
    paired = partner != replica
    pattern = jnp.sum(
        (gossip_peer[:, 0] != 0).astype(jnp.int32) << jnp.arange(section_count, dtype=jnp.int32)
    )
    other_in, other_out = lax.switch(
        pattern,
        [
            lambda a, b, chosen=chosen: swap_sections(a, b, chosen, section_count, replicas)
            for chosen in range(2**section_count)
        ],
        stepped_in,
        stepped_out,
    )
    chosen_in = jnp.where(paired, other_in, stepped_in)
    chosen_out = jnp.where(paired, other_out, stepped_out)
    new_in = (0.5 * (stepped_in.astype(jnp.float32) + chosen_in.astype(jnp.float32))).astype(
        jnp.bfloat16
    )
    new_out = (0.5 * (stepped_out.astype(jnp.float32) + chosen_out.astype(jnp.float32))).astype(
        jnp.bfloat16
    )
    return (new_in[None], new_out[None])


def solution(mesh):
    sections = mesh.shape["section"]
    reps = mesh.shape["rep"]
    inner = Mesh(np.asarray(mesh.devices).reshape(sections, 2, reps // 2), ("section", "half", "plane"))
    rows = ("half", "plane")
    return jax.shard_map(
        on_device,
        mesh=inner,
        in_specs=(
            P(None, None, rows, None),
            P(),
            P(None, None, rows, None),
            P(),
            P("section", None, rows),
            P("section", rows, None),
        ),
        out_specs=(P("section", None, rows), P("section", rows, None)),
        check_vma=False,
    )
```

```python
import numpy as np
import jax
import jax.numpy as jnp
from jax import lax
from jax.experimental import pallas as pl
from jax.experimental.pallas import tpu as pltpu
from jax.sharding import Mesh, PartitionSpec as P

EPSILON = 1e-06
GELU_SCALE = 0.7978845608028654
LEARNING = 8.0
PAIR = ("section", "half")


def gelu_parts(preact):
    inner = GELU_SCALE * (preact + 0.044715 * preact * preact * preact)
    tanh_val = jnp.tanh(inner)
    gelu_val = 0.5 * preact * (1.0 + tanh_val)
    slopes = 0.5 * (1.0 + tanh_val) + 0.5 * preact * (1.0 - tanh_val * tanh_val) * GELU_SCALE * (
        1.0 + 3.0 * 0.044715 * preact * preact
    )
    return (gelu_val, slopes)


def route_tables(routes, blocks):
    micro_count, bound_count, replicas, capacity = routes.shape
    slot_ids = jnp.arange(capacity, dtype=jnp.int32)
    replica_ids = jnp.arange(replicas, dtype=jnp.int32)
    live_now = jnp.broadcast_to(slot_ids[None, None, :] < blocks, (micro_count, replicas, capacity))
    link_list = []
    live_list = [live_now]
    for bound_idx in range(bound_count):
        target = jnp.where(live_now, routes[:, bound_idx], -1).reshape(
            micro_count, replicas * capacity
        )
        matches = (target[:, :, None] == replica_ids[None, None, :]).astype(jnp.int32)
        before = jnp.cumsum(matches, axis=1) - matches
        position = jnp.sum(matches * before, axis=2)
        link_table = matches[:, :, :, None] * (
            position[:, :, None, None] == slot_ids[None, None, None, :]
        ).astype(jnp.int32)
        link_table = link_table.reshape(micro_count, replicas, capacity, replicas, capacity)
        link_list.append(link_table.astype(jnp.float32))
        live_now = jnp.sum(link_table, axis=(1, 2)) > 0
        live_list.append(live_now)
    return (link_list, live_list)


def layer_front(flat_rows, weight_in, scale_in):
    widened = flat_rows.astype(jnp.float32)
    inverse = lax.rsqrt(jnp.mean(widened * widened, axis=-1, keepdims=True) + EPSILON)
    normed = (widened * inverse).astype(jnp.bfloat16)
    preact = jnp.dot(normed, weight_in, preferred_element_type=jnp.float32) * scale_in
    return (widened, inverse, normed, preact)


def plane_kernel(count, spread, active, x_ref, out_ref, held, send_sem, recv_sem):
    section = lax.axis_index("section")

    @pl.when(section == active)
    def _():
        plane_exchange(count, spread, section, x_ref, out_ref, held, send_sem, recv_sem)

    @pl.when(section != active)
    def _():
        out_ref[...] = jnp.zeros_like(out_ref)


def plane_exchange(count, spread, section, x_ref, out_ref, held, send_sem, recv_sem):
    half = lax.axis_index("half")
    me = lax.axis_index("plane")
    barrier = pltpu.get_barrier_semaphore()
    for step in range(1, count):
        peer = lax.rem(me + step, count)
        pl.semaphore_signal(
            barrier, inc=1, device_id=(section, half, peer), device_id_type=pl.DeviceIdType.MESH
        )
    pl.semaphore_wait(barrier, count - 1)
    copies = []
    for step in range(1, count):
        peer = lax.rem(me + step, count)
        copy = pltpu.make_async_remote_copy(
            src_ref=x_ref.at[0] if spread else x_ref.at[peer],
            dst_ref=held.at[me],
            send_sem=send_sem.at[step],
            recv_sem=recv_sem.at[step],
            device_id=(section, half, peer),
            device_id_type=pl.DeviceIdType.MESH,
        )
        copy.start()
        copies.append(copy)
    own = x_ref[0] if spread else x_ref[me]
    for copy in copies:
        copy.wait()
    out_ref[...] = held[...]
    out_ref[me] = own


def plane_call(value, count, spread, ident, active):
    lanes = value[0].size // 16
    dense = plane_dense(value.reshape(value.shape[0], 16, lanes), count, spread, ident, active)
    return dense.reshape((count,) + value.shape[1:])


def plane_dense(value, count, spread, ident, active):
    shape = (count,) + value.shape[1:]
    return pl.pallas_call(
        lambda *refs: plane_kernel(count, spread, active, *refs),
        out_shape=jax.ShapeDtypeStruct(shape, value.dtype),
        in_specs=[pl.BlockSpec(memory_space=pltpu.VMEM)],
        out_specs=pl.BlockSpec(memory_space=pltpu.VMEM),
        scratch_shapes=[
            pltpu.VMEM(shape, value.dtype),
            pltpu.SemaphoreType.DMA((count,)),
            pltpu.SemaphoreType.DMA((count,)),
        ],
        compiler_params=pltpu.CompilerParams(collective_id=ident, has_side_effects=True),
    )(value)


def gather_rows(piece, active):
    return plane_call(piece, lax.axis_size("plane"), True, 4 + active, active)


def sum_rows(partial_value, active):
    parts = plane_call(partial_value.astype(jnp.bfloat16), lax.axis_size("plane"), False, active, active)
    return jnp.sum(parts.astype(jnp.float32), axis=0, keepdims=True)


def own_rows(full, shard_idx):
    return lax.dynamic_slice_in_dim(full, shard_idx, 1, axis=0)


def forward_piece(x_full, weight_in, weight_out, scale_in, scale_out, shard_idx, active):
    shape = x_full.shape
    widened, inverse, normed, preact = layer_front(x_full.reshape(-1, shape[-1]), weight_in, scale_in)
    gelu_val, slopes = gelu_parts(preact)
    activated = gelu_val.astype(jnp.bfloat16)
    partial_value = jnp.dot(activated, weight_out, preferred_element_type=jnp.float32) * scale_out
    summed = sum_rows(partial_value.reshape(shape), active)
    return (own_rows(x_full, shard_idx).astype(jnp.float32) + summed).astype(jnp.bfloat16)


def backward_piece(
    x_full, up_full, up_piece, weight_in, weight_out, scale_in, scale_out, shard_idx, active
):
    shape = x_full.shape
    widened, inverse, normed, preact = layer_front(x_full.reshape(-1, shape[-1]), weight_in, scale_in)
    gelu_val, slopes = gelu_parts(preact)
    d_act = (
        lax.dot_general(
            up_full.reshape(-1, shape[-1]), weight_out, (((1,), (1,)), ((), ())),
            preferred_element_type=jnp.float32,
        )
        * scale_out
    )
    d_pre = (d_act * slopes).astype(jnp.bfloat16)
    d_normed = (
        lax.dot_general(d_pre, weight_in, (((1,), (1,)), ((), ())), preferred_element_type=jnp.float32)
        * scale_in
    )
    normed_piece = sum_rows(d_normed.reshape(shape), active)
    wide_piece = own_rows(x_full, shard_idx).astype(jnp.float32)
    inv_piece = own_rows(inverse.reshape(shape[:-1] + (1,)), shard_idx)
    grad_piece = (
        up_piece.astype(jnp.float32)
        + inv_piece * normed_piece
        - wide_piece
        * inv_piece
        * inv_piece
        * inv_piece
        * jnp.mean(normed_piece * wide_piece, axis=-1, keepdims=True)
    )
    return grad_piece.astype(jnp.bfloat16)


def weight_grads(x_full, up_full, weight_in, weight_out, scale_in, scale_out):
    width = x_full.shape[-1]
    widened, inverse, normed, preact = layer_front(x_full.reshape(-1, width), weight_in, scale_in)
    gelu_val, slopes = gelu_parts(preact)
    activated = gelu_val.astype(jnp.bfloat16)
    ups = up_full.reshape(-1, width)
    d_out = (
        lax.dot_general(activated, ups, (((0,), (0,)), ((), ())), preferred_element_type=jnp.float32)
        * scale_out
    )
    d_act = (
        lax.dot_general(ups, weight_out, (((1,), (1,)), ((), ())), preferred_element_type=jnp.float32)
        * scale_out
    )
    d_pre = (d_act * slopes).astype(jnp.bfloat16)
    d_in = (
        lax.dot_general(normed, d_pre, (((0,), (0,)), ((), ())), preferred_element_type=jnp.float32)
        * scale_in
    )
    return (d_in, d_out)


def cross_boundary(piece, source, target, replicas):
    straight = [(source * replicas + h, target * replicas + h) for h in range(replicas)]
    crossed = [(source * replicas + h, target * replicas + (replicas - 1 - h)) for h in range(replicas)]
    return (lax.ppermute(piece, PAIR, straight), lax.ppermute(piece, PAIR, crossed))


def swap_sections(stepped_in, stepped_out, chosen, section_count, replicas):
    pairs = [
        (section * replicas + h, section * replicas + replicas - 1 - h)
        for section in range(section_count)
        if (chosen >> section) & 1
        for h in range(replicas)
    ]
    if not pairs:
        return (jnp.zeros_like(stepped_in), jnp.zeros_like(stepped_out))
    return (lax.ppermute(stepped_in, PAIR, pairs), lax.ppermute(stepped_out, PAIR, pairs))


def on_device(block_inputs, routes, cotangent, gossip_peer, w_in, w_out):
    section_count = lax.axis_size("section")
    replicas = lax.axis_size("half")
    group_size = lax.axis_size("plane")
    my_section = lax.axis_index("section")
    replica = lax.axis_index("half")
    shard_idx = lax.axis_index("plane")
    micro_count, blocks, piece_rows, model_width = block_inputs.shape
    capacity = cotangent.shape[1]
    weight_in = w_in[0]
    weight_out = w_out[0]
    hidden = weight_in.shape[1]
    scale_in = model_width ** (-0.5)
    scale_out = (hidden * group_size) ** (-0.5)
    link_list, live_list = route_tables(routes, blocks)

    opening = jnp.concatenate(
        [
            block_inputs,
            jnp.zeros((micro_count, capacity - blocks, piece_rows, model_width), jnp.bfloat16),
        ],
        axis=1,
    ).transpose(2, 0, 1, 3)
    x_cur = gather_rows(opening, 0)
    x_keep = x_cur
    for bound in range(section_count - 1):
        piece = forward_piece(x_cur, weight_in, weight_out, scale_in, scale_out, shard_idx, bound)
        straight, crossed = cross_boundary(piece, bound, bound + 1, replicas)
        sources = jnp.stack(
            [jnp.where(replica == h, straight, crossed) for h in range(replicas)]
        )[:, 0]
        mine = lax.dynamic_index_in_dim(link_list[bound], replica, 3, keepdims=False)
        routed = jnp.einsum(
            "mqjk,qmjd->mkd", mine.astype(jnp.bfloat16), sources,
            preferred_element_type=jnp.float32,
        ).astype(jnp.bfloat16)[None]
        x_cur = gather_rows(routed, bound + 1)
        x_keep = jnp.where(my_section == bound + 1, x_cur, x_keep)

    last_live = lax.dynamic_index_in_dim(live_list[section_count - 1], replica, 1, keepdims=False)
    up_piece = jnp.where(
        last_live[None, :, :, None], cotangent.transpose(2, 0, 1, 3), jnp.zeros((), jnp.bfloat16)
    )
    up_full = gather_rows(up_piece, section_count - 1)
    up_keep = up_full
    for depth in reversed(range(1, section_count)):
        grad_piece = backward_piece(
            x_keep, up_full, up_piece, weight_in, weight_out, scale_in, scale_out, shard_idx, depth
        )
        straight, crossed = cross_boundary(grad_piece, depth, depth - 1, replicas)
        sources = jnp.stack(
            [jnp.where(replica == h, straight, crossed) for h in range(replicas)]
        )[:, 0]
        mine = lax.dynamic_index_in_dim(link_list[depth - 1], replica, 1, keepdims=False)
        up_piece = jnp.einsum(
            "mjdk,dmkD->mjD", mine.astype(jnp.bfloat16), sources,
            preferred_element_type=jnp.float32,
        ).astype(jnp.bfloat16)[None]
        up_full = gather_rows(up_piece, depth - 1)
        up_keep = jnp.where(my_section == depth - 1, up_full, up_keep)

    accum_in, accum_out = weight_grads(x_keep, up_keep, weight_in, weight_out, scale_in, scale_out)
    stepped_in = (weight_in.astype(jnp.float32) - LEARNING * accum_in).astype(jnp.bfloat16)
    stepped_out = (weight_out.astype(jnp.float32) - LEARNING * accum_out).astype(jnp.bfloat16)
    partner = gossip_peer[my_section, replica]
    paired = partner != replica
    pattern = jnp.sum(
        (gossip_peer[:, 0] != 0).astype(jnp.int32) << jnp.arange(section_count, dtype=jnp.int32)
    )
    other_in, other_out = lax.switch(
        pattern,
        [
            lambda a, b, chosen=chosen: swap_sections(a, b, chosen, section_count, replicas)
            for chosen in range(2**section_count)
        ],
        stepped_in,
        stepped_out,
    )
    chosen_in = jnp.where(paired, other_in, stepped_in)
    chosen_out = jnp.where(paired, other_out, stepped_out)
    new_in = (0.5 * (stepped_in.astype(jnp.float32) + chosen_in.astype(jnp.float32))).astype(
        jnp.bfloat16
    )
    new_out = (0.5 * (stepped_out.astype(jnp.float32) + chosen_out.astype(jnp.float32))).astype(
        jnp.bfloat16
    )
    return (new_in[None], new_out[None])


def solution(mesh):
    sections = mesh.shape["section"]
    reps = mesh.shape["rep"]
    inner = Mesh(np.asarray(mesh.devices).reshape(sections, 2, reps // 2), ("section", "half", "plane"))
    rows = ("half", "plane")
    return jax.shard_map(
        on_device,
        mesh=inner,
        in_specs=(
            P(None, None, rows, None),
            P(),
            P(None, None, rows, None),
            P(),
            P("section", None, rows),
            P("section", rows, None),
        ),
        out_specs=(P("section", None, rows), P("section", rows, None)),
        check_vma=False,
    )
```

```python
import numpy as np
import jax
import jax.numpy as jnp
from jax import lax
from jax.experimental import pallas as pl
from jax.experimental.pallas import tpu as pltpu
from jax.sharding import Mesh, PartitionSpec as P

EPSILON = 1e-06
GELU_SCALE = 0.7978845608028654
LEARNING = 8.0
PAIR = ("section", "half")


def gelu_parts(preact):
    inner = GELU_SCALE * (preact + 0.044715 * preact * preact * preact)
    tanh_val = jnp.tanh(inner)
    gelu_val = 0.5 * preact * (1.0 + tanh_val)
    slopes = 0.5 * (1.0 + tanh_val) + 0.5 * preact * (1.0 - tanh_val * tanh_val) * GELU_SCALE * (
        1.0 + 3.0 * 0.044715 * preact * preact
    )
    return (gelu_val, slopes)


def route_tables(routes, blocks):
    micro_count, bound_count, replicas, capacity = routes.shape
    slot_ids = jnp.arange(capacity, dtype=jnp.int32)
    replica_ids = jnp.arange(replicas, dtype=jnp.int32)
    live_now = jnp.broadcast_to(slot_ids[None, None, :] < blocks, (micro_count, replicas, capacity))
    link_list = []
    live_list = [live_now]
    for bound_idx in range(bound_count):
        target = jnp.where(live_now, routes[:, bound_idx], -1).reshape(
            micro_count, replicas * capacity
        )
        matches = (target[:, :, None] == replica_ids[None, None, :]).astype(jnp.int32)
        before = jnp.cumsum(matches, axis=1) - matches
        position = jnp.sum(matches * before, axis=2)
        link_table = matches[:, :, :, None] * (
            position[:, :, None, None] == slot_ids[None, None, None, :]
        ).astype(jnp.int32)
        link_table = link_table.reshape(micro_count, replicas, capacity, replicas, capacity)
        link_list.append(link_table.astype(jnp.float32))
        live_now = jnp.sum(link_table, axis=(1, 2)) > 0
        live_list.append(live_now)
    return (link_list, live_list)


def layer_front(flat_rows, weight_in, scale_in):
    widened = flat_rows.astype(jnp.float32)
    inverse = lax.rsqrt(jnp.mean(widened * widened, axis=-1, keepdims=True) + EPSILON)
    normed = (widened * inverse).astype(jnp.bfloat16)
    preact = jnp.dot(normed, weight_in, preferred_element_type=jnp.float32) * scale_in
    return (widened, inverse, normed, preact)


def plane_kernel(count, spread, active, x_ref, out_ref, held, send_sem, recv_sem):
    section = lax.axis_index("section")

    @pl.when(section == active)
    def _():
        plane_exchange(count, spread, section, x_ref, out_ref, held, send_sem, recv_sem)

    @pl.when(section != active)
    def _():
        out_ref[...] = jnp.zeros_like(out_ref)


def plane_exchange(count, spread, section, x_ref, out_ref, held, send_sem, recv_sem):
    half = lax.axis_index("half")
    me = lax.axis_index("plane")
    barrier = pltpu.get_barrier_semaphore()
    for step in range(1, count):
        peer = lax.rem(me + step, count)
        pl.semaphore_signal(
            barrier, inc=1, device_id=(section, half, peer), device_id_type=pl.DeviceIdType.MESH
        )
    pl.semaphore_wait(barrier, count - 1)
    copies = []
    for step in range(1, count):
        peer = lax.rem(me + step, count)
        copy = pltpu.make_async_remote_copy(
            src_ref=x_ref.at[0] if spread else x_ref.at[peer],
            dst_ref=held.at[me],
            send_sem=send_sem.at[step],
            recv_sem=recv_sem.at[step],
            device_id=(section, half, peer),
            device_id_type=pl.DeviceIdType.MESH,
        )
        copy.start()
        copies.append(copy)
    own = x_ref[0] if spread else x_ref[me]
    for copy in copies:
        copy.wait()
    out_ref[...] = held[...]
    out_ref[me] = own


def plane_call(value, count, spread, ident, active):
    lanes = value[0].size // 16
    dense = plane_dense(value.reshape(value.shape[0], 16, lanes), count, spread, ident, active)
    return dense.reshape((count,) + value.shape[1:])


def plane_dense(value, count, spread, ident, active):
    shape = (count,) + value.shape[1:]
    return pl.pallas_call(
        lambda *refs: plane_kernel(count, spread, active, *refs),
        out_shape=jax.ShapeDtypeStruct(shape, value.dtype),
        in_specs=[pl.BlockSpec(memory_space=pltpu.VMEM)],
        out_specs=pl.BlockSpec(memory_space=pltpu.VMEM),
        scratch_shapes=[
            pltpu.VMEM(shape, value.dtype),
            pltpu.SemaphoreType.DMA((count,)),
            pltpu.SemaphoreType.DMA((count,)),
        ],
        compiler_params=pltpu.CompilerParams(collective_id=ident, has_side_effects=True),
    )(value)


def gather_rows(piece, active):
    return plane_call(piece, lax.axis_size("plane"), True, 4 + active, active)


def sum_rows(partial_value, active):
    parts = plane_call(partial_value.astype(jnp.bfloat16), lax.axis_size("plane"), False, active, active)
    return jnp.sum(parts.astype(jnp.float32), axis=0, keepdims=True)


def own_rows(full, shard_idx):
    return lax.dynamic_slice_in_dim(full, shard_idx, 1, axis=0)


def forward_piece(x_full, weight_in, weight_out, scale_in, scale_out, shard_idx, active):
    shape = x_full.shape
    widened, inverse, normed, preact = layer_front(x_full.reshape(-1, shape[-1]), weight_in, scale_in)
    gelu_val, slopes = gelu_parts(preact)
    activated = gelu_val.astype(jnp.bfloat16)
    partial_value = jnp.dot(activated, weight_out, preferred_element_type=jnp.float32) * scale_out
    summed = sum_rows(partial_value.reshape(shape), active)
    return (own_rows(x_full, shard_idx).astype(jnp.float32) + summed).astype(jnp.bfloat16)


def backward_piece(
    x_full, up_full, up_piece, weight_in, weight_out, scale_in, scale_out, shard_idx, active
):
    shape = x_full.shape
    widened, inverse, normed, preact = layer_front(x_full.reshape(-1, shape[-1]), weight_in, scale_in)
    gelu_val, slopes = gelu_parts(preact)
    d_act = (
        lax.dot_general(
            up_full.reshape(-1, shape[-1]), weight_out, (((1,), (1,)), ((), ())),
            preferred_element_type=jnp.float32,
        )
        * scale_out
    )
    d_pre = (d_act * slopes).astype(jnp.bfloat16)
    d_normed = (
        lax.dot_general(d_pre, weight_in, (((1,), (1,)), ((), ())), preferred_element_type=jnp.float32)
        * scale_in
    )
    normed_piece = sum_rows(d_normed.reshape(shape), active)
    wide_piece = own_rows(x_full, shard_idx).astype(jnp.float32)
    inv_piece = own_rows(inverse.reshape(shape[:-1] + (1,)), shard_idx)
    grad_piece = (
        up_piece.astype(jnp.float32)
        + inv_piece * normed_piece
        - wide_piece
        * inv_piece
        * inv_piece
        * inv_piece
        * jnp.mean(normed_piece * wide_piece, axis=-1, keepdims=True)
    )
    return grad_piece.astype(jnp.bfloat16)


def weight_grads(x_full, up_full, weight_in, weight_out, scale_in, scale_out):
    width = x_full.shape[-1]
    widened, inverse, normed, preact = layer_front(x_full.reshape(-1, width), weight_in, scale_in)
    gelu_val, slopes = gelu_parts(preact)
    activated = gelu_val.astype(jnp.bfloat16)
    ups = up_full.reshape(-1, width)
    d_out = (
        lax.dot_general(activated, ups, (((0,), (0,)), ((), ())), preferred_element_type=jnp.float32)
        * scale_out
    )
    d_act = (
        lax.dot_general(ups, weight_out, (((1,), (1,)), ((), ())), preferred_element_type=jnp.float32)
        * scale_out
    )
    d_pre = (d_act * slopes).astype(jnp.bfloat16)
    d_in = (
        lax.dot_general(normed, d_pre, (((0,), (0,)), ((), ())), preferred_element_type=jnp.float32)
        * scale_in
    )
    return (d_in, d_out)


def cross_boundary(piece, source, target, replicas):
    straight = [(source * replicas + h, target * replicas + h) for h in range(replicas)]
    crossed = [(source * replicas + h, target * replicas + (replicas - 1 - h)) for h in range(replicas)]
    return (lax.ppermute(piece, PAIR, straight), lax.ppermute(piece, PAIR, crossed))


def swap_sections(stepped_in, stepped_out, chosen, section_count, replicas):
    pairs = [
        (section * replicas + h, section * replicas + replicas - 1 - h)
        for section in range(section_count)
        if (chosen >> section) & 1
        for h in range(replicas)
    ]
    if not pairs:
        return (jnp.zeros_like(stepped_in), jnp.zeros_like(stepped_out))
    return (lax.ppermute(stepped_in, PAIR, pairs), lax.ppermute(stepped_out, PAIR, pairs))


def sent_early(payload, anchor, source, target, replicas, flip):
    pairs = [
        (source * replicas + h, target * replicas + (replicas - 1 - h if flip else h))
        for h in range(replicas)
    ]
    tied = lax.optimization_barrier((payload, anchor))[0]
    return lax.ppermute(tied, PAIR, pairs)


def on_device(block_inputs, routes, cotangent, gossip_peer, w_in, w_out):
    section_count = lax.axis_size("section")
    replicas = lax.axis_size("half")
    group_size = lax.axis_size("plane")
    my_section = lax.axis_index("section")
    replica = lax.axis_index("half")
    shard_idx = lax.axis_index("plane")
    micro_count, blocks, piece_rows, model_width = block_inputs.shape
    capacity = cotangent.shape[1]
    weight_in = w_in[0]
    weight_out = w_out[0]
    hidden = weight_in.shape[1]
    scale_in = model_width ** (-0.5)
    scale_out = (hidden * group_size) ** (-0.5)
    link_list, live_list = route_tables(routes, blocks)
    weights = jnp.stack([weight_in, weight_out.T])

    opening = jnp.concatenate(
        [
            block_inputs,
            jnp.zeros((micro_count, capacity - blocks, piece_rows, model_width), jnp.bfloat16),
        ],
        axis=1,
    ).transpose(2, 0, 1, 3)
    x_cur = gather_rows(opening, 0)
    x_keep = x_cur
    for bound in range(section_count - 1):
        piece = forward_piece(x_cur, weight_in, weight_out, scale_in, scale_out, shard_idx, bound)
        if bound == 0:
            early_zero = sent_early(weights, piece, 0, 0, replicas, True)
            early_one = sent_early(weights, piece, 1, 0, replicas, True)
        straight, crossed = cross_boundary(piece, bound, bound + 1, replicas)
        sources = jnp.stack(
            [jnp.where(replica == h, straight, crossed) for h in range(replicas)]
        )[:, 0]
        mine = lax.dynamic_index_in_dim(link_list[bound], replica, 3, keepdims=False)
        routed = jnp.einsum(
            "mqjk,qmjd->mkd", mine.astype(jnp.bfloat16), sources,
            preferred_element_type=jnp.float32,
        ).astype(jnp.bfloat16)[None]
        x_cur = gather_rows(routed, bound + 1)
        x_keep = jnp.where(my_section == bound + 1, x_cur, x_keep)

    last_live = lax.dynamic_index_in_dim(live_list[section_count - 1], replica, 1, keepdims=False)
    up_piece = jnp.where(
        last_live[None, :, :, None], cotangent.transpose(2, 0, 1, 3), jnp.zeros((), jnp.bfloat16)
    )
    up_full = gather_rows(up_piece, section_count - 1)
    up_keep = up_full
    last = section_count - 1
    for depth in reversed(range(1, section_count)):
        grad_piece = backward_piece(
            x_keep, up_full, up_piece, weight_in, weight_out, scale_in, scale_out, shard_idx, depth
        )
        if depth == last:
            early_last = sent_early(weights, grad_piece, last, last, replicas, True)
            early_near = sent_early(weights, grad_piece, last - 1, last, replicas, True)
        straight, crossed = cross_boundary(grad_piece, depth, depth - 1, replicas)
        sources = jnp.stack(
            [jnp.where(replica == h, straight, crossed) for h in range(replicas)]
        )[:, 0]
        mine = lax.dynamic_index_in_dim(link_list[depth - 1], replica, 1, keepdims=False)
        up_piece = jnp.einsum(
            "mjdk,dmkD->mjD", mine.astype(jnp.bfloat16), sources,
            preferred_element_type=jnp.float32,
        ).astype(jnp.bfloat16)[None]
        up_full = gather_rows(up_piece, depth - 1)
        up_keep = jnp.where(my_section == depth - 1, up_full, up_keep)

    accum_in, accum_out = weight_grads(x_keep, up_keep, weight_in, weight_out, scale_in, scale_out)
    stepped_in = (weight_in.astype(jnp.float32) - LEARNING * accum_in).astype(jnp.bfloat16)
    stepped_out = (weight_out.astype(jnp.float32) - LEARNING * accum_out).astype(jnp.bfloat16)
    partner = gossip_peer[my_section, replica]
    paired = partner != replica
    relay_pairs = [(h, replicas + h) for h in range(replicas)] + [
        (last * replicas + h, (last - 1) * replicas + h) for h in range(replicas)
    ]
    early_zero, early_one, early_last, early_near, up_keep = lax.optimization_barrier(
        (early_zero, early_one, early_last, early_near, up_keep)
    )
    relayed = lax.ppermute(jnp.where(my_section == 0, early_one, early_near), PAIR, relay_pairs)
    peer_weights = jnp.where(
        my_section == 0, early_zero, jnp.where(my_section == last, early_last, relayed)
    )
    peer_in = peer_weights[0]
    peer_out = peer_weights[1].T
    swap = [(h, replicas - 1 - h) for h in range(replicas)]
    peer_x = lax.ppermute(x_keep, "half", swap)
    peer_up = lax.ppermute(up_keep, "half", swap)
    peer_d_in, peer_d_out = weight_grads(peer_x, peer_up, peer_in, peer_out, scale_in, scale_out)
    other_in = (peer_in.astype(jnp.float32) - LEARNING * peer_d_in).astype(jnp.bfloat16)
    other_out = (peer_out.astype(jnp.float32) - LEARNING * peer_d_out).astype(jnp.bfloat16)
    chosen_in = jnp.where(paired, other_in, stepped_in)
    chosen_out = jnp.where(paired, other_out, stepped_out)
    new_in = (0.5 * (stepped_in.astype(jnp.float32) + chosen_in.astype(jnp.float32))).astype(
        jnp.bfloat16
    )
    new_out = (0.5 * (stepped_out.astype(jnp.float32) + chosen_out.astype(jnp.float32))).astype(
        jnp.bfloat16
    )
    return (new_in[None], new_out[None])


def solution(mesh):
    sections = mesh.shape["section"]
    reps = mesh.shape["rep"]
    inner = Mesh(np.asarray(mesh.devices).reshape(sections, 2, reps // 2), ("section", "half", "plane"))
    rows = ("half", "plane")
    return jax.shard_map(
        on_device,
        mesh=inner,
        in_specs=(
            P(None, None, rows, None),
            P(),
            P(None, None, rows, None),
            P(),
            P("section", None, rows),
            P("section", rows, None),
        ),
        out_specs=(P("section", None, rows), P("section", rows, None)),
        check_vma=False,
    )
```

```python
import numpy as np
import jax
import jax.numpy as jnp
from jax import lax
from jax.experimental import pallas as pl
from jax.experimental.pallas import tpu as pltpu
from jax.sharding import Mesh, PartitionSpec as P

EPSILON = 1e-06
GELU_SCALE = 0.7978845608028654
LEARNING = 8.0
PAIR = ("section", "half")


def gelu_parts(preact):
    inner = GELU_SCALE * (preact + 0.044715 * preact * preact * preact)
    tanh_val = jnp.tanh(inner)
    gelu_val = 0.5 * preact * (1.0 + tanh_val)
    slopes = 0.5 * (1.0 + tanh_val) + 0.5 * preact * (1.0 - tanh_val * tanh_val) * GELU_SCALE * (
        1.0 + 3.0 * 0.044715 * preact * preact
    )
    return (gelu_val, slopes)


def route_tables(routes, blocks):
    micro_count, bound_count, replicas, capacity = routes.shape
    slot_ids = jnp.arange(capacity, dtype=jnp.int32)
    replica_ids = jnp.arange(replicas, dtype=jnp.int32)
    live_now = jnp.broadcast_to(slot_ids[None, None, :] < blocks, (micro_count, replicas, capacity))
    link_list = []
    live_list = [live_now]
    for bound_idx in range(bound_count):
        target = jnp.where(live_now, routes[:, bound_idx], -1).reshape(
            micro_count, replicas * capacity
        )
        matches = (target[:, :, None] == replica_ids[None, None, :]).astype(jnp.int32)
        before = jnp.cumsum(matches, axis=1) - matches
        position = jnp.sum(matches * before, axis=2)
        link_table = matches[:, :, :, None] * (
            position[:, :, None, None] == slot_ids[None, None, None, :]
        ).astype(jnp.int32)
        link_table = link_table.reshape(micro_count, replicas, capacity, replicas, capacity)
        link_list.append(link_table.astype(jnp.float32))
        live_now = jnp.sum(link_table, axis=(1, 2)) > 0
        live_list.append(live_now)
    return (link_list, live_list)


def layer_front(flat_rows, weight_in, scale_in):
    widened = flat_rows.astype(jnp.float32)
    inverse = lax.rsqrt(jnp.mean(widened * widened, axis=-1, keepdims=True) + EPSILON)
    normed = (widened * inverse).astype(jnp.bfloat16)
    preact = jnp.dot(normed, weight_in, preferred_element_type=jnp.float32) * scale_in
    return (widened, inverse, normed, preact)


def plane_kernel(count, spread, active, x_ref, out_ref, held, send_sem, recv_sem):
    section = lax.axis_index("section")

    @pl.when(section == active)
    def _():
        plane_exchange(count, spread, section, x_ref, out_ref, held, send_sem, recv_sem)

    @pl.when(section != active)
    def _():
        out_ref[...] = jnp.zeros_like(out_ref)


def plane_exchange(count, spread, section, x_ref, out_ref, held, send_sem, recv_sem):
    half = lax.axis_index("half")
    me = lax.axis_index("plane")
    barrier = pltpu.get_barrier_semaphore()
    for step in range(1, count):
        peer = lax.rem(me + step, count)
        pl.semaphore_signal(
            barrier, inc=1, device_id=(section, half, peer), device_id_type=pl.DeviceIdType.MESH
        )
    pl.semaphore_wait(barrier, count - 1)
    copies = []
    for step in range(1, count):
        peer = lax.rem(me + step, count)
        copy = pltpu.make_async_remote_copy(
            src_ref=x_ref.at[0] if spread else x_ref.at[peer],
            dst_ref=held.at[me],
            send_sem=send_sem.at[step],
            recv_sem=recv_sem.at[step],
            device_id=(section, half, peer),
            device_id_type=pl.DeviceIdType.MESH,
        )
        copy.start()
        copies.append(copy)
    own = x_ref[0] if spread else x_ref[me]
    for copy in copies:
        copy.wait()
    out_ref[...] = held[...]
    out_ref[me] = own


def plane_call(value, count, spread, ident, active):
    lanes = value[0].size // 16
    dense = plane_dense(value.reshape(value.shape[0], 16, lanes), count, spread, ident, active)
    return dense.reshape((count,) + value.shape[1:])


def plane_dense(value, count, spread, ident, active):
    shape = (count,) + value.shape[1:]
    return pl.pallas_call(
        lambda *refs: plane_kernel(count, spread, active, *refs),
        out_shape=jax.ShapeDtypeStruct(shape, value.dtype),
        in_specs=[pl.BlockSpec(memory_space=pltpu.VMEM)],
        out_specs=pl.BlockSpec(memory_space=pltpu.VMEM),
        scratch_shapes=[
            pltpu.VMEM(shape, value.dtype),
            pltpu.SemaphoreType.DMA((count,)),
            pltpu.SemaphoreType.DMA((count,)),
        ],
        compiler_params=pltpu.CompilerParams(collective_id=ident, has_side_effects=True),
    )(value)


def gather_rows(piece, active):
    return plane_call(piece, lax.axis_size("plane"), True, 4 + active, active)


def sum_rows(partial_value, active):
    parts = plane_call(partial_value.astype(jnp.bfloat16), lax.axis_size("plane"), False, active, active)
    return jnp.sum(parts.astype(jnp.float32), axis=0, keepdims=True)


def own_rows(full, shard_idx):
    return lax.dynamic_slice_in_dim(full, shard_idx, 1, axis=0)


def forward_piece(x_full, weight_in, weight_out, scale_in, scale_out, shard_idx, active):
    shape = x_full.shape
    widened, inverse, normed, preact = layer_front(x_full.reshape(-1, shape[-1]), weight_in, scale_in)
    gelu_val, slopes = gelu_parts(preact)
    activated = gelu_val.astype(jnp.bfloat16)
    partial_value = jnp.dot(activated, weight_out, preferred_element_type=jnp.float32) * scale_out
    summed = sum_rows(partial_value.reshape(shape), active)
    return (own_rows(x_full, shard_idx).astype(jnp.float32) + summed).astype(jnp.bfloat16)


def backward_piece(
    x_full, up_full, up_piece, weight_in, weight_out, scale_in, scale_out, shard_idx, active
):
    shape = x_full.shape
    widened, inverse, normed, preact = layer_front(x_full.reshape(-1, shape[-1]), weight_in, scale_in)
    gelu_val, slopes = gelu_parts(preact)
    d_act = (
        lax.dot_general(
            up_full.reshape(-1, shape[-1]), weight_out, (((1,), (1,)), ((), ())),
            preferred_element_type=jnp.float32,
        )
        * scale_out
    )
    d_pre = (d_act * slopes).astype(jnp.bfloat16)
    d_normed = (
        lax.dot_general(d_pre, weight_in, (((1,), (1,)), ((), ())), preferred_element_type=jnp.float32)
        * scale_in
    )
    normed_piece = sum_rows(d_normed.reshape(shape), active)
    wide_piece = own_rows(x_full, shard_idx).astype(jnp.float32)
    inv_piece = own_rows(inverse.reshape(shape[:-1] + (1,)), shard_idx)
    grad_piece = (
        up_piece.astype(jnp.float32)
        + inv_piece * normed_piece
        - wide_piece
        * inv_piece
        * inv_piece
        * inv_piece
        * jnp.mean(normed_piece * wide_piece, axis=-1, keepdims=True)
    )
    return grad_piece.astype(jnp.bfloat16)


def weight_grads(x_full, up_full, weight_in, weight_out, scale_in, scale_out):
    width = x_full.shape[-1]
    widened, inverse, normed, preact = layer_front(x_full.reshape(-1, width), weight_in, scale_in)
    gelu_val, slopes = gelu_parts(preact)
    activated = gelu_val.astype(jnp.bfloat16)
    ups = up_full.reshape(-1, width)
    d_out = (
        lax.dot_general(activated, ups, (((0,), (0,)), ((), ())), preferred_element_type=jnp.float32)
        * scale_out
    )
    d_act = (
        lax.dot_general(ups, weight_out, (((1,), (1,)), ((), ())), preferred_element_type=jnp.float32)
        * scale_out
    )
    d_pre = (d_act * slopes).astype(jnp.bfloat16)
    d_in = (
        lax.dot_general(normed, d_pre, (((0,), (0,)), ((), ())), preferred_element_type=jnp.float32)
        * scale_in
    )
    return (d_in, d_out)


def route_kernel(source, target, piece_ref, out_ref, held, send_sem, recv_sem):
    section = lax.axis_index("section")
    half = lax.axis_index("half")
    plane = lax.axis_index("plane")
    barrier = pltpu.get_barrier_semaphore()
    mesh_ids = pl.DeviceIdType.MESH

    def transfer(way, far):
        return pltpu.make_async_remote_copy(
            src_ref=piece_ref,
            dst_ref=held.at[way],
            send_sem=send_sem.at[way],
            recv_sem=recv_sem.at[way],
            device_id=(far, lax.select(way == 0, half, 1 - half), plane),
            device_id_type=mesh_ids,
        )

    @pl.when(section == source)
    def _():
        for way in range(2):
            pl.semaphore_signal(
                barrier, inc=1, device_id=(target, lax.select(way == 0, half, 1 - half), plane),
                device_id_type=mesh_ids,
            )
        pl.semaphore_wait(barrier, 2)
        copies = [transfer(way, target) for way in range(2)]
        for copy in copies:
            copy.start()
        for copy in copies:
            copy.wait_send()
        out_ref[...] = jnp.zeros_like(out_ref)

    @pl.when(section == target)
    def _():
        for way in range(2):
            pl.semaphore_signal(
                barrier, inc=1, device_id=(source, lax.select(way == 0, half, 1 - half), plane),
                device_id_type=mesh_ids,
            )
        pl.semaphore_wait(barrier, 2)
        for way in range(2):
            transfer(way, source).wait_recv()
        out_ref[...] = held[...]

    @pl.when(jnp.logical_and(section != source, section != target))
    def _():
        out_ref[...] = jnp.zeros_like(out_ref)


def cross_boundary(piece, source, target, replicas):
    lanes = piece.size // 16
    dense = piece.reshape(16, lanes)
    both = pl.pallas_call(
        lambda *refs: route_kernel(source, target, *refs),
        out_shape=jax.ShapeDtypeStruct((2, 16, lanes), piece.dtype),
        in_specs=[pl.BlockSpec(memory_space=pltpu.VMEM)],
        out_specs=pl.BlockSpec(memory_space=pltpu.VMEM),
        scratch_shapes=[
            pltpu.VMEM((2, 16, lanes), piece.dtype),
            pltpu.SemaphoreType.DMA((2,)),
            pltpu.SemaphoreType.DMA((2,)),
        ],
        compiler_params=pltpu.CompilerParams(
            collective_id=8 + source * 4 + target, has_side_effects=True
        ),
    )(dense)
    return (both[0].reshape(piece.shape), both[1].reshape(piece.shape))


def swap_sections(stepped_in, stepped_out, chosen, section_count, replicas):
    pairs = [
        (section * replicas + h, section * replicas + replicas - 1 - h)
        for section in range(section_count)
        if (chosen >> section) & 1
        for h in range(replicas)
    ]
    if not pairs:
        return (jnp.zeros_like(stepped_in), jnp.zeros_like(stepped_out))
    return (lax.ppermute(stepped_in, PAIR, pairs), lax.ppermute(stepped_out, PAIR, pairs))


def sent_early(payload, anchor, source, target, replicas, flip):
    pairs = [
        (source * replicas + h, target * replicas + (replicas - 1 - h if flip else h))
        for h in range(replicas)
    ]
    tied = lax.optimization_barrier((payload, anchor))[0]
    return lax.ppermute(tied, PAIR, pairs)


def on_device(block_inputs, routes, cotangent, gossip_peer, w_in, w_out):
    section_count = lax.axis_size("section")
    replicas = lax.axis_size("half")
    group_size = lax.axis_size("plane")
    my_section = lax.axis_index("section")
    replica = lax.axis_index("half")
    shard_idx = lax.axis_index("plane")
    micro_count, blocks, piece_rows, model_width = block_inputs.shape
    capacity = cotangent.shape[1]
    weight_in = w_in[0]
    weight_out = w_out[0]
    hidden = weight_in.shape[1]
    scale_in = model_width ** (-0.5)
    scale_out = (hidden * group_size) ** (-0.5)
    link_list, live_list = route_tables(routes, blocks)
    weights = jnp.stack([weight_in, weight_out.T])

    opening = jnp.concatenate(
        [
            block_inputs,
            jnp.zeros((micro_count, capacity - blocks, piece_rows, model_width), jnp.bfloat16),
        ],
        axis=1,
    ).transpose(2, 0, 1, 3)
    x_cur = gather_rows(opening, 0)
    x_keep = x_cur
    for bound in range(section_count - 1):
        piece = forward_piece(x_cur, weight_in, weight_out, scale_in, scale_out, shard_idx, bound)
        if bound == 0:
            early_zero = sent_early(weights, piece, 0, 0, replicas, True)
            early_one = sent_early(weights, piece, 1, 0, replicas, True)
        straight, crossed = cross_boundary(piece, bound, bound + 1, replicas)
        sources = jnp.stack(
            [jnp.where(replica == h, straight, crossed) for h in range(replicas)]
        )[:, 0]
        mine = lax.dynamic_index_in_dim(link_list[bound], replica, 3, keepdims=False)
        routed = jnp.einsum(
            "mqjk,qmjd->mkd", mine.astype(jnp.bfloat16), sources,
            preferred_element_type=jnp.float32,
        ).astype(jnp.bfloat16)[None]
        x_cur = gather_rows(routed, bound + 1)
        x_keep = jnp.where(my_section == bound + 1, x_cur, x_keep)

    last_live = lax.dynamic_index_in_dim(live_list[section_count - 1], replica, 1, keepdims=False)
    up_piece = jnp.where(
        last_live[None, :, :, None], cotangent.transpose(2, 0, 1, 3), jnp.zeros((), jnp.bfloat16)
    )
    up_full = gather_rows(up_piece, section_count - 1)
    up_keep = up_full
    last = section_count - 1
    for depth in reversed(range(1, section_count)):
        grad_piece = backward_piece(
            x_keep, up_full, up_piece, weight_in, weight_out, scale_in, scale_out, shard_idx, depth
        )
        if depth == last:
            early_last = sent_early(weights, grad_piece, last, last, replicas, True)
            early_near = sent_early(weights, grad_piece, last - 1, last, replicas, True)
        straight, crossed = cross_boundary(grad_piece, depth, depth - 1, replicas)
        sources = jnp.stack(
            [jnp.where(replica == h, straight, crossed) for h in range(replicas)]
        )[:, 0]
        mine = lax.dynamic_index_in_dim(link_list[depth - 1], replica, 1, keepdims=False)
        up_piece = jnp.einsum(
            "mjdk,dmkD->mjD", mine.astype(jnp.bfloat16), sources,
            preferred_element_type=jnp.float32,
        ).astype(jnp.bfloat16)[None]
        up_full = gather_rows(up_piece, depth - 1)
        up_keep = jnp.where(my_section == depth - 1, up_full, up_keep)

    accum_in, accum_out = weight_grads(x_keep, up_keep, weight_in, weight_out, scale_in, scale_out)
    stepped_in = (weight_in.astype(jnp.float32) - LEARNING * accum_in).astype(jnp.bfloat16)
    stepped_out = (weight_out.astype(jnp.float32) - LEARNING * accum_out).astype(jnp.bfloat16)
    partner = gossip_peer[my_section, replica]
    paired = partner != replica
    relay_pairs = [(h, replicas + h) for h in range(replicas)] + [
        (last * replicas + h, (last - 1) * replicas + h) for h in range(replicas)
    ]
    early_zero, early_one, early_last, early_near, up_keep = lax.optimization_barrier(
        (early_zero, early_one, early_last, early_near, up_keep)
    )
    relayed = lax.ppermute(jnp.where(my_section == 0, early_one, early_near), PAIR, relay_pairs)
    peer_weights = jnp.where(
        my_section == 0, early_zero, jnp.where(my_section == last, early_last, relayed)
    )
    peer_in = peer_weights[0]
    peer_out = peer_weights[1].T
    swap = [(h, replicas - 1 - h) for h in range(replicas)]
    peer_x = lax.ppermute(x_keep, "half", swap)
    peer_up = lax.ppermute(up_keep, "half", swap)
    peer_d_in, peer_d_out = weight_grads(peer_x, peer_up, peer_in, peer_out, scale_in, scale_out)
    other_in = (peer_in.astype(jnp.float32) - LEARNING * peer_d_in).astype(jnp.bfloat16)
    other_out = (peer_out.astype(jnp.float32) - LEARNING * peer_d_out).astype(jnp.bfloat16)
    chosen_in = jnp.where(paired, other_in, stepped_in)
    chosen_out = jnp.where(paired, other_out, stepped_out)
    new_in = (0.5 * (stepped_in.astype(jnp.float32) + chosen_in.astype(jnp.float32))).astype(
        jnp.bfloat16
    )
    new_out = (0.5 * (stepped_out.astype(jnp.float32) + chosen_out.astype(jnp.float32))).astype(
        jnp.bfloat16
    )
    return (new_in[None], new_out[None])


def solution(mesh):
    sections = mesh.shape["section"]
    reps = mesh.shape["rep"]
    inner = Mesh(np.asarray(mesh.devices).reshape(sections, 2, reps // 2), ("section", "half", "plane"))
    rows = ("half", "plane")
    return jax.shard_map(
        on_device,
        mesh=inner,
        in_specs=(
            P(None, None, rows, None),
            P(),
            P(None, None, rows, None),
            P(),
            P("section", None, rows),
            P("section", rows, None),
        ),
        out_specs=(P("section", None, rows), P("section", rows, None)),
        check_vma=False,
    )
```

```python
import numpy as np
import jax
import jax.numpy as jnp
from jax import lax
from jax.experimental import pallas as pl
from jax.experimental.pallas import tpu as pltpu
from jax.sharding import Mesh, PartitionSpec as P

EPSILON = 1e-06
GELU_SCALE = 0.7978845608028654
LEARNING = 8.0
PAIR = ("section", "half")


def gelu_parts(preact):
    inner = GELU_SCALE * (preact + 0.044715 * preact * preact * preact)
    tanh_val = jnp.tanh(inner)
    gelu_val = 0.5 * preact * (1.0 + tanh_val)
    slopes = 0.5 * (1.0 + tanh_val) + 0.5 * preact * (1.0 - tanh_val * tanh_val) * GELU_SCALE * (
        1.0 + 3.0 * 0.044715 * preact * preact
    )
    return (gelu_val, slopes)


def route_tables(routes, blocks):
    micro_count, bound_count, replicas, capacity = routes.shape
    slot_ids = jnp.arange(capacity, dtype=jnp.int32)
    replica_ids = jnp.arange(replicas, dtype=jnp.int32)
    live_now = jnp.broadcast_to(slot_ids[None, None, :] < blocks, (micro_count, replicas, capacity))
    link_list = []
    live_list = [live_now]
    for bound_idx in range(bound_count):
        target = jnp.where(live_now, routes[:, bound_idx], -1).reshape(
            micro_count, replicas * capacity
        )
        matches = (target[:, :, None] == replica_ids[None, None, :]).astype(jnp.int32)
        before = jnp.cumsum(matches, axis=1) - matches
        position = jnp.sum(matches * before, axis=2)
        link_table = matches[:, :, :, None] * (
            position[:, :, None, None] == slot_ids[None, None, None, :]
        ).astype(jnp.int32)
        link_table = link_table.reshape(micro_count, replicas, capacity, replicas, capacity)
        link_list.append(link_table.astype(jnp.float32))
        live_now = jnp.sum(link_table, axis=(1, 2)) > 0
        live_list.append(live_now)
    return (link_list, live_list)


def layer_front(flat_rows, weight_in, scale_in):
    widened = flat_rows.astype(jnp.float32)
    inverse = lax.rsqrt(jnp.mean(widened * widened, axis=-1, keepdims=True) + EPSILON)
    normed = (widened * inverse).astype(jnp.bfloat16)
    preact = jnp.dot(normed, weight_in, preferred_element_type=jnp.float32) * scale_in
    return (widened, inverse, normed, preact)


def plane_kernel(count, spread, active, x_ref, out_ref, held, send_sem, recv_sem):
    section = lax.axis_index("section")

    @pl.when(section == active)
    def _():
        plane_exchange(count, spread, section, x_ref, out_ref, held, send_sem, recv_sem)

    @pl.when(section != active)
    def _():
        out_ref[...] = jnp.zeros_like(out_ref)


def plane_exchange(count, spread, section, x_ref, out_ref, held, send_sem, recv_sem):
    half = lax.axis_index("half")
    me = lax.axis_index("plane")
    barrier = pltpu.get_barrier_semaphore()
    for step in range(1, count):
        peer = lax.rem(me + step, count)
        pl.semaphore_signal(
            barrier, inc=1, device_id=(section, half, peer), device_id_type=pl.DeviceIdType.MESH
        )
    pl.semaphore_wait(barrier, count - 1)
    copies = []
    for step in range(1, count):
        peer = lax.rem(me + step, count)
        copy = pltpu.make_async_remote_copy(
            src_ref=x_ref.at[0] if spread else x_ref.at[peer],
            dst_ref=held.at[me],
            send_sem=send_sem.at[step],
            recv_sem=recv_sem.at[step],
            device_id=(section, half, peer),
            device_id_type=pl.DeviceIdType.MESH,
        )
        copy.start()
        copies.append(copy)
    own = x_ref[0] if spread else x_ref[me]
    for copy in copies:
        copy.wait()
    out_ref[...] = held[...]
    out_ref[me] = own


def plane_call(value, count, spread, ident, active):
    lanes = value[0].size // 16
    dense = plane_dense(value.reshape(value.shape[0], 16, lanes), count, spread, ident, active)
    return dense.reshape((count,) + value.shape[1:])


def plane_dense(value, count, spread, ident, active):
    shape = (count,) + value.shape[1:]
    return pl.pallas_call(
        lambda *refs: plane_kernel(count, spread, active, *refs),
        out_shape=jax.ShapeDtypeStruct(shape, value.dtype),
        in_specs=[pl.BlockSpec(memory_space=pltpu.VMEM)],
        out_specs=pl.BlockSpec(memory_space=pltpu.VMEM),
        scratch_shapes=[
            pltpu.VMEM(shape, value.dtype),
            pltpu.SemaphoreType.DMA((count,)),
            pltpu.SemaphoreType.DMA((count,)),
        ],
        compiler_params=pltpu.CompilerParams(collective_id=ident, has_side_effects=True),
    )(value)


def gather_rows(piece, active):
    return plane_call(piece, lax.axis_size("plane"), True, 4 + active, active)


def sum_rows(partial_value, active):
    parts = plane_call(partial_value.astype(jnp.bfloat16), lax.axis_size("plane"), False, active, active)
    return jnp.sum(parts.astype(jnp.float32), axis=0, keepdims=True)


def own_rows(full, shard_idx):
    return lax.dynamic_slice_in_dim(full, shard_idx, 1, axis=0)


def forward_piece(x_full, weight_in, weight_out, scale_in, scale_out, shard_idx, active):
    shape = x_full.shape
    widened, inverse, normed, preact = layer_front(x_full.reshape(-1, shape[-1]), weight_in, scale_in)
    gelu_val, slopes = gelu_parts(preact)
    activated = gelu_val.astype(jnp.bfloat16)
    partial_value = jnp.dot(activated, weight_out, preferred_element_type=jnp.float32) * scale_out
    summed = sum_rows(partial_value.reshape(shape), active)
    return (own_rows(x_full, shard_idx).astype(jnp.float32) + summed).astype(jnp.bfloat16)


def backward_piece(
    x_full, up_full, up_piece, weight_in, weight_out, scale_in, scale_out, shard_idx, active
):
    shape = x_full.shape
    widened, inverse, normed, preact = layer_front(x_full.reshape(-1, shape[-1]), weight_in, scale_in)
    gelu_val, slopes = gelu_parts(preact)
    d_act = (
        lax.dot_general(
            up_full.reshape(-1, shape[-1]), weight_out, (((1,), (1,)), ((), ())),
            preferred_element_type=jnp.float32,
        )
        * scale_out
    )
    d_pre = (d_act * slopes).astype(jnp.bfloat16)
    d_normed = (
        lax.dot_general(d_pre, weight_in, (((1,), (1,)), ((), ())), preferred_element_type=jnp.float32)
        * scale_in
    )
    normed_piece = sum_rows(d_normed.reshape(shape), active)
    wide_piece = own_rows(x_full, shard_idx).astype(jnp.float32)
    inv_piece = own_rows(inverse.reshape(shape[:-1] + (1,)), shard_idx)
    grad_piece = (
        up_piece.astype(jnp.float32)
        + inv_piece * normed_piece
        - wide_piece
        * inv_piece
        * inv_piece
        * inv_piece
        * jnp.mean(normed_piece * wide_piece, axis=-1, keepdims=True)
    )
    return grad_piece.astype(jnp.bfloat16)


def weight_grads(x_full, up_full, weight_in, weight_out, scale_in, scale_out):
    width = x_full.shape[-1]
    widened, inverse, normed, preact = layer_front(x_full.reshape(-1, width), weight_in, scale_in)
    gelu_val, slopes = gelu_parts(preact)
    activated = gelu_val.astype(jnp.bfloat16)
    ups = up_full.reshape(-1, width)
    d_out = (
        lax.dot_general(activated, ups, (((0,), (0,)), ((), ())), preferred_element_type=jnp.float32)
        * scale_out
    )
    d_act = (
        lax.dot_general(ups, weight_out, (((1,), (1,)), ((), ())), preferred_element_type=jnp.float32)
        * scale_out
    )
    d_pre = (d_act * slopes).astype(jnp.bfloat16)
    d_in = (
        lax.dot_general(normed, d_pre, (((0,), (0,)), ((), ())), preferred_element_type=jnp.float32)
        * scale_in
    )
    return (d_in, d_out)


def cross_boundary(piece, source, target, replicas):
    straight = [(source * replicas + h, target * replicas + h) for h in range(replicas)]
    crossed = [(source * replicas + h, target * replicas + (replicas - 1 - h)) for h in range(replicas)]
    return (lax.ppermute(piece, PAIR, straight), lax.ppermute(piece, PAIR, crossed))


def swap_sections(stepped_in, stepped_out, chosen, section_count, replicas):
    pairs = [
        (section * replicas + h, section * replicas + replicas - 1 - h)
        for section in range(section_count)
        if (chosen >> section) & 1
        for h in range(replicas)
    ]
    if not pairs:
        return (jnp.zeros_like(stepped_in), jnp.zeros_like(stepped_out))
    return (lax.ppermute(stepped_in, PAIR, pairs), lax.ppermute(stepped_out, PAIR, pairs))


def on_device(block_inputs, routes, cotangent, gossip_peer, w_in, w_out):
    section_count = lax.axis_size("section")
    replicas = lax.axis_size("half")
    group_size = lax.axis_size("plane")
    my_section = lax.axis_index("section")
    replica = lax.axis_index("half")
    shard_idx = lax.axis_index("plane")
    micro_count, blocks, piece_rows, model_width = block_inputs.shape
    capacity = cotangent.shape[1]
    weight_in = w_in[0]
    weight_out = w_out[0]
    hidden = weight_in.shape[1]
    scale_in = model_width ** (-0.5)
    scale_out = (hidden * group_size) ** (-0.5)
    link_list, live_list = route_tables(routes, blocks)

    def padded(full):
        filler = jnp.zeros(full.shape[:2] + (capacity - full.shape[2],) + full.shape[3:], full.dtype)
        return jnp.concatenate([full, filler], axis=2)

    x_cur = gather_rows(block_inputs.transpose(2, 0, 1, 3), 0)
    x_keep = padded(x_cur)
    for bound in range(section_count - 1):
        piece = forward_piece(x_cur, weight_in, weight_out, scale_in, scale_out, shard_idx, bound)
        straight, crossed = cross_boundary(piece, bound, bound + 1, replicas)
        sources = jnp.stack(
            [jnp.where(replica == h, straight, crossed) for h in range(replicas)]
        )[:, 0]
        mine = lax.dynamic_index_in_dim(link_list[bound], replica, 3, keepdims=False)
        mine = mine[:, :, : piece.shape[2], :]
        routed = jnp.einsum(
            "mqjk,qmjd->mkd", mine.astype(jnp.bfloat16), sources,
            preferred_element_type=jnp.float32,
        ).astype(jnp.bfloat16)[None]
        x_cur = gather_rows(routed, bound + 1)
        x_keep = jnp.where(my_section == bound + 1, x_cur, x_keep)

    last_live = lax.dynamic_index_in_dim(live_list[section_count - 1], replica, 1, keepdims=False)
    up_piece = jnp.where(
        last_live[None, :, :, None], cotangent.transpose(2, 0, 1, 3), jnp.zeros((), jnp.bfloat16)
    )
    up_full = gather_rows(up_piece, section_count - 1)
    up_keep = up_full
    for depth in reversed(range(1, section_count)):
        grad_piece = backward_piece(
            x_keep, up_full, up_piece, weight_in, weight_out, scale_in, scale_out, shard_idx, depth
        )
        straight, crossed = cross_boundary(grad_piece, depth, depth - 1, replicas)
        sources = jnp.stack(
            [jnp.where(replica == h, straight, crossed) for h in range(replicas)]
        )[:, 0]
        mine = lax.dynamic_index_in_dim(link_list[depth - 1], replica, 1, keepdims=False)
        if depth == 1:
            mine = mine[:, :blocks]
        up_piece = jnp.einsum(
            "mjdk,dmkD->mjD", mine.astype(jnp.bfloat16), sources,
            preferred_element_type=jnp.float32,
        ).astype(jnp.bfloat16)[None]
        up_full = gather_rows(up_piece, depth - 1)
        up_keep = jnp.where(my_section == depth - 1, padded(up_full), up_keep)

    accum_in, accum_out = weight_grads(x_keep, up_keep, weight_in, weight_out, scale_in, scale_out)
    stepped_in = (weight_in.astype(jnp.float32) - LEARNING * accum_in).astype(jnp.bfloat16)
    stepped_out = (weight_out.astype(jnp.float32) - LEARNING * accum_out).astype(jnp.bfloat16)
    partner = gossip_peer[my_section, replica]
    paired = partner != replica
    pattern = jnp.sum(
        (gossip_peer[:, 0] != 0).astype(jnp.int32) << jnp.arange(section_count, dtype=jnp.int32)
    )
    other_in, other_out = lax.switch(
        pattern,
        [
            lambda a, b, chosen=chosen: swap_sections(a, b, chosen, section_count, replicas)
            for chosen in range(2**section_count)
        ],
        stepped_in,
        stepped_out,
    )
    chosen_in = jnp.where(paired, other_in, stepped_in)
    chosen_out = jnp.where(paired, other_out, stepped_out)
    new_in = (0.5 * (stepped_in.astype(jnp.float32) + chosen_in.astype(jnp.float32))).astype(
        jnp.bfloat16
    )
    new_out = (0.5 * (stepped_out.astype(jnp.float32) + chosen_out.astype(jnp.float32))).astype(
        jnp.bfloat16
    )
    return (new_in[None], new_out[None])


def solution(mesh):
    sections = mesh.shape["section"]
    reps = mesh.shape["rep"]
    inner = Mesh(np.asarray(mesh.devices).reshape(sections, 2, reps // 2), ("section", "half", "plane"))
    rows = ("half", "plane")
    return jax.shard_map(
        on_device,
        mesh=inner,
        in_specs=(
            P(None, None, rows, None),
            P(),
            P(None, None, rows, None),
            P(),
            P("section", None, rows),
            P("section", rows, None),
        ),
        out_specs=(P("section", None, rows), P("section", rows, None)),
        check_vma=False,
    )
```

```python
import numpy as np
import jax
import jax.numpy as jnp
from jax import lax
from jax.experimental import pallas as pl
from jax.experimental.pallas import tpu as pltpu
from jax.sharding import Mesh, PartitionSpec as P

EPSILON = 1e-06
GELU_SCALE = 0.7978845608028654
LEARNING = 8.0
PAIR = ("section", "half")


def gelu_parts(preact):
    inner = GELU_SCALE * (preact + 0.044715 * preact * preact * preact)
    tanh_val = jnp.tanh(inner)
    gelu_val = 0.5 * preact * (1.0 + tanh_val)
    slopes = 0.5 * (1.0 + tanh_val) + 0.5 * preact * (1.0 - tanh_val * tanh_val) * GELU_SCALE * (
        1.0 + 3.0 * 0.044715 * preact * preact
    )
    return (gelu_val, slopes)


def route_tables(routes, blocks):
    micro_count, bound_count, replicas, capacity = routes.shape
    slot_ids = jnp.arange(capacity, dtype=jnp.int32)
    replica_ids = jnp.arange(replicas, dtype=jnp.int32)
    live_now = jnp.broadcast_to(slot_ids[None, None, :] < blocks, (micro_count, replicas, capacity))
    link_list = []
    live_list = [live_now]
    for bound_idx in range(bound_count):
        target = jnp.where(live_now, routes[:, bound_idx], -1).reshape(
            micro_count, replicas * capacity
        )
        matches = (target[:, :, None] == replica_ids[None, None, :]).astype(jnp.int32)
        before = jnp.cumsum(matches, axis=1) - matches
        position = jnp.sum(matches * before, axis=2)
        link_table = matches[:, :, :, None] * (
            position[:, :, None, None] == slot_ids[None, None, None, :]
        ).astype(jnp.int32)
        link_table = link_table.reshape(micro_count, replicas, capacity, replicas, capacity)
        link_list.append(link_table.astype(jnp.float32))
        live_now = jnp.sum(link_table, axis=(1, 2)) > 0
        live_list.append(live_now)
    return (link_list, live_list)


def layer_front(flat_rows, weight_in, scale_in):
    widened = flat_rows.astype(jnp.float32)
    inverse = lax.rsqrt(jnp.mean(widened * widened, axis=-1, keepdims=True) + EPSILON)
    normed = (widened * inverse).astype(jnp.bfloat16)
    preact = jnp.dot(normed, weight_in, preferred_element_type=jnp.float32) * scale_in
    return (widened, inverse, normed, preact)


def plane_kernel(count, spread, active, x_ref, out_ref, held, send_sem, recv_sem):
    section = lax.axis_index("section")

    @pl.when(section == active)
    def _():
        plane_exchange(count, spread, section, x_ref, out_ref, held, send_sem, recv_sem)

    @pl.when(section != active)
    def _():
        out_ref[...] = jnp.zeros_like(out_ref)


def plane_exchange(count, spread, section, x_ref, out_ref, held, send_sem, recv_sem):
    half = lax.axis_index("half")
    me = lax.axis_index("plane")
    barrier = pltpu.get_barrier_semaphore()
    for step in range(1, count):
        peer = lax.rem(me + step, count)
        pl.semaphore_signal(
            barrier, inc=1, device_id=(section, half, peer), device_id_type=pl.DeviceIdType.MESH
        )
    pl.semaphore_wait(barrier, count - 1)
    copies = []
    for step in range(1, count):
        peer = lax.rem(me + step, count)
        copy = pltpu.make_async_remote_copy(
            src_ref=x_ref.at[0] if spread else x_ref.at[peer],
            dst_ref=held.at[me],
            send_sem=send_sem.at[step],
            recv_sem=recv_sem.at[step],
            device_id=(section, half, peer),
            device_id_type=pl.DeviceIdType.MESH,
        )
        copy.start()
        copies.append(copy)
    own = x_ref[0] if spread else x_ref[me]
    for copy in copies:
        copy.wait()
    out_ref[...] = held[...]
    out_ref[me] = own


def plane_call(value, count, spread, ident, active):
    lanes = value[0].size // 16
    dense = plane_dense(value.reshape(value.shape[0], 16, lanes), count, spread, ident, active)
    return dense.reshape((count,) + value.shape[1:])


def plane_dense(value, count, spread, ident, active):
    shape = (count,) + value.shape[1:]
    return pl.pallas_call(
        lambda *refs: plane_kernel(count, spread, active, *refs),
        out_shape=jax.ShapeDtypeStruct(shape, value.dtype),
        in_specs=[pl.BlockSpec(memory_space=pltpu.VMEM)],
        out_specs=pl.BlockSpec(memory_space=pltpu.VMEM),
        scratch_shapes=[
            pltpu.VMEM(shape, value.dtype),
            pltpu.SemaphoreType.DMA((count,)),
            pltpu.SemaphoreType.DMA((count,)),
        ],
        compiler_params=pltpu.CompilerParams(collective_id=ident, has_side_effects=True),
    )(value)


def gather_rows(piece, active):
    return plane_call(piece, lax.axis_size("plane"), True, 4 + active, active)


def sum_rows(partial_value, active):
    parts = plane_call(partial_value.astype(jnp.bfloat16), lax.axis_size("plane"), False, active, active)
    return jnp.sum(parts.astype(jnp.float32), axis=0, keepdims=True)


def own_rows(full, shard_idx):
    return lax.dynamic_slice_in_dim(full, shard_idx, 1, axis=0)


def forward_piece(x_full, weight_in, weight_out, scale_in, scale_out, shard_idx, active):
    shape = x_full.shape
    widened, inverse, normed, preact = layer_front(x_full.reshape(-1, shape[-1]), weight_in, scale_in)
    gelu_val, slopes = gelu_parts(preact)
    activated = gelu_val.astype(jnp.bfloat16)
    partial_value = jnp.dot(activated, weight_out, preferred_element_type=jnp.float32) * scale_out
    summed = sum_rows(partial_value.reshape(shape), active)
    return (own_rows(x_full, shard_idx).astype(jnp.float32) + summed).astype(jnp.bfloat16)


def backward_piece(
    x_full, up_full, up_piece, weight_in, weight_out, scale_in, scale_out, shard_idx, active
):
    shape = x_full.shape
    widened, inverse, normed, preact = layer_front(x_full.reshape(-1, shape[-1]), weight_in, scale_in)
    gelu_val, slopes = gelu_parts(preact)
    d_act = (
        lax.dot_general(
            up_full.reshape(-1, shape[-1]), weight_out, (((1,), (1,)), ((), ())),
            preferred_element_type=jnp.float32,
        )
        * scale_out
    )
    d_pre = (d_act * slopes).astype(jnp.bfloat16)
    d_normed = (
        lax.dot_general(d_pre, weight_in, (((1,), (1,)), ((), ())), preferred_element_type=jnp.float32)
        * scale_in
    )
    normed_piece = sum_rows(d_normed.reshape(shape), active)
    wide_piece = own_rows(x_full, shard_idx).astype(jnp.float32)
    inv_piece = own_rows(inverse.reshape(shape[:-1] + (1,)), shard_idx)
    grad_piece = (
        up_piece.astype(jnp.float32)
        + inv_piece * normed_piece
        - wide_piece
        * inv_piece
        * inv_piece
        * inv_piece
        * jnp.mean(normed_piece * wide_piece, axis=-1, keepdims=True)
    )
    return grad_piece.astype(jnp.bfloat16)


def weight_grads(x_full, up_full, weight_in, weight_out, scale_in, scale_out):
    width = x_full.shape[-1]
    widened, inverse, normed, preact = layer_front(x_full.reshape(-1, width), weight_in, scale_in)
    gelu_val, slopes = gelu_parts(preact)
    activated = gelu_val.astype(jnp.bfloat16)
    ups = up_full.reshape(-1, width)
    d_out = (
        lax.dot_general(activated, ups, (((0,), (0,)), ((), ())), preferred_element_type=jnp.float32)
        * scale_out
    )
    d_act = (
        lax.dot_general(ups, weight_out, (((1,), (1,)), ((), ())), preferred_element_type=jnp.float32)
        * scale_out
    )
    d_pre = (d_act * slopes).astype(jnp.bfloat16)
    d_in = (
        lax.dot_general(normed, d_pre, (((0,), (0,)), ((), ())), preferred_element_type=jnp.float32)
        * scale_in
    )
    return (d_in, d_out)


def cross_boundary(piece, source, target, replicas):
    straight = [(source * replicas + h, target * replicas + h) for h in range(replicas)]
    crossed = [(source * replicas + h, target * replicas + (replicas - 1 - h)) for h in range(replicas)]
    return (lax.ppermute(piece, PAIR, straight), lax.ppermute(piece, PAIR, crossed))


def swap_sections(stepped_in, stepped_out, chosen, section_count, replicas):
    pairs = [
        (section * replicas + h, section * replicas + replicas - 1 - h)
        for section in range(section_count)
        if (chosen >> section) & 1
        for h in range(replicas)
    ]
    if not pairs:
        return (jnp.zeros_like(stepped_in), jnp.zeros_like(stepped_out))
    return (lax.ppermute(stepped_in, PAIR, pairs), lax.ppermute(stepped_out, PAIR, pairs))


def on_device(block_inputs, routes, cotangent, gossip_peer, w_in, w_out):
    section_count = lax.axis_size("section")
    replicas = lax.axis_size("half")
    group_size = lax.axis_size("plane")
    my_section = lax.axis_index("section")
    replica = lax.axis_index("half")
    shard_idx = lax.axis_index("plane")
    micro_count, blocks, piece_rows, model_width = block_inputs.shape
    capacity = cotangent.shape[1]
    weight_in = w_in[0]
    weight_out = w_out[0]
    hidden = weight_in.shape[1]
    scale_in = model_width ** (-0.5)
    scale_out = (hidden * group_size) ** (-0.5)
    link_list, live_list = route_tables(routes, blocks)

    def padded(full):
        filler = jnp.zeros(full.shape[:2] + (capacity - full.shape[2],) + full.shape[3:], full.dtype)
        return jnp.concatenate([full, filler], axis=2)

    last_live = lax.dynamic_index_in_dim(live_list[section_count - 1], replica, 1, keepdims=False)
    up_piece = jnp.where(
        last_live[None, :, :, None], cotangent.transpose(2, 0, 1, 3), jnp.zeros((), jnp.bfloat16)
    )
    up_full = gather_rows(up_piece, section_count - 1)
    x_cur = gather_rows(block_inputs.transpose(2, 0, 1, 3), 0)
    x_cur, up_full = lax.optimization_barrier((x_cur, up_full))
    x_keep = padded(x_cur)
    for bound in range(section_count - 1):
        piece = forward_piece(x_cur, weight_in, weight_out, scale_in, scale_out, shard_idx, bound)
        straight, crossed = cross_boundary(piece, bound, bound + 1, replicas)
        sources = jnp.stack(
            [jnp.where(replica == h, straight, crossed) for h in range(replicas)]
        )[:, 0]
        mine = lax.dynamic_index_in_dim(link_list[bound], replica, 3, keepdims=False)
        mine = mine[:, :, : piece.shape[2], :]
        routed = jnp.einsum(
            "mqjk,qmjd->mkd", mine.astype(jnp.bfloat16), sources,
            preferred_element_type=jnp.float32,
        ).astype(jnp.bfloat16)[None]
        x_cur = gather_rows(routed, bound + 1)
        x_keep = jnp.where(my_section == bound + 1, x_cur, x_keep)

    up_keep = up_full
    for depth in reversed(range(1, section_count)):
        grad_piece = backward_piece(
            x_keep, up_full, up_piece, weight_in, weight_out, scale_in, scale_out, shard_idx, depth
        )
        straight, crossed = cross_boundary(grad_piece, depth, depth - 1, replicas)
        sources = jnp.stack(
            [jnp.where(replica == h, straight, crossed) for h in range(replicas)]
        )[:, 0]
        mine = lax.dynamic_index_in_dim(link_list[depth - 1], replica, 1, keepdims=False)
        if depth == 1:
            mine = mine[:, :blocks]
        up_piece = jnp.einsum(
            "mjdk,dmkD->mjD", mine.astype(jnp.bfloat16), sources,
            preferred_element_type=jnp.float32,
        ).astype(jnp.bfloat16)[None]
        up_full = gather_rows(up_piece, depth - 1)
        up_keep = jnp.where(my_section == depth - 1, padded(up_full), up_keep)

    accum_in, accum_out = weight_grads(x_keep, up_keep, weight_in, weight_out, scale_in, scale_out)
    stepped_in = (weight_in.astype(jnp.float32) - LEARNING * accum_in).astype(jnp.bfloat16)
    stepped_out = (weight_out.astype(jnp.float32) - LEARNING * accum_out).astype(jnp.bfloat16)
    partner = gossip_peer[my_section, replica]
    paired = partner != replica
    pattern = jnp.sum(
        (gossip_peer[:, 0] != 0).astype(jnp.int32) << jnp.arange(section_count, dtype=jnp.int32)
    )
    other_in, other_out = lax.switch(
        pattern,
        [
            lambda a, b, chosen=chosen: swap_sections(a, b, chosen, section_count, replicas)
            for chosen in range(2**section_count)
        ],
        stepped_in,
        stepped_out,
    )
    chosen_in = jnp.where(paired, other_in, stepped_in)
    chosen_out = jnp.where(paired, other_out, stepped_out)
    new_in = (0.5 * (stepped_in.astype(jnp.float32) + chosen_in.astype(jnp.float32))).astype(
        jnp.bfloat16
    )
    new_out = (0.5 * (stepped_out.astype(jnp.float32) + chosen_out.astype(jnp.float32))).astype(
        jnp.bfloat16
    )
    return (new_in[None], new_out[None])


def solution(mesh):
    sections = mesh.shape["section"]
    reps = mesh.shape["rep"]
    inner = Mesh(np.asarray(mesh.devices).reshape(sections, 2, reps // 2), ("section", "half", "plane"))
    rows = ("half", "plane")
    return jax.shard_map(
        on_device,
        mesh=inner,
        in_specs=(
            P(None, None, rows, None),
            P(),
            P(None, None, rows, None),
            P(),
            P("section", None, rows),
            P("section", rows, None),
        ),
        out_specs=(P("section", None, rows), P("section", rows, None)),
        check_vma=False,
    )
```

```python
import numpy as np
import jax
import jax.numpy as jnp
from jax import lax
from jax.experimental import pallas as pl
from jax.experimental.pallas import tpu as pltpu
from jax.sharding import Mesh, PartitionSpec as P

EPSILON = 1e-06
GELU_SCALE = 0.7978845608028654
LEARNING = 8.0
PAIR = ("section", "half")


def gelu_parts(preact):
    inner = GELU_SCALE * (preact + 0.044715 * preact * preact * preact)
    tanh_val = jnp.tanh(inner)
    gelu_val = 0.5 * preact * (1.0 + tanh_val)
    slopes = 0.5 * (1.0 + tanh_val) + 0.5 * preact * (1.0 - tanh_val * tanh_val) * GELU_SCALE * (
        1.0 + 3.0 * 0.044715 * preact * preact
    )
    return (gelu_val, slopes)


def route_tables(routes, blocks):
    micro_count, bound_count, replicas, capacity = routes.shape
    slot_ids = jnp.arange(capacity, dtype=jnp.int32)
    replica_ids = jnp.arange(replicas, dtype=jnp.int32)
    live_now = jnp.broadcast_to(slot_ids[None, None, :] < blocks, (micro_count, replicas, capacity))
    link_list = []
    live_list = [live_now]
    for bound_idx in range(bound_count):
        target = jnp.where(live_now, routes[:, bound_idx], -1).reshape(
            micro_count, replicas * capacity
        )
        matches = (target[:, :, None] == replica_ids[None, None, :]).astype(jnp.int32)
        before = jnp.cumsum(matches, axis=1) - matches
        position = jnp.sum(matches * before, axis=2)
        link_table = matches[:, :, :, None] * (
            position[:, :, None, None] == slot_ids[None, None, None, :]
        ).astype(jnp.int32)
        link_table = link_table.reshape(micro_count, replicas, capacity, replicas, capacity)
        link_list.append(link_table.astype(jnp.float32))
        live_now = jnp.sum(link_table, axis=(1, 2)) > 0
        live_list.append(live_now)
    return (link_list, live_list)


def layer_front(flat_rows, weight_in, scale_in):
    widened = flat_rows.astype(jnp.float32)
    inverse = lax.rsqrt(jnp.mean(widened * widened, axis=-1, keepdims=True) + EPSILON)
    normed = (widened * inverse).astype(jnp.bfloat16)
    preact = jnp.dot(normed, weight_in, preferred_element_type=jnp.float32) * scale_in
    return (widened, inverse, normed, preact)


def ring_hops(offset, size):
    return min(offset, size - offset)


def far_first(count):
    side = 4 if count == 16 else 1
    def hops(step):
        return ring_hops(step % side, side) + ring_hops(step // side, count // side)
    return sorted(range(1, count), key=lambda step: (-hops(step), step))


def plane_kernel(count, spread, active, x_ref, out_ref, held, send_sem, recv_sem):
    section = lax.axis_index("section")

    @pl.when(section == active)
    def _():
        plane_exchange(count, spread, section, x_ref, out_ref, held, send_sem, recv_sem)

    @pl.when(section != active)
    def _():
        out_ref[...] = jnp.zeros_like(out_ref)


def plane_exchange(count, spread, section, x_ref, out_ref, held, send_sem, recv_sem):
    half = lax.axis_index("half")
    me = lax.axis_index("plane")
    barrier = pltpu.get_barrier_semaphore()
    order = far_first(count)
    for step in order:
        peer = lax.bitwise_xor(me, step)
        pl.semaphore_signal(
            barrier, inc=1, device_id=(section, half, peer), device_id_type=pl.DeviceIdType.MESH
        )
    pl.semaphore_wait(barrier, count - 1)
    copies = []
    for step in order:
        peer = lax.bitwise_xor(me, step)
        copy = pltpu.make_async_remote_copy(
            src_ref=x_ref.at[0] if spread else x_ref.at[peer],
            dst_ref=held.at[me],
            send_sem=send_sem.at[step],
            recv_sem=recv_sem.at[step],
            device_id=(section, half, peer),
            device_id_type=pl.DeviceIdType.MESH,
        )
        copy.start()
        copies.append(copy)
    own = x_ref[0] if spread else x_ref[me]
    for copy in copies:
        copy.wait()
    out_ref[...] = held[...]
    out_ref[me] = own


def plane_call(value, count, spread, ident, active):
    lanes = value[0].size // 16
    dense = plane_dense(value.reshape(value.shape[0], 16, lanes), count, spread, ident, active)
    return dense.reshape((count,) + value.shape[1:])


def plane_dense(value, count, spread, ident, active):
    shape = (count,) + value.shape[1:]
    return pl.pallas_call(
        lambda *refs: plane_kernel(count, spread, active, *refs),
        out_shape=jax.ShapeDtypeStruct(shape, value.dtype),
        in_specs=[pl.BlockSpec(memory_space=pltpu.VMEM)],
        out_specs=pl.BlockSpec(memory_space=pltpu.VMEM),
        scratch_shapes=[
            pltpu.VMEM(shape, value.dtype),
            pltpu.SemaphoreType.DMA((count,)),
            pltpu.SemaphoreType.DMA((count,)),
        ],
        compiler_params=pltpu.CompilerParams(collective_id=ident, has_side_effects=True),
    )(value)


def gather_rows(piece, active):
    return plane_call(piece, lax.axis_size("plane"), True, 4 + active, active)


def sum_rows(partial_value, active):
    parts = plane_call(partial_value.astype(jnp.bfloat16), lax.axis_size("plane"), False, active, active)
    return jnp.sum(parts.astype(jnp.float32), axis=0, keepdims=True)


def own_rows(full, shard_idx):
    return lax.dynamic_slice_in_dim(full, shard_idx, 1, axis=0)


def forward_piece(x_full, weight_in, weight_out, scale_in, scale_out, shard_idx, active):
    shape = x_full.shape
    widened, inverse, normed, preact = layer_front(x_full.reshape(-1, shape[-1]), weight_in, scale_in)
    gelu_val, slopes = gelu_parts(preact)
    activated = gelu_val.astype(jnp.bfloat16)
    partial_value = jnp.dot(activated, weight_out, preferred_element_type=jnp.float32) * scale_out
    summed = sum_rows(partial_value.reshape(shape), active)
    return (own_rows(x_full, shard_idx).astype(jnp.float32) + summed).astype(jnp.bfloat16)


def backward_piece(
    x_full, up_full, up_piece, weight_in, weight_out, scale_in, scale_out, shard_idx, active
):
    shape = x_full.shape
    widened, inverse, normed, preact = layer_front(x_full.reshape(-1, shape[-1]), weight_in, scale_in)
    gelu_val, slopes = gelu_parts(preact)
    d_act = (
        lax.dot_general(
            up_full.reshape(-1, shape[-1]), weight_out, (((1,), (1,)), ((), ())),
            preferred_element_type=jnp.float32,
        )
        * scale_out
    )
    d_pre = (d_act * slopes).astype(jnp.bfloat16)
    d_normed = (
        lax.dot_general(d_pre, weight_in, (((1,), (1,)), ((), ())), preferred_element_type=jnp.float32)
        * scale_in
    )
    normed_piece = sum_rows(d_normed.reshape(shape), active)
    wide_piece = own_rows(x_full, shard_idx).astype(jnp.float32)
    inv_piece = own_rows(inverse.reshape(shape[:-1] + (1,)), shard_idx)
    grad_piece = (
        up_piece.astype(jnp.float32)
        + inv_piece * normed_piece
        - wide_piece
        * inv_piece
        * inv_piece
        * inv_piece
        * jnp.mean(normed_piece * wide_piece, axis=-1, keepdims=True)
    )
    return grad_piece.astype(jnp.bfloat16)


def weight_grads(x_full, up_full, weight_in, weight_out, scale_in, scale_out):
    width = x_full.shape[-1]
    widened, inverse, normed, preact = layer_front(x_full.reshape(-1, width), weight_in, scale_in)
    gelu_val, slopes = gelu_parts(preact)
    activated = gelu_val.astype(jnp.bfloat16)
    ups = up_full.reshape(-1, width)
    d_out = (
        lax.dot_general(activated, ups, (((0,), (0,)), ((), ())), preferred_element_type=jnp.float32)
        * scale_out
    )
    d_act = (
        lax.dot_general(ups, weight_out, (((1,), (1,)), ((), ())), preferred_element_type=jnp.float32)
        * scale_out
    )
    d_pre = (d_act * slopes).astype(jnp.bfloat16)
    d_in = (
        lax.dot_general(normed, d_pre, (((0,), (0,)), ((), ())), preferred_element_type=jnp.float32)
        * scale_in
    )
    return (d_in, d_out)


def cross_boundary(piece, source, target, replicas):
    straight = [(source * replicas + h, target * replicas + h) for h in range(replicas)]
    crossed = [(source * replicas + h, target * replicas + (replicas - 1 - h)) for h in range(replicas)]
    return (lax.ppermute(piece, PAIR, straight), lax.ppermute(piece, PAIR, crossed))


def swap_sections(stepped_in, stepped_out, chosen, section_count, replicas):
    pairs = [
        (section * replicas + h, section * replicas + replicas - 1 - h)
        for section in range(section_count)
        if (chosen >> section) & 1
        for h in range(replicas)
    ]
    if not pairs:
        return (jnp.zeros_like(stepped_in), jnp.zeros_like(stepped_out))
    return (lax.ppermute(stepped_in, PAIR, pairs), lax.ppermute(stepped_out, PAIR, pairs))


def on_device(block_inputs, routes, cotangent, gossip_peer, w_in, w_out):
    section_count = lax.axis_size("section")
    replicas = lax.axis_size("half")
    group_size = lax.axis_size("plane")
    my_section = lax.axis_index("section")
    replica = lax.axis_index("half")
    shard_idx = lax.axis_index("plane")
    micro_count, blocks, piece_rows, model_width = block_inputs.shape
    capacity = cotangent.shape[1]
    weight_in = w_in[0]
    weight_out = w_out[0]
    hidden = weight_in.shape[1]
    scale_in = model_width ** (-0.5)
    scale_out = (hidden * group_size) ** (-0.5)
    link_list, live_list = route_tables(routes, blocks)

    def padded(full):
        filler = jnp.zeros(full.shape[:2] + (capacity - full.shape[2],) + full.shape[3:], full.dtype)
        return jnp.concatenate([full, filler], axis=2)

    x_cur = gather_rows(block_inputs.transpose(2, 0, 1, 3), 0)
    x_keep = padded(x_cur)
    for bound in range(section_count - 1):
        piece = forward_piece(x_cur, weight_in, weight_out, scale_in, scale_out, shard_idx, bound)
        straight, crossed = cross_boundary(piece, bound, bound + 1, replicas)
        sources = jnp.stack(
            [jnp.where(replica == h, straight, crossed) for h in range(replicas)]
        )[:, 0]
        mine = lax.dynamic_index_in_dim(link_list[bound], replica, 3, keepdims=False)
        mine = mine[:, :, : piece.shape[2], :]
        routed = jnp.einsum(
            "mqjk,qmjd->mkd", mine.astype(jnp.bfloat16), sources,
            preferred_element_type=jnp.float32,
        ).astype(jnp.bfloat16)[None]
        x_cur = gather_rows(routed, bound + 1)
        x_keep = jnp.where(my_section == bound + 1, x_cur, x_keep)

    last_live = lax.dynamic_index_in_dim(live_list[section_count - 1], replica, 1, keepdims=False)
    up_piece = jnp.where(
        last_live[None, :, :, None], cotangent.transpose(2, 0, 1, 3), jnp.zeros((), jnp.bfloat16)
    )
    up_full = gather_rows(up_piece, section_count - 1)
    up_keep = up_full
    for depth in reversed(range(1, section_count)):
        grad_piece = backward_piece(
            x_keep, up_full, up_piece, weight_in, weight_out, scale_in, scale_out, shard_idx, depth
        )
        straight, crossed = cross_boundary(grad_piece, depth, depth - 1, replicas)
        sources = jnp.stack(
            [jnp.where(replica == h, straight, crossed) for h in range(replicas)]
        )[:, 0]
        mine = lax.dynamic_index_in_dim(link_list[depth - 1], replica, 1, keepdims=False)
        if depth == 1:
            mine = mine[:, :blocks]
        up_piece = jnp.einsum(
            "mjdk,dmkD->mjD", mine.astype(jnp.bfloat16), sources,
            preferred_element_type=jnp.float32,
        ).astype(jnp.bfloat16)[None]
        up_full = gather_rows(up_piece, depth - 1)
        up_keep = jnp.where(my_section == depth - 1, padded(up_full), up_keep)

    accum_in, accum_out = weight_grads(x_keep, up_keep, weight_in, weight_out, scale_in, scale_out)
    stepped_in = (weight_in.astype(jnp.float32) - LEARNING * accum_in).astype(jnp.bfloat16)
    stepped_out = (weight_out.astype(jnp.float32) - LEARNING * accum_out).astype(jnp.bfloat16)
    partner = gossip_peer[my_section, replica]
    paired = partner != replica
    pattern = jnp.sum(
        (gossip_peer[:, 0] != 0).astype(jnp.int32) << jnp.arange(section_count, dtype=jnp.int32)
    )
    other_in, other_out = lax.switch(
        pattern,
        [
            lambda a, b, chosen=chosen: swap_sections(a, b, chosen, section_count, replicas)
            for chosen in range(2**section_count)
        ],
        stepped_in,
        stepped_out,
    )
    chosen_in = jnp.where(paired, other_in, stepped_in)
    chosen_out = jnp.where(paired, other_out, stepped_out)
    new_in = (0.5 * (stepped_in.astype(jnp.float32) + chosen_in.astype(jnp.float32))).astype(
        jnp.bfloat16
    )
    new_out = (0.5 * (stepped_out.astype(jnp.float32) + chosen_out.astype(jnp.float32))).astype(
        jnp.bfloat16
    )
    return (new_in[None], new_out[None])


def solution(mesh):
    sections = mesh.shape["section"]
    reps = mesh.shape["rep"]
    inner = Mesh(np.asarray(mesh.devices).reshape(sections, 2, reps // 2), ("section", "half", "plane"))
    rows = ("half", "plane")
    return jax.shard_map(
        on_device,
        mesh=inner,
        in_specs=(
            P(None, None, rows, None),
            P(),
            P(None, None, rows, None),
            P(),
            P("section", None, rows),
            P("section", rows, None),
        ),
        out_specs=(P("section", None, rows), P("section", rows, None)),
        check_vma=False,
    )
```

```python
import numpy as np
import jax
import jax.numpy as jnp
from jax import lax
from jax.experimental import pallas as pl
from jax.experimental.pallas import tpu as pltpu
from jax.sharding import Mesh, PartitionSpec as P

EPSILON = 1e-06
GELU_SCALE = 0.7978845608028654
LEARNING = 8.0
PAIR = ("section", "half")


def gelu_parts(preact):
    inner = GELU_SCALE * (preact + 0.044715 * preact * preact * preact)
    tanh_val = jnp.tanh(inner)
    gelu_val = 0.5 * preact * (1.0 + tanh_val)
    slopes = 0.5 * (1.0 + tanh_val) + 0.5 * preact * (1.0 - tanh_val * tanh_val) * GELU_SCALE * (
        1.0 + 3.0 * 0.044715 * preact * preact
    )
    return (gelu_val, slopes)


def route_tables(routes, blocks):
    micro_count, bound_count, replicas, capacity = routes.shape
    slot_ids = jnp.arange(capacity, dtype=jnp.int32)
    replica_ids = jnp.arange(replicas, dtype=jnp.int32)
    live_now = jnp.broadcast_to(slot_ids[None, None, :] < blocks, (micro_count, replicas, capacity))
    link_list = []
    live_list = [live_now]
    for bound_idx in range(bound_count):
        target = jnp.where(live_now, routes[:, bound_idx], -1).reshape(
            micro_count, replicas * capacity
        )
        matches = (target[:, :, None] == replica_ids[None, None, :]).astype(jnp.int32)
        before = jnp.cumsum(matches, axis=1) - matches
        position = jnp.sum(matches * before, axis=2)
        link_table = matches[:, :, :, None] * (
            position[:, :, None, None] == slot_ids[None, None, None, :]
        ).astype(jnp.int32)
        link_table = link_table.reshape(micro_count, replicas, capacity, replicas, capacity)
        link_list.append(link_table.astype(jnp.float32))
        live_now = jnp.sum(link_table, axis=(1, 2)) > 0
        live_list.append(live_now)
    return (link_list, live_list)


def layer_front(flat_rows, weight_in, scale_in):
    widened = flat_rows.astype(jnp.float32)
    inverse = lax.rsqrt(jnp.mean(widened * widened, axis=-1, keepdims=True) + EPSILON)
    normed = (widened * inverse).astype(jnp.bfloat16)
    preact = jnp.dot(normed, weight_in, preferred_element_type=jnp.float32) * scale_in
    return (widened, inverse, normed, preact)


def ring_hops(offset, size):
    return min(offset, size - offset)


def far_first(count):
    side = 4 if count == 16 else 1
    def hops(step):
        return ring_hops(step % side, side) + ring_hops(step // side, count // side)
    return sorted(range(1, count), key=lambda step: (-hops(step), step))


def plane_kernel(count, spread, active, x_ref, out_ref, held, send_sem, recv_sem):
    section = lax.axis_index("section")

    @pl.when(section == active)
    def _():
        plane_exchange(count, spread, section, x_ref, out_ref, held, send_sem, recv_sem)

    @pl.when(section != active)
    def _():
        out_ref[...] = jnp.zeros_like(out_ref)


def plane_exchange(count, spread, section, x_ref, out_ref, held, send_sem, recv_sem):
    half = lax.axis_index("half")
    me = lax.axis_index("plane")
    if not spread:
        held[me] = x_ref[me]
    barrier = pltpu.get_barrier_semaphore()
    order = far_first(count)
    for step in order:
        peer = lax.bitwise_xor(me, step)
        pl.semaphore_signal(
            barrier, inc=1, device_id=(section, half, peer), device_id_type=pl.DeviceIdType.MESH
        )
    pl.semaphore_wait(barrier, count - 1)
    copies = []
    for step in order:
        peer = lax.bitwise_xor(me, step)
        copy = pltpu.make_async_remote_copy(
            src_ref=x_ref.at[0] if spread else x_ref.at[peer],
            dst_ref=held.at[me],
            send_sem=send_sem.at[step],
            recv_sem=recv_sem.at[step],
            device_id=(section, half, peer),
            device_id_type=pl.DeviceIdType.MESH,
        )
        copy.start()
        copies.append(copy)
    for copy in copies:
        copy.wait()
    if spread:
        out_ref[...] = held[...]
        out_ref[me] = x_ref[0]
    else:
        total = held[0].astype(jnp.float32)
        for chunk in range(1, count):
            total = total + held[chunk].astype(jnp.float32)
        out_ref[0] = total


def plane_call(value, count, spread, ident, active):
    lanes = value[0].size // 16
    dense = plane_dense(value.reshape(value.shape[0], 16, lanes), count, spread, ident, active)
    return dense.reshape((dense.shape[0],) + value.shape[1:])


def plane_dense(value, count, spread, ident, active):
    shape = (count,) + value.shape[1:]
    result = shape if spread else (1,) + value.shape[1:]
    return pl.pallas_call(
        lambda *refs: plane_kernel(count, spread, active, *refs),
        out_shape=jax.ShapeDtypeStruct(result, value.dtype if spread else jnp.float32),
        in_specs=[pl.BlockSpec(memory_space=pltpu.VMEM)],
        out_specs=pl.BlockSpec(memory_space=pltpu.VMEM),
        scratch_shapes=[
            pltpu.VMEM(shape, value.dtype),
            pltpu.SemaphoreType.DMA((count,)),
            pltpu.SemaphoreType.DMA((count,)),
        ],
        compiler_params=pltpu.CompilerParams(collective_id=ident, has_side_effects=True),
    )(value)


def gather_rows(piece, active):
    return plane_call(piece, lax.axis_size("plane"), True, 4 + active, active)


def sum_rows(partial_value, active):
    return plane_call(partial_value.astype(jnp.bfloat16), lax.axis_size("plane"), False, active, active)


def own_rows(full, shard_idx):
    return lax.dynamic_slice_in_dim(full, shard_idx, 1, axis=0)


def forward_piece(x_full, weight_in, weight_out, scale_in, scale_out, shard_idx, active):
    shape = x_full.shape
    widened, inverse, normed, preact = layer_front(x_full.reshape(-1, shape[-1]), weight_in, scale_in)
    gelu_val, slopes = gelu_parts(preact)
    activated = gelu_val.astype(jnp.bfloat16)
    partial_value = jnp.dot(activated, weight_out, preferred_element_type=jnp.float32) * scale_out
    summed = sum_rows(partial_value.reshape(shape), active)
    return (own_rows(x_full, shard_idx).astype(jnp.float32) + summed).astype(jnp.bfloat16)


def backward_piece(
    x_full, up_full, up_piece, weight_in, weight_out, scale_in, scale_out, shard_idx, active
):
    shape = x_full.shape
    widened, inverse, normed, preact = layer_front(x_full.reshape(-1, shape[-1]), weight_in, scale_in)
    gelu_val, slopes = gelu_parts(preact)
    d_act = (
        lax.dot_general(
            up_full.reshape(-1, shape[-1]), weight_out, (((1,), (1,)), ((), ())),
            preferred_element_type=jnp.float32,
        )
        * scale_out
    )
    d_pre = (d_act * slopes).astype(jnp.bfloat16)
    d_normed = (
        lax.dot_general(d_pre, weight_in, (((1,), (1,)), ((), ())), preferred_element_type=jnp.float32)
        * scale_in
    )
    normed_piece = sum_rows(d_normed.reshape(shape), active)
    wide_piece = own_rows(x_full, shard_idx).astype(jnp.float32)
    inv_piece = own_rows(inverse.reshape(shape[:-1] + (1,)), shard_idx)
    grad_piece = (
        up_piece.astype(jnp.float32)
        + inv_piece * normed_piece
        - wide_piece
        * inv_piece
        * inv_piece
        * inv_piece
        * jnp.mean(normed_piece * wide_piece, axis=-1, keepdims=True)
    )
    return grad_piece.astype(jnp.bfloat16)


def weight_grads(x_full, up_full, weight_in, weight_out, scale_in, scale_out):
    width = x_full.shape[-1]
    widened, inverse, normed, preact = layer_front(x_full.reshape(-1, width), weight_in, scale_in)
    gelu_val, slopes = gelu_parts(preact)
    activated = gelu_val.astype(jnp.bfloat16)
    ups = up_full.reshape(-1, width)
    d_out = (
        lax.dot_general(activated, ups, (((0,), (0,)), ((), ())), preferred_element_type=jnp.float32)
        * scale_out
    )
    d_act = (
        lax.dot_general(ups, weight_out, (((1,), (1,)), ((), ())), preferred_element_type=jnp.float32)
        * scale_out
    )
    d_pre = (d_act * slopes).astype(jnp.bfloat16)
    d_in = (
        lax.dot_general(normed, d_pre, (((0,), (0,)), ((), ())), preferred_element_type=jnp.float32)
        * scale_in
    )
    return (d_in, d_out)


def cross_boundary(piece, source, target, replicas):
    straight = [(source * replicas + h, target * replicas + h) for h in range(replicas)]
    crossed = [(source * replicas + h, target * replicas + (replicas - 1 - h)) for h in range(replicas)]
    return (lax.ppermute(piece, PAIR, straight), lax.ppermute(piece, PAIR, crossed))


def swap_sections(stepped_in, stepped_out, chosen, section_count, replicas):
    pairs = [
        (section * replicas + h, section * replicas + replicas - 1 - h)
        for section in range(section_count)
        if (chosen >> section) & 1
        for h in range(replicas)
    ]
    if not pairs:
        return (jnp.zeros_like(stepped_in), jnp.zeros_like(stepped_out))
    return (lax.ppermute(stepped_in, PAIR, pairs), lax.ppermute(stepped_out, PAIR, pairs))


def on_device(block_inputs, routes, cotangent, gossip_peer, w_in, w_out):
    section_count = lax.axis_size("section")
    replicas = lax.axis_size("half")
    group_size = lax.axis_size("plane")
    my_section = lax.axis_index("section")
    replica = lax.axis_index("half")
    shard_idx = lax.axis_index("plane")
    micro_count, blocks, piece_rows, model_width = block_inputs.shape
    capacity = cotangent.shape[1]
    weight_in = w_in[0]
    weight_out = w_out[0]
    hidden = weight_in.shape[1]
    scale_in = model_width ** (-0.5)
    scale_out = (hidden * group_size) ** (-0.5)
    link_list, live_list = route_tables(routes, blocks)

    def padded(full):
        filler = jnp.zeros(full.shape[:2] + (capacity - full.shape[2],) + full.shape[3:], full.dtype)
        return jnp.concatenate([full, filler], axis=2)

    x_cur = gather_rows(block_inputs.transpose(2, 0, 1, 3), 0)
    x_keep = padded(x_cur)
    for bound in range(section_count - 1):
        piece = forward_piece(x_cur, weight_in, weight_out, scale_in, scale_out, shard_idx, bound)
        straight, crossed = cross_boundary(piece, bound, bound + 1, replicas)
        sources = jnp.stack(
            [jnp.where(replica == h, straight, crossed) for h in range(replicas)]
        )[:, 0]
        mine = lax.dynamic_index_in_dim(link_list[bound], replica, 3, keepdims=False)
        mine = mine[:, :, : piece.shape[2], :]
        routed = jnp.einsum(
            "mqjk,qmjd->mkd", mine.astype(jnp.bfloat16), sources,
            preferred_element_type=jnp.float32,
        ).astype(jnp.bfloat16)[None]
        x_cur = gather_rows(routed, bound + 1)
        x_keep = jnp.where(my_section == bound + 1, x_cur, x_keep)

    last_live = lax.dynamic_index_in_dim(live_list[section_count - 1], replica, 1, keepdims=False)
    up_piece = jnp.where(
        last_live[None, :, :, None], cotangent.transpose(2, 0, 1, 3), jnp.zeros((), jnp.bfloat16)
    )
    up_full = gather_rows(up_piece, section_count - 1)
    up_keep = up_full
    for depth in reversed(range(1, section_count)):
        grad_piece = backward_piece(
            x_keep, up_full, up_piece, weight_in, weight_out, scale_in, scale_out, shard_idx, depth
        )
        straight, crossed = cross_boundary(grad_piece, depth, depth - 1, replicas)
        sources = jnp.stack(
            [jnp.where(replica == h, straight, crossed) for h in range(replicas)]
        )[:, 0]
        mine = lax.dynamic_index_in_dim(link_list[depth - 1], replica, 1, keepdims=False)
        if depth == 1:
            mine = mine[:, :blocks]
        up_piece = jnp.einsum(
            "mjdk,dmkD->mjD", mine.astype(jnp.bfloat16), sources,
            preferred_element_type=jnp.float32,
        ).astype(jnp.bfloat16)[None]
        up_full = gather_rows(up_piece, depth - 1)
        up_keep = jnp.where(my_section == depth - 1, padded(up_full), up_keep)

    accum_in, accum_out = weight_grads(x_keep, up_keep, weight_in, weight_out, scale_in, scale_out)
    stepped_in = (weight_in.astype(jnp.float32) - LEARNING * accum_in).astype(jnp.bfloat16)
    stepped_out = (weight_out.astype(jnp.float32) - LEARNING * accum_out).astype(jnp.bfloat16)
    partner = gossip_peer[my_section, replica]
    paired = partner != replica
    pattern = jnp.sum(
        (gossip_peer[:, 0] != 0).astype(jnp.int32) << jnp.arange(section_count, dtype=jnp.int32)
    )
    other_in, other_out = lax.switch(
        pattern,
        [
            lambda a, b, chosen=chosen: swap_sections(a, b, chosen, section_count, replicas)
            for chosen in range(2**section_count)
        ],
        stepped_in,
        stepped_out,
    )
    chosen_in = jnp.where(paired, other_in, stepped_in)
    chosen_out = jnp.where(paired, other_out, stepped_out)
    new_in = (0.5 * (stepped_in.astype(jnp.float32) + chosen_in.astype(jnp.float32))).astype(
        jnp.bfloat16
    )
    new_out = (0.5 * (stepped_out.astype(jnp.float32) + chosen_out.astype(jnp.float32))).astype(
        jnp.bfloat16
    )
    return (new_in[None], new_out[None])


def solution(mesh):
    sections = mesh.shape["section"]
    reps = mesh.shape["rep"]
    inner = Mesh(np.asarray(mesh.devices).reshape(sections, 2, reps // 2), ("section", "half", "plane"))
    rows = ("half", "plane")
    return jax.shard_map(
        on_device,
        mesh=inner,
        in_specs=(
            P(None, None, rows, None),
            P(),
            P(None, None, rows, None),
            P(),
            P("section", None, rows),
            P("section", rows, None),
        ),
        out_specs=(P("section", None, rows), P("section", rows, None)),
        check_vma=False,
    )
```

```python
import numpy as np
import jax
import jax.numpy as jnp
from jax import lax
from jax.experimental import pallas as pl
from jax.experimental.pallas import tpu as pltpu
from jax.sharding import Mesh, PartitionSpec as P

EPSILON = 1e-06
GELU_SCALE = 0.7978845608028654
LEARNING = 8.0
PAIR = ("section", "half")


def gelu_parts(preact):
    inner = GELU_SCALE * (preact + 0.044715 * preact * preact * preact)
    tanh_val = jnp.tanh(inner)
    gelu_val = 0.5 * preact * (1.0 + tanh_val)
    slopes = 0.5 * (1.0 + tanh_val) + 0.5 * preact * (1.0 - tanh_val * tanh_val) * GELU_SCALE * (
        1.0 + 3.0 * 0.044715 * preact * preact
    )
    return (gelu_val, slopes)


def route_tables(routes, blocks):
    micro_count, bound_count, replicas, capacity = routes.shape
    slot_ids = jnp.arange(capacity, dtype=jnp.int32)
    replica_ids = jnp.arange(replicas, dtype=jnp.int32)
    live_now = jnp.broadcast_to(slot_ids[None, None, :] < blocks, (micro_count, replicas, capacity))
    link_list = []
    live_list = [live_now]
    for bound_idx in range(bound_count):
        target = jnp.where(live_now, routes[:, bound_idx], -1).reshape(
            micro_count, replicas * capacity
        )
        matches = (target[:, :, None] == replica_ids[None, None, :]).astype(jnp.int32)
        before = jnp.cumsum(matches, axis=1) - matches
        position = jnp.sum(matches * before, axis=2)
        link_table = matches[:, :, :, None] * (
            position[:, :, None, None] == slot_ids[None, None, None, :]
        ).astype(jnp.int32)
        link_table = link_table.reshape(micro_count, replicas, capacity, replicas, capacity)
        link_list.append(link_table.astype(jnp.float32))
        live_now = jnp.sum(link_table, axis=(1, 2)) > 0
        live_list.append(live_now)
    return (link_list, live_list)


def layer_front(flat_rows, weight_in, scale_in):
    widened = flat_rows.astype(jnp.float32)
    inverse = lax.rsqrt(jnp.mean(widened * widened, axis=-1, keepdims=True) + EPSILON)
    normed = (widened * inverse).astype(jnp.bfloat16)
    preact = jnp.dot(normed, weight_in, preferred_element_type=jnp.float32) * scale_in
    return (widened, inverse, normed, preact)


def ring_hops(offset, size):
    return min(offset, size - offset)


def far_first(count):
    side = 4 if count == 16 else 1
    def hops(step):
        return ring_hops(step % side, side) + ring_hops(step // side, count // side)
    return sorted(range(1, count), key=lambda step: (-hops(step), step))


def plane_kernel(count, spread, active, x_ref, out_ref, held, send_sem, recv_sem):
    section = lax.axis_index("section")

    @pl.when(section == active)
    def _():
        plane_exchange(count, spread, section, x_ref, out_ref, held, send_sem, recv_sem)

    @pl.when(section != active)
    def _():
        out_ref[...] = jnp.zeros_like(out_ref)


def plane_exchange(count, spread, section, x_ref, out_ref, held, send_sem, recv_sem):
    half = lax.axis_index("half")
    me = lax.axis_index("plane")
    if not spread:
        held[me] = x_ref[me]
    barrier = pltpu.get_barrier_semaphore()
    order = far_first(count)
    for step in order:
        peer = lax.bitwise_xor(me, step)
        pl.semaphore_signal(
            barrier, inc=1, device_id=(section, half, peer), device_id_type=pl.DeviceIdType.MESH
        )
    pl.semaphore_wait(barrier, count - 1)
    copies = []
    for step in order:
        peer = lax.bitwise_xor(me, step)
        copy = pltpu.make_async_remote_copy(
            src_ref=x_ref.at[0] if spread else x_ref.at[peer],
            dst_ref=held.at[me],
            send_sem=send_sem.at[step],
            recv_sem=recv_sem.at[step],
            device_id=(section, half, peer),
            device_id_type=pl.DeviceIdType.MESH,
        )
        copy.start()
        copies.append(copy)
    for copy in copies:
        copy.wait()
    if spread:
        out_ref[...] = held[...]
        out_ref[me] = x_ref[0]
    else:
        total = held[0].astype(jnp.float32)
        for chunk in range(1, count):
            total = total + held[chunk].astype(jnp.float32)
        out_ref[0] = total


def plane_call(value, count, spread, ident, active):
    lanes = value[0].size // 16
    dense = plane_dense(value.reshape(value.shape[0], 16, lanes), count, spread, ident, active)
    return dense.reshape((dense.shape[0],) + value.shape[1:])


def plane_dense(value, count, spread, ident, active):
    shape = (count,) + value.shape[1:]
    result = shape if spread else (1,) + value.shape[1:]
    return pl.pallas_call(
        lambda *refs: plane_kernel(count, spread, active, *refs),
        out_shape=jax.ShapeDtypeStruct(result, value.dtype if spread else jnp.float32),
        in_specs=[pl.BlockSpec(memory_space=pltpu.VMEM)],
        out_specs=pl.BlockSpec(memory_space=pltpu.VMEM),
        scratch_shapes=[
            pltpu.VMEM(shape, value.dtype),
            pltpu.SemaphoreType.DMA((count,)),
            pltpu.SemaphoreType.DMA((count,)),
        ],
        compiler_params=pltpu.CompilerParams(collective_id=ident, has_side_effects=True),
    )(value)


def gather_rows(piece, active):
    return plane_call(piece, lax.axis_size("plane"), True, 4 + active, active)


def sum_rows(partial_value, active):
    return plane_call(partial_value.astype(jnp.bfloat16), lax.axis_size("plane"), False, active, active)


def own_rows(full, shard_idx):
    return lax.dynamic_slice_in_dim(full, shard_idx, 1, axis=0)


def forward_piece(x_full, weight_in, weight_out, scale_in, scale_out, shard_idx, active):
    shape = x_full.shape
    widened, inverse, normed, preact = layer_front(x_full.reshape(-1, shape[-1]), weight_in, scale_in)
    gelu_val, slopes = gelu_parts(preact)
    activated = gelu_val.astype(jnp.bfloat16)
    partial_value = jnp.dot(activated, weight_out, preferred_element_type=jnp.float32) * scale_out
    summed = sum_rows(partial_value.reshape(shape), active)
    piece = (own_rows(x_full, shard_idx).astype(jnp.float32) + summed).astype(jnp.bfloat16)
    return (piece, inverse, preact)


def backward_piece(
    x_full, up_full, up_piece, weight_in, weight_out, scale_in, scale_out, shard_idx, active, front
):
    shape = x_full.shape
    if front is None:
        widened, inverse, normed, preact = layer_front(
            x_full.reshape(-1, shape[-1]), weight_in, scale_in
        )
    else:
        inverse, preact = front
    gelu_val, slopes = gelu_parts(preact)
    d_act = (
        lax.dot_general(
            up_full.reshape(-1, shape[-1]), weight_out, (((1,), (1,)), ((), ())),
            preferred_element_type=jnp.float32,
        )
        * scale_out
    )
    d_pre = (d_act * slopes).astype(jnp.bfloat16)
    d_normed = (
        lax.dot_general(d_pre, weight_in, (((1,), (1,)), ((), ())), preferred_element_type=jnp.float32)
        * scale_in
    )
    normed_piece = sum_rows(d_normed.reshape(shape), active)
    wide_piece = own_rows(x_full, shard_idx).astype(jnp.float32)
    inv_piece = own_rows(inverse.reshape(shape[:-1] + (1,)), shard_idx)
    grad_piece = (
        up_piece.astype(jnp.float32)
        + inv_piece * normed_piece
        - wide_piece
        * inv_piece
        * inv_piece
        * inv_piece
        * jnp.mean(normed_piece * wide_piece, axis=-1, keepdims=True)
    )
    return grad_piece.astype(jnp.bfloat16)


def weight_grads(x_full, up_full, weight_in, weight_out, scale_in, scale_out):
    width = x_full.shape[-1]
    widened, inverse, normed, preact = layer_front(x_full.reshape(-1, width), weight_in, scale_in)
    gelu_val, slopes = gelu_parts(preact)
    activated = gelu_val.astype(jnp.bfloat16)
    ups = up_full.reshape(-1, width)
    d_out = (
        lax.dot_general(activated, ups, (((0,), (0,)), ((), ())), preferred_element_type=jnp.float32)
        * scale_out
    )
    d_act = (
        lax.dot_general(ups, weight_out, (((1,), (1,)), ((), ())), preferred_element_type=jnp.float32)
        * scale_out
    )
    d_pre = (d_act * slopes).astype(jnp.bfloat16)
    d_in = (
        lax.dot_general(normed, d_pre, (((0,), (0,)), ((), ())), preferred_element_type=jnp.float32)
        * scale_in
    )
    return (d_in, d_out)


def cross_boundary(piece, source, target, replicas):
    straight = [(source * replicas + h, target * replicas + h) for h in range(replicas)]
    crossed = [(source * replicas + h, target * replicas + (replicas - 1 - h)) for h in range(replicas)]
    return (lax.ppermute(piece, PAIR, straight), lax.ppermute(piece, PAIR, crossed))


def swap_sections(stepped_in, stepped_out, chosen, section_count, replicas):
    pairs = [
        (section * replicas + h, section * replicas + replicas - 1 - h)
        for section in range(section_count)
        if (chosen >> section) & 1
        for h in range(replicas)
    ]
    if not pairs:
        return (jnp.zeros_like(stepped_in), jnp.zeros_like(stepped_out))
    return (lax.ppermute(stepped_in, PAIR, pairs), lax.ppermute(stepped_out, PAIR, pairs))


def on_device(block_inputs, routes, cotangent, gossip_peer, w_in, w_out):
    section_count = lax.axis_size("section")
    replicas = lax.axis_size("half")
    group_size = lax.axis_size("plane")
    my_section = lax.axis_index("section")
    replica = lax.axis_index("half")
    shard_idx = lax.axis_index("plane")
    micro_count, blocks, piece_rows, model_width = block_inputs.shape
    capacity = cotangent.shape[1]
    weight_in = w_in[0]
    weight_out = w_out[0]
    hidden = weight_in.shape[1]
    scale_in = model_width ** (-0.5)
    scale_out = (hidden * group_size) ** (-0.5)
    link_list, live_list = route_tables(routes, blocks)

    def padded(full):
        filler = jnp.zeros(full.shape[:2] + (capacity - full.shape[2],) + full.shape[3:], full.dtype)
        return jnp.concatenate([full, filler], axis=2)

    x_cur = gather_rows(block_inputs.transpose(2, 0, 1, 3), 0)
    x_keep = padded(x_cur)
    for bound in range(section_count - 1):
        piece, inverse, preact = forward_piece(
            x_cur, weight_in, weight_out, scale_in, scale_out, shard_idx, bound
        )
        if bound == 1:
            front_keep = (inverse, preact)
        elif bound > 1:
            front_keep = tuple(
                jnp.where(my_section == bound, new, old) for new, old in zip((inverse, preact), front_keep)
            )
        straight, crossed = cross_boundary(piece, bound, bound + 1, replicas)
        sources = jnp.stack(
            [jnp.where(replica == h, straight, crossed) for h in range(replicas)]
        )[:, 0]
        mine = lax.dynamic_index_in_dim(link_list[bound], replica, 3, keepdims=False)
        mine = mine[:, :, : piece.shape[2], :]
        routed = jnp.einsum(
            "mqjk,qmjd->mkd", mine.astype(jnp.bfloat16), sources,
            preferred_element_type=jnp.float32,
        ).astype(jnp.bfloat16)[None]
        x_cur = gather_rows(routed, bound + 1)
        x_keep = jnp.where(my_section == bound + 1, x_cur, x_keep)

    last_live = lax.dynamic_index_in_dim(live_list[section_count - 1], replica, 1, keepdims=False)
    up_piece = jnp.where(
        last_live[None, :, :, None], cotangent.transpose(2, 0, 1, 3), jnp.zeros((), jnp.bfloat16)
    )
    up_full = gather_rows(up_piece, section_count - 1)
    up_keep = up_full
    last_section = section_count - 1
    for depth in reversed(range(1, section_count)):
        grad_piece = backward_piece(
            x_keep, up_full, up_piece, weight_in, weight_out, scale_in, scale_out, shard_idx, depth,
            None if depth == last_section else front_keep,
        )
        straight, crossed = cross_boundary(grad_piece, depth, depth - 1, replicas)
        sources = jnp.stack(
            [jnp.where(replica == h, straight, crossed) for h in range(replicas)]
        )[:, 0]
        mine = lax.dynamic_index_in_dim(link_list[depth - 1], replica, 1, keepdims=False)
        if depth == 1:
            mine = mine[:, :blocks]
        up_piece = jnp.einsum(
            "mjdk,dmkD->mjD", mine.astype(jnp.bfloat16), sources,
            preferred_element_type=jnp.float32,
        ).astype(jnp.bfloat16)[None]
        up_full = gather_rows(up_piece, depth - 1)
        up_keep = jnp.where(my_section == depth - 1, padded(up_full), up_keep)

    accum_in, accum_out = weight_grads(x_keep, up_keep, weight_in, weight_out, scale_in, scale_out)
    stepped_in = (weight_in.astype(jnp.float32) - LEARNING * accum_in).astype(jnp.bfloat16)
    stepped_out = (weight_out.astype(jnp.float32) - LEARNING * accum_out).astype(jnp.bfloat16)
    partner = gossip_peer[my_section, replica]
    paired = partner != replica
    pattern = jnp.sum(
        (gossip_peer[:, 0] != 0).astype(jnp.int32) << jnp.arange(section_count, dtype=jnp.int32)
    )
    other_in, other_out = lax.switch(
        pattern,
        [
            lambda a, b, chosen=chosen: swap_sections(a, b, chosen, section_count, replicas)
            for chosen in range(2**section_count)
        ],
        stepped_in,
        stepped_out,
    )
    chosen_in = jnp.where(paired, other_in, stepped_in)
    chosen_out = jnp.where(paired, other_out, stepped_out)
    new_in = (0.5 * (stepped_in.astype(jnp.float32) + chosen_in.astype(jnp.float32))).astype(
        jnp.bfloat16
    )
    new_out = (0.5 * (stepped_out.astype(jnp.float32) + chosen_out.astype(jnp.float32))).astype(
        jnp.bfloat16
    )
    return (new_in[None], new_out[None])


def solution(mesh):
    sections = mesh.shape["section"]
    reps = mesh.shape["rep"]
    inner = Mesh(np.asarray(mesh.devices).reshape(sections, 2, reps // 2), ("section", "half", "plane"))
    rows = ("half", "plane")
    return jax.shard_map(
        on_device,
        mesh=inner,
        in_specs=(
            P(None, None, rows, None),
            P(),
            P(None, None, rows, None),
            P(),
            P("section", None, rows),
            P("section", rows, None),
        ),
        out_specs=(P("section", None, rows), P("section", rows, None)),
        check_vma=False,
    )
```

```python
import numpy as np
import jax
import jax.numpy as jnp
from jax import lax
from jax.experimental import pallas as pl
from jax.experimental.pallas import tpu as pltpu
from jax.sharding import Mesh, PartitionSpec as P

EPSILON = 1e-06
GELU_SCALE = 0.7978845608028654
LEARNING = 8.0
PAIR = ("section", "half")


def gelu_parts(preact):
    inner = GELU_SCALE * (preact + 0.044715 * preact * preact * preact)
    tanh_val = jnp.tanh(inner)
    gelu_val = 0.5 * preact * (1.0 + tanh_val)
    slopes = 0.5 * (1.0 + tanh_val) + 0.5 * preact * (1.0 - tanh_val * tanh_val) * GELU_SCALE * (
        1.0 + 3.0 * 0.044715 * preact * preact
    )
    return (gelu_val, slopes)


def route_tables(routes, blocks):
    micro_count, bound_count, replicas, capacity = routes.shape
    slot_ids = jnp.arange(capacity, dtype=jnp.int32)
    replica_ids = jnp.arange(replicas, dtype=jnp.int32)
    live_now = jnp.broadcast_to(slot_ids[None, None, :] < blocks, (micro_count, replicas, capacity))
    link_list = []
    live_list = [live_now]
    for bound_idx in range(bound_count):
        target = jnp.where(live_now, routes[:, bound_idx], -1).reshape(
            micro_count, replicas * capacity
        )
        matches = (target[:, :, None] == replica_ids[None, None, :]).astype(jnp.int32)
        before = jnp.cumsum(matches, axis=1) - matches
        position = jnp.sum(matches * before, axis=2)
        link_table = matches[:, :, :, None] * (
            position[:, :, None, None] == slot_ids[None, None, None, :]
        ).astype(jnp.int32)
        link_table = link_table.reshape(micro_count, replicas, capacity, replicas, capacity)
        link_list.append(link_table.astype(jnp.float32))
        live_now = jnp.sum(link_table, axis=(1, 2)) > 0
        live_list.append(live_now)
    return (link_list, live_list)


def layer_front(flat_rows, weight_in, scale_in):
    widened = flat_rows.astype(jnp.float32)
    inverse = lax.rsqrt(jnp.mean(widened * widened, axis=-1, keepdims=True) + EPSILON)
    normed = (widened * inverse).astype(jnp.bfloat16)
    preact = jnp.dot(normed, weight_in, preferred_element_type=jnp.float32) * scale_in
    return (widened, inverse, normed, preact)


def ring_hops(offset, size):
    return min(offset, size - offset)


def far_first(count):
    side = 4 if count == 16 else 1
    def hops(step):
        return ring_hops(step % side, side) + ring_hops(step // side, count // side)
    return sorted(range(1, count), key=lambda step: (-hops(step), step))


def plane_kernel(count, spread, active, x_ref, out_ref, held, send_sem, recv_sem):
    section = lax.axis_index("section")

    @pl.when(section == active)
    def _():
        plane_exchange(count, spread, section, x_ref, out_ref, held, send_sem, recv_sem)

    @pl.when(section != active)
    def _():
        out_ref[...] = jnp.zeros_like(out_ref)


def plane_exchange(count, spread, section, x_ref, out_ref, held, send_sem, recv_sem):
    half = lax.axis_index("half")
    me = lax.axis_index("plane")
    if not spread:
        held[me] = x_ref[me]
    barrier = pltpu.get_barrier_semaphore()
    order = far_first(count)
    for step in order:
        peer = lax.bitwise_xor(me, step)
        pl.semaphore_signal(
            barrier, inc=1, device_id=(section, half, peer), device_id_type=pl.DeviceIdType.MESH
        )
    pl.semaphore_wait(barrier, count - 1)
    copies = []
    for step in order:
        peer = lax.bitwise_xor(me, step)
        copy = pltpu.make_async_remote_copy(
            src_ref=x_ref.at[0] if spread else x_ref.at[peer],
            dst_ref=held.at[me],
            send_sem=send_sem.at[step],
            recv_sem=recv_sem.at[step],
            device_id=(section, half, peer),
            device_id_type=pl.DeviceIdType.MESH,
        )
        copy.start()
        copies.append(copy)
    for copy in copies:
        copy.wait()
    if spread:
        out_ref[...] = held[...]
        out_ref[me] = x_ref[0]
    else:
        total = held[0].astype(jnp.float32)
        for chunk in range(1, count):
            total = total + held[chunk].astype(jnp.float32)
        out_ref[0] = total


def plane_call(value, count, spread, ident, active):
    lanes = value[0].size // 16
    dense = plane_dense(value.reshape(value.shape[0], 16, lanes), count, spread, ident, active)
    return dense.reshape((dense.shape[0],) + value.shape[1:])


def plane_dense(value, count, spread, ident, active):
    shape = (count,) + value.shape[1:]
    result = shape if spread else (1,) + value.shape[1:]
    return pl.pallas_call(
        lambda *refs: plane_kernel(count, spread, active, *refs),
        out_shape=jax.ShapeDtypeStruct(result, value.dtype if spread else jnp.float32),
        in_specs=[pl.BlockSpec(memory_space=pltpu.VMEM)],
        out_specs=pl.BlockSpec(memory_space=pltpu.VMEM),
        scratch_shapes=[
            pltpu.VMEM(shape, value.dtype),
            pltpu.SemaphoreType.DMA((count,)),
            pltpu.SemaphoreType.DMA((count,)),
        ],
        compiler_params=pltpu.CompilerParams(collective_id=ident, has_side_effects=True),
    )(value)


def gather_rows(piece, active):
    return plane_call(piece, lax.axis_size("plane"), True, 4 + active, active)


def sum_rows(partial_value, active):
    return plane_call(partial_value.astype(jnp.bfloat16), lax.axis_size("plane"), False, active, active)


def own_rows(full, shard_idx):
    return lax.dynamic_slice_in_dim(full, shard_idx, 1, axis=0)


def forward_piece(x_full, weight_in, weight_out, scale_in, scale_out, shard_idx, active):
    shape = x_full.shape
    widened, inverse, normed, preact = layer_front(x_full.reshape(-1, shape[-1]), weight_in, scale_in)
    gelu_val, slopes = gelu_parts(preact)
    activated = gelu_val.astype(jnp.bfloat16)
    partial_value = jnp.dot(activated, weight_out, preferred_element_type=jnp.float32) * scale_out
    summed = sum_rows(partial_value.reshape(shape), active)
    return (own_rows(x_full, shard_idx).astype(jnp.float32) + summed).astype(jnp.bfloat16)


def backward_piece(
    x_full, up_full, up_piece, weight_in, weight_out, scale_in, scale_out, shard_idx, active
):
    shape = x_full.shape
    widened, inverse, normed, preact = layer_front(x_full.reshape(-1, shape[-1]), weight_in, scale_in)
    gelu_val, slopes = gelu_parts(preact)
    d_act = (
        lax.dot_general(
            up_full.reshape(-1, shape[-1]), weight_out, (((1,), (1,)), ((), ())),
            preferred_element_type=jnp.float32,
        )
        * scale_out
    )
    d_pre = (d_act * slopes).astype(jnp.bfloat16)
    d_normed = (
        lax.dot_general(d_pre, weight_in, (((1,), (1,)), ((), ())), preferred_element_type=jnp.float32)
        * scale_in
    )
    normed_piece = sum_rows(d_normed.reshape(shape), active)
    wide_piece = own_rows(x_full, shard_idx).astype(jnp.float32)
    inv_piece = own_rows(inverse.reshape(shape[:-1] + (1,)), shard_idx)
    grad_piece = (
        up_piece.astype(jnp.float32)
        + inv_piece * normed_piece
        - wide_piece
        * inv_piece
        * inv_piece
        * inv_piece
        * jnp.mean(normed_piece * wide_piece, axis=-1, keepdims=True)
    )
    return grad_piece.astype(jnp.bfloat16)


def weight_grads(x_full, up_full, weight_in, weight_out, scale_in, scale_out):
    width = x_full.shape[-1]
    widened, inverse, normed, preact = layer_front(x_full.reshape(-1, width), weight_in, scale_in)
    gelu_val, slopes = gelu_parts(preact)
    activated = gelu_val.astype(jnp.bfloat16)
    ups = up_full.reshape(-1, width)
    d_out = (
        lax.dot_general(activated, ups, (((0,), (0,)), ((), ())), preferred_element_type=jnp.float32)
        * scale_out
    )
    d_act = (
        lax.dot_general(ups, weight_out, (((1,), (1,)), ((), ())), preferred_element_type=jnp.float32)
        * scale_out
    )
    d_pre = (d_act * slopes).astype(jnp.bfloat16)
    d_in = (
        lax.dot_general(normed, d_pre, (((0,), (0,)), ((), ())), preferred_element_type=jnp.float32)
        * scale_in
    )
    return (d_in, d_out)


def route_kernel(source, target, piece_ref, out_ref, held, send_sem, recv_sem):
    section = lax.axis_index("section")
    half = lax.axis_index("half")
    plane = lax.axis_index("plane")
    barrier = pltpu.get_barrier_semaphore()
    mesh_ids = pl.DeviceIdType.MESH

    def transfer(way, far):
        return pltpu.make_async_remote_copy(
            src_ref=piece_ref,
            dst_ref=held.at[way],
            send_sem=send_sem.at[way],
            recv_sem=recv_sem.at[way],
            device_id=(far, lax.select(way == 0, half, 1 - half), plane),
            device_id_type=mesh_ids,
        )

    @pl.when(section == source)
    def _():
        for way in range(2):
            pl.semaphore_signal(
                barrier, inc=1, device_id=(target, lax.select(way == 0, half, 1 - half), plane),
                device_id_type=mesh_ids,
            )
        pl.semaphore_wait(barrier, 2)
        copies = [transfer(way, target) for way in range(2)]
        for copy in copies:
            copy.start()
        for copy in copies:
            copy.wait_send()
        out_ref[...] = jnp.zeros_like(out_ref)

    @pl.when(section == target)
    def _():
        for way in range(2):
            pl.semaphore_signal(
                barrier, inc=1, device_id=(source, lax.select(way == 0, half, 1 - half), plane),
                device_id_type=mesh_ids,
            )
        pl.semaphore_wait(barrier, 2)
        for way in range(2):
            transfer(way, source).wait_recv()
        out_ref[...] = held[...]

    @pl.when(jnp.logical_and(section != source, section != target))
    def _():
        out_ref[...] = jnp.zeros_like(out_ref)


def cross_boundary(piece, source, target, replicas):
    lanes = piece.size // 16
    dense = piece.reshape(16, lanes)
    both = pl.pallas_call(
        lambda *refs: route_kernel(source, target, *refs),
        out_shape=jax.ShapeDtypeStruct((2, 16, lanes), piece.dtype),
        in_specs=[pl.BlockSpec(memory_space=pltpu.VMEM)],
        out_specs=pl.BlockSpec(memory_space=pltpu.VMEM),
        scratch_shapes=[
            pltpu.VMEM((2, 16, lanes), piece.dtype),
            pltpu.SemaphoreType.DMA((2,)),
            pltpu.SemaphoreType.DMA((2,)),
        ],
        compiler_params=pltpu.CompilerParams(
            collective_id=8 + source * 4 + target, has_side_effects=True
        ),
    )(dense)
    return (both[0].reshape(piece.shape), both[1].reshape(piece.shape))


def swap_sections(stepped_in, stepped_out, chosen, section_count, replicas):
    pairs = [
        (section * replicas + h, section * replicas + replicas - 1 - h)
        for section in range(section_count)
        if (chosen >> section) & 1
        for h in range(replicas)
    ]
    if not pairs:
        return (jnp.zeros_like(stepped_in), jnp.zeros_like(stepped_out))
    return (lax.ppermute(stepped_in, PAIR, pairs), lax.ppermute(stepped_out, PAIR, pairs))


def on_device(block_inputs, routes, cotangent, gossip_peer, w_in, w_out):
    section_count = lax.axis_size("section")
    replicas = lax.axis_size("half")
    group_size = lax.axis_size("plane")
    my_section = lax.axis_index("section")
    replica = lax.axis_index("half")
    shard_idx = lax.axis_index("plane")
    micro_count, blocks, piece_rows, model_width = block_inputs.shape
    capacity = cotangent.shape[1]
    weight_in = w_in[0]
    weight_out = w_out[0]
    hidden = weight_in.shape[1]
    scale_in = model_width ** (-0.5)
    scale_out = (hidden * group_size) ** (-0.5)
    link_list, live_list = route_tables(routes, blocks)

    def padded(full):
        filler = jnp.zeros(full.shape[:2] + (capacity - full.shape[2],) + full.shape[3:], full.dtype)
        return jnp.concatenate([full, filler], axis=2)

    x_cur = gather_rows(block_inputs.transpose(2, 0, 1, 3), 0)
    x_keep = padded(x_cur)
    for bound in range(section_count - 1):
        piece = forward_piece(x_cur, weight_in, weight_out, scale_in, scale_out, shard_idx, bound)
        straight, crossed = cross_boundary(piece, bound, bound + 1, replicas)
        sources = jnp.stack(
            [jnp.where(replica == h, straight, crossed) for h in range(replicas)]
        )[:, 0]
        mine = lax.dynamic_index_in_dim(link_list[bound], replica, 3, keepdims=False)
        mine = mine[:, :, : piece.shape[2], :]
        routed = jnp.einsum(
            "mqjk,qmjd->mkd", mine.astype(jnp.bfloat16), sources,
            preferred_element_type=jnp.float32,
        ).astype(jnp.bfloat16)[None]
        x_cur = gather_rows(routed, bound + 1)
        x_keep = jnp.where(my_section == bound + 1, x_cur, x_keep)

    last_live = lax.dynamic_index_in_dim(live_list[section_count - 1], replica, 1, keepdims=False)
    up_piece = jnp.where(
        last_live[None, :, :, None], cotangent.transpose(2, 0, 1, 3), jnp.zeros((), jnp.bfloat16)
    )
    up_full = gather_rows(up_piece, section_count - 1)
    up_keep = up_full
    for depth in reversed(range(1, section_count)):
        grad_piece = backward_piece(
            x_keep, up_full, up_piece, weight_in, weight_out, scale_in, scale_out, shard_idx, depth
        )
        straight, crossed = cross_boundary(grad_piece, depth, depth - 1, replicas)
        sources = jnp.stack(
            [jnp.where(replica == h, straight, crossed) for h in range(replicas)]
        )[:, 0]
        mine = lax.dynamic_index_in_dim(link_list[depth - 1], replica, 1, keepdims=False)
        if depth == 1:
            mine = mine[:, :blocks]
        up_piece = jnp.einsum(
            "mjdk,dmkD->mjD", mine.astype(jnp.bfloat16), sources,
            preferred_element_type=jnp.float32,
        ).astype(jnp.bfloat16)[None]
        up_full = gather_rows(up_piece, depth - 1)
        up_keep = jnp.where(my_section == depth - 1, padded(up_full), up_keep)

    accum_in, accum_out = weight_grads(x_keep, up_keep, weight_in, weight_out, scale_in, scale_out)
    stepped_in = (weight_in.astype(jnp.float32) - LEARNING * accum_in).astype(jnp.bfloat16)
    stepped_out = (weight_out.astype(jnp.float32) - LEARNING * accum_out).astype(jnp.bfloat16)
    partner = gossip_peer[my_section, replica]
    paired = partner != replica
    pattern = jnp.sum(
        (gossip_peer[:, 0] != 0).astype(jnp.int32) << jnp.arange(section_count, dtype=jnp.int32)
    )
    other_in, other_out = lax.switch(
        pattern,
        [
            lambda a, b, chosen=chosen: swap_sections(a, b, chosen, section_count, replicas)
            for chosen in range(2**section_count)
        ],
        stepped_in,
        stepped_out,
    )
    chosen_in = jnp.where(paired, other_in, stepped_in)
    chosen_out = jnp.where(paired, other_out, stepped_out)
    new_in = (0.5 * (stepped_in.astype(jnp.float32) + chosen_in.astype(jnp.float32))).astype(
        jnp.bfloat16
    )
    new_out = (0.5 * (stepped_out.astype(jnp.float32) + chosen_out.astype(jnp.float32))).astype(
        jnp.bfloat16
    )
    return (new_in[None], new_out[None])


def solution(mesh):
    sections = mesh.shape["section"]
    reps = mesh.shape["rep"]
    inner = Mesh(np.asarray(mesh.devices).reshape(sections, 2, reps // 2), ("section", "half", "plane"))
    rows = ("half", "plane")
    return jax.shard_map(
        on_device,
        mesh=inner,
        in_specs=(
            P(None, None, rows, None),
            P(),
            P(None, None, rows, None),
            P(),
            P("section", None, rows),
            P("section", rows, None),
        ),
        out_specs=(P("section", None, rows), P("section", rows, None)),
        check_vma=False,
    )
```

```python
import numpy as np
import jax
import jax.numpy as jnp
from jax import lax
from jax.experimental import pallas as pl
from jax.experimental.pallas import tpu as pltpu
from jax.sharding import Mesh, PartitionSpec as P

EPSILON = 1e-06
GELU_SCALE = 0.7978845608028654
LEARNING = 8.0
PAIR = ("section", "half")


def gelu_parts(preact):
    inner = GELU_SCALE * (preact + 0.044715 * preact * preact * preact)
    tanh_val = jnp.tanh(inner)
    gelu_val = 0.5 * preact * (1.0 + tanh_val)
    slopes = 0.5 * (1.0 + tanh_val) + 0.5 * preact * (1.0 - tanh_val * tanh_val) * GELU_SCALE * (
        1.0 + 3.0 * 0.044715 * preact * preact
    )
    return (gelu_val, slopes)


def route_tables(routes, blocks):
    micro_count, bound_count, replicas, capacity = routes.shape
    slot_ids = jnp.arange(capacity, dtype=jnp.int32)
    replica_ids = jnp.arange(replicas, dtype=jnp.int32)
    live_now = jnp.broadcast_to(slot_ids[None, None, :] < blocks, (micro_count, replicas, capacity))
    link_list = []
    live_list = [live_now]
    for bound_idx in range(bound_count):
        target = jnp.where(live_now, routes[:, bound_idx], -1).reshape(
            micro_count, replicas * capacity
        )
        matches = (target[:, :, None] == replica_ids[None, None, :]).astype(jnp.int32)
        before = jnp.cumsum(matches, axis=1) - matches
        position = jnp.sum(matches * before, axis=2)
        link_table = matches[:, :, :, None] * (
            position[:, :, None, None] == slot_ids[None, None, None, :]
        ).astype(jnp.int32)
        link_table = link_table.reshape(micro_count, replicas, capacity, replicas, capacity)
        link_list.append(link_table.astype(jnp.float32))
        live_now = jnp.sum(link_table, axis=(1, 2)) > 0
        live_list.append(live_now)
    return (link_list, live_list)


def layer_front(flat_rows, weight_in, scale_in):
    widened = flat_rows.astype(jnp.float32)
    inverse = lax.rsqrt(jnp.mean(widened * widened, axis=-1, keepdims=True) + EPSILON)
    normed = (widened * inverse).astype(jnp.bfloat16)
    preact = jnp.dot(normed, weight_in, preferred_element_type=jnp.float32) * scale_in
    return (widened, inverse, normed, preact)


def ring_hops(offset, size):
    return min(offset, size - offset)


def far_first(count):
    side = 4 if count == 16 else 1
    def hops(step):
        return ring_hops(step % side, side) + ring_hops(step // side, count // side)
    return sorted(range(1, count), key=lambda step: (-hops(step), step))


def plane_kernel(count, spread, active, x_ref, out_ref, held, send_sem, recv_sem):
    section = lax.axis_index("section")

    @pl.when(section == active)
    def _():
        plane_exchange(count, spread, section, x_ref, out_ref, held, send_sem, recv_sem)

    @pl.when(section != active)
    def _():
        out_ref[...] = jnp.zeros_like(out_ref)


def plane_exchange(count, spread, section, x_ref, out_ref, held, send_sem, recv_sem):
    half = lax.axis_index("half")
    me = lax.axis_index("plane")
    if not spread:
        held[me] = x_ref[me]
    barrier = pltpu.get_barrier_semaphore()
    order = far_first(count)
    for step in order:
        peer = lax.bitwise_xor(me, step)
        pl.semaphore_signal(
            barrier, inc=1, device_id=(section, half, peer), device_id_type=pl.DeviceIdType.MESH
        )
    pl.semaphore_wait(barrier, count - 1)
    copies = []
    for step in order:
        peer = lax.bitwise_xor(me, step)
        copy = pltpu.make_async_remote_copy(
            src_ref=x_ref.at[0] if spread else x_ref.at[peer],
            dst_ref=out_ref.at[me] if spread else held.at[me],
            send_sem=send_sem.at[step],
            recv_sem=recv_sem.at[step],
            device_id=(section, half, peer),
            device_id_type=pl.DeviceIdType.MESH,
        )
        copy.start()
        copies.append(copy)
    for copy in copies:
        copy.wait()
    if spread:
        out_ref[me] = x_ref[0]
    else:
        total = held[0].astype(jnp.float32)
        for chunk in range(1, count):
            total = total + held[chunk].astype(jnp.float32)
        out_ref[0] = total


def plane_call(value, count, spread, ident, active):
    lanes = value[0].size // 16
    dense = plane_dense(value.reshape(value.shape[0], 16, lanes), count, spread, ident, active)
    return dense.reshape((dense.shape[0],) + value.shape[1:])


def plane_dense(value, count, spread, ident, active):
    shape = (count,) + value.shape[1:]
    result = shape if spread else (1,) + value.shape[1:]
    return pl.pallas_call(
        lambda *refs: plane_kernel(count, spread, active, *refs),
        out_shape=jax.ShapeDtypeStruct(result, value.dtype if spread else jnp.float32),
        in_specs=[pl.BlockSpec(memory_space=pltpu.VMEM)],
        out_specs=pl.BlockSpec(memory_space=pltpu.VMEM),
        scratch_shapes=[
            pltpu.VMEM(shape, value.dtype),
            pltpu.SemaphoreType.DMA((count,)),
            pltpu.SemaphoreType.DMA((count,)),
        ],
        compiler_params=pltpu.CompilerParams(collective_id=ident, has_side_effects=True),
    )(value)


def gather_rows(piece, active):
    return plane_call(piece, lax.axis_size("plane"), True, 4 + active, active)


def sum_rows(partial_value, active):
    return plane_call(partial_value.astype(jnp.bfloat16), lax.axis_size("plane"), False, active, active)


def own_rows(full, shard_idx):
    return lax.dynamic_slice_in_dim(full, shard_idx, 1, axis=0)


def forward_piece(x_full, weight_in, weight_out, scale_in, scale_out, shard_idx, active):
    shape = x_full.shape
    widened, inverse, normed, preact = layer_front(x_full.reshape(-1, shape[-1]), weight_in, scale_in)
    gelu_val, slopes = gelu_parts(preact)
    activated = gelu_val.astype(jnp.bfloat16)
    partial_value = jnp.dot(activated, weight_out, preferred_element_type=jnp.float32) * scale_out
    summed = sum_rows(partial_value.reshape(shape), active)
    return (own_rows(x_full, shard_idx).astype(jnp.float32) + summed).astype(jnp.bfloat16)


def backward_piece(
    x_full, up_full, up_piece, weight_in, weight_out, scale_in, scale_out, shard_idx, active
):
    shape = x_full.shape
    widened, inverse, normed, preact = layer_front(x_full.reshape(-1, shape[-1]), weight_in, scale_in)
    gelu_val, slopes = gelu_parts(preact)
    d_act = (
        lax.dot_general(
            up_full.reshape(-1, shape[-1]), weight_out, (((1,), (1,)), ((), ())),
            preferred_element_type=jnp.float32,
        )
        * scale_out
    )
    d_pre = (d_act * slopes).astype(jnp.bfloat16)
    d_normed = (
        lax.dot_general(d_pre, weight_in, (((1,), (1,)), ((), ())), preferred_element_type=jnp.float32)
        * scale_in
    )
    normed_piece = sum_rows(d_normed.reshape(shape), active)
    wide_piece = own_rows(x_full, shard_idx).astype(jnp.float32)
    inv_piece = own_rows(inverse.reshape(shape[:-1] + (1,)), shard_idx)
    grad_piece = (
        up_piece.astype(jnp.float32)
        + inv_piece * normed_piece
        - wide_piece
        * inv_piece
        * inv_piece
        * inv_piece
        * jnp.mean(normed_piece * wide_piece, axis=-1, keepdims=True)
    )
    return grad_piece.astype(jnp.bfloat16)


def weight_grads(x_full, up_full, weight_in, weight_out, scale_in, scale_out):
    width = x_full.shape[-1]
    widened, inverse, normed, preact = layer_front(x_full.reshape(-1, width), weight_in, scale_in)
    gelu_val, slopes = gelu_parts(preact)
    activated = gelu_val.astype(jnp.bfloat16)
    ups = up_full.reshape(-1, width)
    d_out = (
        lax.dot_general(activated, ups, (((0,), (0,)), ((), ())), preferred_element_type=jnp.float32)
        * scale_out
    )
    d_act = (
        lax.dot_general(ups, weight_out, (((1,), (1,)), ((), ())), preferred_element_type=jnp.float32)
        * scale_out
    )
    d_pre = (d_act * slopes).astype(jnp.bfloat16)
    d_in = (
        lax.dot_general(normed, d_pre, (((0,), (0,)), ((), ())), preferred_element_type=jnp.float32)
        * scale_in
    )
    return (d_in, d_out)


def cross_boundary(piece, source, target, replicas):
    straight = [(source * replicas + h, target * replicas + h) for h in range(replicas)]
    crossed = [(source * replicas + h, target * replicas + (replicas - 1 - h)) for h in range(replicas)]
    return (lax.ppermute(piece, PAIR, straight), lax.ppermute(piece, PAIR, crossed))


def swap_sections(stepped_in, stepped_out, chosen, section_count, replicas):
    pairs = [
        (section * replicas + h, section * replicas + replicas - 1 - h)
        for section in range(section_count)
        if (chosen >> section) & 1
        for h in range(replicas)
    ]
    if not pairs:
        return (jnp.zeros_like(stepped_in), jnp.zeros_like(stepped_out))
    return (lax.ppermute(stepped_in, PAIR, pairs), lax.ppermute(stepped_out, PAIR, pairs))


def on_device(block_inputs, routes, cotangent, gossip_peer, w_in, w_out):
    section_count = lax.axis_size("section")
    replicas = lax.axis_size("half")
    group_size = lax.axis_size("plane")
    my_section = lax.axis_index("section")
    replica = lax.axis_index("half")
    shard_idx = lax.axis_index("plane")
    micro_count, blocks, piece_rows, model_width = block_inputs.shape
    capacity = cotangent.shape[1]
    weight_in = w_in[0]
    weight_out = w_out[0]
    hidden = weight_in.shape[1]
    scale_in = model_width ** (-0.5)
    scale_out = (hidden * group_size) ** (-0.5)
    link_list, live_list = route_tables(routes, blocks)

    def padded(full):
        filler = jnp.zeros(full.shape[:2] + (capacity - full.shape[2],) + full.shape[3:], full.dtype)
        return jnp.concatenate([full, filler], axis=2)

    x_cur = gather_rows(block_inputs.transpose(2, 0, 1, 3), 0)
    x_keep = padded(x_cur)
    for bound in range(section_count - 1):
        piece = forward_piece(x_cur, weight_in, weight_out, scale_in, scale_out, shard_idx, bound)
        straight, crossed = cross_boundary(piece, bound, bound + 1, replicas)
        sources = jnp.stack(
            [jnp.where(replica == h, straight, crossed) for h in range(replicas)]
        )[:, 0]
        mine = lax.dynamic_index_in_dim(link_list[bound], replica, 3, keepdims=False)
        mine = mine[:, :, : piece.shape[2], :]
        routed = jnp.einsum(
            "mqjk,qmjd->mkd", mine.astype(jnp.bfloat16), sources,
            preferred_element_type=jnp.float32,
        ).astype(jnp.bfloat16)[None]
        x_cur = gather_rows(routed, bound + 1)
        x_keep = jnp.where(my_section == bound + 1, x_cur, x_keep)

    last_live = lax.dynamic_index_in_dim(live_list[section_count - 1], replica, 1, keepdims=False)
    up_piece = jnp.where(
        last_live[None, :, :, None], cotangent.transpose(2, 0, 1, 3), jnp.zeros((), jnp.bfloat16)
    )
    up_full = gather_rows(up_piece, section_count - 1)
    up_keep = up_full
    for depth in reversed(range(1, section_count)):
        grad_piece = backward_piece(
            x_keep, up_full, up_piece, weight_in, weight_out, scale_in, scale_out, shard_idx, depth
        )
        straight, crossed = cross_boundary(grad_piece, depth, depth - 1, replicas)
        sources = jnp.stack(
            [jnp.where(replica == h, straight, crossed) for h in range(replicas)]
        )[:, 0]
        mine = lax.dynamic_index_in_dim(link_list[depth - 1], replica, 1, keepdims=False)
        if depth == 1:
            mine = mine[:, :blocks]
        up_piece = jnp.einsum(
            "mjdk,dmkD->mjD", mine.astype(jnp.bfloat16), sources,
            preferred_element_type=jnp.float32,
        ).astype(jnp.bfloat16)[None]
        up_full = gather_rows(up_piece, depth - 1)
        up_keep = jnp.where(my_section == depth - 1, padded(up_full), up_keep)

    accum_in, accum_out = weight_grads(x_keep, up_keep, weight_in, weight_out, scale_in, scale_out)
    stepped_in = (weight_in.astype(jnp.float32) - LEARNING * accum_in).astype(jnp.bfloat16)
    stepped_out = (weight_out.astype(jnp.float32) - LEARNING * accum_out).astype(jnp.bfloat16)
    partner = gossip_peer[my_section, replica]
    paired = partner != replica
    pattern = jnp.sum(
        (gossip_peer[:, 0] != 0).astype(jnp.int32) << jnp.arange(section_count, dtype=jnp.int32)
    )
    other_in, other_out = lax.switch(
        pattern,
        [
            lambda a, b, chosen=chosen: swap_sections(a, b, chosen, section_count, replicas)
            for chosen in range(2**section_count)
        ],
        stepped_in,
        stepped_out,
    )
    chosen_in = jnp.where(paired, other_in, stepped_in)
    chosen_out = jnp.where(paired, other_out, stepped_out)
    new_in = (0.5 * (stepped_in.astype(jnp.float32) + chosen_in.astype(jnp.float32))).astype(
        jnp.bfloat16
    )
    new_out = (0.5 * (stepped_out.astype(jnp.float32) + chosen_out.astype(jnp.float32))).astype(
        jnp.bfloat16
    )
    return (new_in[None], new_out[None])


def solution(mesh):
    sections = mesh.shape["section"]
    reps = mesh.shape["rep"]
    inner = Mesh(np.asarray(mesh.devices).reshape(sections, 2, reps // 2), ("section", "half", "plane"))
    rows = ("half", "plane")
    return jax.shard_map(
        on_device,
        mesh=inner,
        in_specs=(
            P(None, None, rows, None),
            P(),
            P(None, None, rows, None),
            P(),
            P("section", None, rows),
            P("section", rows, None),
        ),
        out_specs=(P("section", None, rows), P("section", rows, None)),
        check_vma=False,
    )
```
